32 devices in a mesh: grp: 2 (over x), ctx: 8 (over z, y), hd: 2 (over core).
Axes of the slice: x: 2, y: 2, z: 4, core: 2. Of those that a mesh axis runs over, the one named last changes fastest.
Arguments:
- queries: bfloat16 [128, 32, 128], P(('grp', 'ctx'), 'hd'), parts along dimension 0, may hold values from -200 to 200
- prefix_keys: bfloat16 [32768, 4, 128], P(('grp', 'ctx'), 'hd'), parts along dimension 0, may hold values from -6 to 6
- prefix_values: bfloat16 [32768, 4, 128], P(('grp', 'ctx'), 'hd'), parts along dimension 0, may hold values from -6 to 6
- out_weight: bfloat16 [4096, 2048], P(('hd', 'ctx')), may hold values from -0.09375 to 0.09375
- residual_in: bfloat16 [128, 2048], P(('grp', 'ctx', 'hd')), parts along dimension 0, may hold values from -6 to 6
- expert_ids: int32 [128, 8], P(('grp', 'ctx', 'hd')), parts along dimension 0, may hold values from 0 to 15, all different within a row; in each aligned block of 4 rows (0 to 3, 4 to 7, ...) at most 4 rows name the same one
- gate_weights: float32 [128, 8], P(('grp', 'ctx', 'hd')), parts along dimension 0, may hold values from 0.05 to 0.4
- w_gate: bfloat16 [16, 2048, 768], P(('ctx', 'hd')), may hold values from -0.125 to 0.125
- w_up: bfloat16 [16, 2048, 768], P(('ctx', 'hd')), may hold values from -0.125 to 0.125
- w_down: bfloat16 [16, 768, 2048], P(('ctx', 'hd')), may hold values from -0.21875 to 0.21875
Outputs:
- layer_out: bfloat16 [128, 2048], P(('grp', 'ctx', 'hd')), parts along dimension 0
The draws below stay inside these ranges and needn't reach their ends.
There are 2 independent parts, one for each index of `grp`. The reference program is written for one: setup_inputs(seed, part) draws one part's arguments, and reference() takes and returns one part's arrays. A program takes and returns all parts, laid end to end along the dimension named above; an argument that names none is the same for every part. Nothing has to cross between parts.
Inputs may be any that keep to these rules, and one draw needn't show every extreme that they name: `expert_ids`: each row names 8 different experts; within each aligned block of 4 rows no expert is named by more than 4 rows.
All inputs are finite; a program needn't handle non-finite values.
Results may differ from the reference program's by a relative error of at most 0.013.
Values may be sent and summed in bfloat16 or wider, within the bound.
A program may use at most 128 MiB of HBM per device.

```python
import math
import jax
import jax.numpy as jnp
import numpy as np
from jax import lax

D = 2048
HEADS = 32
KV_HEADS = 4
HEAD_DIM = 128
FFN = 768
TOP = 8
TOK_DEV = 4
KV_BLOCK = 512
PREFIX = 16384
TOKENS = 64
EXPERTS = 16
CAP = 4


def draw_queries(key, part):
    array_shape = (TOKENS, HEADS, HEAD_DIM)
    standard = jax.random.normal(jax.random.fold_in(key, 11), array_shape, jnp.float32)
    drawn = standard * 2.5
    return jnp.clip(drawn, -200.0, 200.0).astype(jnp.bfloat16)


def shard_levels(rng, extent, cuts, smallest, top_value):
    def one(axis_at, blocks):
        heights = jax.random.uniform(jax.random.fold_in(jax.random.fold_in(rng, 6), axis_at), (blocks,), jnp.float32, smallest / len(cuts), top_value / len(cuts))
        return jnp.repeat(jnp.exp(heights), extent[axis_at] // blocks).reshape((-1,) + (1,) * (len(extent) - axis_at - 1))

    factor_of = one(*cuts[0])
    for cut in cuts[1:]:
        factor_of = factor_of * one(*cut)
    return factor_of


def shared_out(key, own, number, rows, count, top, limit, lean):
    ranking = jax.random.permutation(key, count)
    crowded, usual = load_shares(count, rows * top, limit, lean, True), load_shares(count, rows * top, limit, lean, False)
    places = jnp.arange(count)

    def named(sizes, rotation):
        used = int((sizes > 0).sum())
        fixed = max(1, used // 4)
        shifted = fixed + (places - fixed + rotation * (used - fixed)) % max(1, count - fixed)
        return jnp.zeros((count,), jnp.int32).at[ranking[jnp.where(places < fixed, places, shifted)]].set(jnp.asarray(sizes, jnp.int32))

    sizes = jnp.where(number % 4 == 0, named(crowded, number // 4), named(usual, number - number // 4 - 1))
    mixed = jax.random.permutation(jax.random.fold_in(own, 3), count)
    giver, sink = mixed[0:count // 2 * 2:2], mixed[1:count // 2 * 2:2]
    room = jnp.minimum(sizes[giver] - 1, limit - sizes[sink]) // 2
    room = jnp.where((giver == ranking[0]) | (sink == ranking[0]) | (sizes[sink] == 0), 0, jnp.maximum(room, 0))
    shifted = jax.random.randint(jax.random.fold_in(own, 4), (count // 2,), 0, 1 << 20) % (room + 1)
    sizes = sizes.at[giver].add(-shifted).at[sink].add(shifted)
    items = jnp.searchsorted(jnp.cumsum(sizes), jnp.arange(rows * top), side="right").astype(jnp.int32)
    listing = items.reshape(top, rows).T
    listing = listing[jax.random.permutation(jax.random.fold_in(own, 1), rows)]
    rotation = jax.random.randint(jax.random.fold_in(own, 2), (rows, 1), 0, top)
    return jnp.take_along_axis(listing, (jnp.arange(top)[None, :] + rotation) % top, axis=1)


def load_shares(number_of, total, reach, skew, full):
    loads = [(1 << 20) // math.isqrt(standing ** skew) + 1 for standing in range(1, number_of + 1)]
    largest = reach if full else min(reach, max(-(-total // number_of), total * loads[0] // sum(loads)))
    least = 1 if total - largest >= number_of - 1 else 0
    counts, rest = [largest] + [least] * (number_of - 1), total - largest - least * (number_of - 1)
    while rest > 0:
        candidates = [i for i in range(1, number_of) if counts[i] < largest] or [i for i in range(1, number_of) if counts[i] < reach]
        pool, remaining = sum([loads[i] for i in candidates]), rest
        for i in candidates:
            extra = min(reach - counts[i], max(1, remaining * loads[i] // pool), rest)
            counts[i] = counts[i] + extra
            rest = rest - extra
    return np.array(counts)


def centred(key, shape, scale, most, cuts=(), kind=jnp.bfloat16):
    array = jax.random.normal(key, shape, jnp.float32) * scale
    if len(cuts) > 0:
        array = shard_levels(key, shape, cuts, -0.22, 0.18) * array
    return jnp.clip(array, min=-most, max=most).astype(kind)


def setup_inputs(seed: int = 0, part: int = 0) -> dict:
    keys = jax.random.split(jax.random.key(seed), 11)
    part_keys = jax.random.split(jax.random.fold_in(keys[10], part), 11)
    queries = draw_queries(jax.random.fold_in(jax.random.fold_in(keys[10], part), 71), part)
    prefix_keys = centred(part_keys[1], (PREFIX, KV_HEADS, HEAD_DIM), 1.0, 6.0, ((0, 8), (1, 2)))
    prefix_values = centred(part_keys[2], (PREFIX, KV_HEADS, HEAD_DIM), 1.0, 6.0, ((0, 8), (1, 2)))
    out_weight = centred(keys[3], (HEADS * HEAD_DIM, D), (HEADS * HEAD_DIM) ** -0.5, 0.09375, ((0, 16),))
    residual_in = centred(part_keys[4], (TOKENS, D), 1.0, 6.0, ((0, 16),))
    expert_ids_keys = jax.random.split(jax.random.fold_in(part_keys[5], 1), TOKENS // TOK_DEV)
    expert_ids_turns = jax.random.permutation(jax.random.fold_in(part_keys[5], 3), TOKENS // TOK_DEV)
    expert_ids = jax.vmap(lambda own, number: shared_out(jax.random.fold_in(part_keys[5], 2), own, number, TOK_DEV, EXPERTS, TOP, CAP, 2))(expert_ids_keys, expert_ids_turns).reshape((TOKENS, TOP))
    gate_weights = jnp.clip(jnp.exp(math.log(0.4) - 2.0794415 * jax.random.uniform(part_keys[6], (TOKENS, TOP), jnp.float32) ** shard_levels(part_keys[6], (TOKENS, TOP), ((0, 16),), -0.2, 0.2)), 0.05, 0.4)
    w_gate = centred(keys[7], (EXPERTS, D, FFN), D ** -0.5, 0.125, ((0, 16),))
    w_up = centred(keys[8], (EXPERTS, D, FFN), D ** -0.5, 0.125, ((0, 16),))
    w_down = centred(keys[9], (EXPERTS, FFN, D), FFN ** -0.5, 0.21875, ((0, 16),))
    return dict(queries=queries, prefix_keys=prefix_keys, prefix_values=prefix_values, out_weight=out_weight, residual_in=residual_in, expert_ids=expert_ids, gate_weights=gate_weights, w_gate=w_gate, w_up=w_up, w_down=w_down)


NEG_START = -1e+30

def prefix_attention(queries, prefix_keys, prefix_values):
    grouped = HEADS // KV_HEADS
    query_view = queries.reshape(TOKENS, KV_HEADS, grouped, HEAD_DIM).astype(jnp.float32)
    block_count = PREFIX // KV_BLOCK
    key_blocks = prefix_keys.reshape(block_count, KV_BLOCK, KV_HEADS, HEAD_DIM)
    value_blocks = prefix_values.reshape(block_count, KV_BLOCK, KV_HEADS, HEAD_DIM)
    scaling = HEAD_DIM ** (-0.5)

    def advance(running, pieces):
        peak_scores, totals, accumulated = running
        key_piece, value_piece = pieces
        scores = jnp.einsum('sgjd,kgd->sgjk', query_view, key_piece.astype(jnp.float32)) * scaling
        block_peak = lax.optimization_barrier(jnp.max(scores, axis=-1))
        weights = jnp.exp(scores - block_peak[..., None]).astype(jnp.bfloat16)
        weights = lax.optimization_barrier(weights).astype(jnp.float32)
        block_total = lax.optimization_barrier(jnp.sum(weights, axis=-1))
        block_out = jnp.einsum('sgjk,kgd->sgjd', weights, value_piece.astype(jnp.float32))
        raised = jnp.maximum(peak_scores, block_peak)
        old_factor = jnp.exp(peak_scores - raised)
        new_factor = jnp.exp(block_peak - raised)
        totals = totals * old_factor + block_total * new_factor
        accumulated = accumulated * old_factor[..., None] + block_out * new_factor[..., None]
        return ((raised, totals, accumulated), None)
    start_state = (jnp.full((TOKENS, KV_HEADS, grouped), NEG_START, jnp.float32), jnp.zeros((TOKENS, KV_HEADS, grouped), jnp.float32), jnp.zeros((TOKENS, KV_HEADS, grouped, HEAD_DIM), jnp.float32))
    final_state, leftover = lax.scan(advance, start_state, (key_blocks, value_blocks))
    totals = final_state[1]
    accumulated = final_state[2]
    attended = accumulated / totals[..., None]
    return attended.reshape(TOKENS, HEADS * HEAD_DIM).astype(jnp.bfloat16)

def expert_layer(normed, expert_ids, gate_weights, w_gate, w_up, w_down):
    block_count = TOKENS // TOK_DEV
    slot_total = TOK_DEV * TOP
    id_blocks = expert_ids.reshape(block_count, slot_total)
    expert_iota = jnp.arange(EXPERTS, dtype=jnp.int32)
    onehot = (id_blocks[:, :, None] == expert_iota[None, None, :]).astype(jnp.int32)
    earlier = jnp.cumsum(onehot, axis=1) - onehot
    position = lax.optimization_barrier(jnp.sum(onehot * earlier, axis=2)).astype(jnp.int32)
    slot_iota = jnp.arange(CAP, dtype=jnp.int32)
    dispatch = ((id_blocks[:, None, None, :] == expert_iota[None, :, None, None]) & (position[:, None, None, :] == slot_iota[None, None, :, None])).astype(jnp.float32)
    repeated = jnp.repeat(normed.reshape(block_count, TOK_DEV, D), TOP, axis=1).astype(jnp.float32)
    buffer = jnp.einsum('becn,bnd->ebcd', dispatch, repeated).astype(jnp.bfloat16)

    def run_expert(operands):
        inputs, gate_matrix, up_matrix, down_matrix = operands
        flattened = inputs.reshape(block_count * CAP, D)
        gate_values = jnp.dot(flattened, gate_matrix, preferred_element_type=jnp.float32)
        up_values = jnp.dot(flattened, up_matrix, preferred_element_type=jnp.float32)
        hidden = (jax.nn.silu(gate_values) * up_values).astype(jnp.bfloat16)
        expert_out = jnp.dot(hidden, down_matrix, preferred_element_type=jnp.float32).astype(jnp.bfloat16)
        return expert_out.reshape(block_count, CAP, D)
    results = lax.map(run_expert, (buffer, w_gate, w_up, w_down))
    gathered = jnp.einsum('becn,ebcd->bnd', dispatch, results.astype(jnp.float32))
    weighted = gathered.reshape(TOKENS, TOP, D) * gate_weights[:, :, None]
    return lax.optimization_barrier(jnp.sum(weighted, axis=1))

def reference(queries, prefix_keys, prefix_values, out_weight, residual_in, expert_ids, gate_weights, w_gate, w_up, w_down):
    attended = prefix_attention(queries, prefix_keys, prefix_values)
    projected = jnp.dot(attended, out_weight, preferred_element_type=jnp.float32)
    stream = residual_in.astype(jnp.float32) + projected
    normed = (stream * lax.rsqrt(lax.optimization_barrier(jnp.mean(stream * stream, axis=-1, keepdims=True)) + 1e-06)).astype(jnp.bfloat16)
    mixture = expert_layer(normed, expert_ids, gate_weights, w_gate, w_up, w_down)
    return (stream + mixture).astype(jnp.bfloat16)
```

```python
import jax
import jax.numpy as jnp
from jax import lax
from jax.experimental import pallas as pl
from jax.experimental.pallas import tpu as pltpu
from jax.sharding import PartitionSpec as P
import functools
import math

TOP = 8
KV_BLOCK = 512


NEG_START = -1e30


def local_attention(queries, prefix_keys, prefix_values):
    token_count, heads_local, head_width = queries.shape
    key_heads = prefix_keys.shape[1]
    grouped = heads_local // key_heads
    query_view = queries.reshape(token_count, key_heads, grouped, head_width)
    block_count = prefix_keys.shape[0] // KV_BLOCK
    key_blocks = prefix_keys.reshape(block_count, KV_BLOCK, key_heads, head_width)
    value_blocks = prefix_values.reshape(block_count, KV_BLOCK, key_heads, head_width)
    scaling = head_width ** (-0.5)

    def advance(running, pieces):
        peak_scores, totals, accumulated = running
        key_piece, value_piece = pieces
        scores = (
            jnp.einsum("sgjd,kgd->sgjk", query_view, key_piece, preferred_element_type=jnp.float32)
            * scaling
        )
        block_peak = jnp.max(scores, axis=-1)
        weights = jnp.exp(scores - block_peak[..., None]).astype(jnp.bfloat16)
        block_total = jnp.sum(weights.astype(jnp.float32), axis=-1)
        block_out = jnp.einsum(
            "sgjk,kgd->sgjd", weights, value_piece, preferred_element_type=jnp.float32
        )
        raised = jnp.maximum(peak_scores, block_peak)
        old_factor = jnp.exp(peak_scores - raised)
        new_factor = jnp.exp(block_peak - raised)
        totals = totals * old_factor + block_total * new_factor
        accumulated = accumulated * old_factor[..., None] + block_out * new_factor[..., None]
        return ((raised, totals, accumulated), None)

    start_state = (
        jnp.full((token_count, key_heads, grouped), NEG_START, jnp.float32),
        jnp.zeros((token_count, key_heads, grouped), jnp.float32),
        jnp.zeros((token_count, key_heads, grouped, head_width), jnp.float32),
    )
    final_state, leftover = lax.scan(advance, start_state, (key_blocks, value_blocks))
    peak_scores = final_state[0].reshape(token_count, heads_local)
    totals = final_state[1].reshape(token_count, heads_local)
    accumulated = final_state[2].reshape(token_count, heads_local, head_width)
    return (peak_scores, totals, accumulated)


def on_device_general(
    queries,
    prefix_keys,
    prefix_values,
    out_weight,
    residual_in,
    expert_ids,
    gate_weights,
    w_gate,
    w_up,
    w_down,
):
    every_query = lax.all_gather(queries, "ctx", axis=0, tiled=True)
    peak_scores, totals, accumulated = local_attention(every_query, prefix_keys, prefix_values)
    token_count, heads_local, head_width = accumulated.shape
    top_peak = lax.pmax(peak_scores, "ctx")
    factor = jnp.exp(peak_scores - top_peak)
    scaled_totals = totals * factor
    scaled_accum = (accumulated * factor[..., None]).reshape(token_count, heads_local * head_width)
    model_width = out_weight.shape[1]
    column_accum = lax.psum_scatter(
        scaled_accum.astype(jnp.bfloat16), "ctx", scatter_dimension=1, tiled=True
    ).astype(jnp.float32)
    all_totals = lax.psum(scaled_totals, "ctx")
    width_here = column_accum.shape[1]
    column_ids = lax.axis_index("ctx") * width_here + jnp.arange(width_here, dtype=jnp.int32)
    selector = (
        (column_ids // head_width)[None, :] == jnp.arange(heads_local, dtype=jnp.int32)[:, None]
    ).astype(jnp.float32)
    denominators = jnp.dot(all_totals, selector, precision=lax.Precision.HIGHEST)
    attended = (column_accum / denominators).astype(jnp.bfloat16)
    projected = lax.psum_scatter(
        jnp.dot(attended, out_weight, preferred_element_type=jnp.float32),
        ("ctx", "hd"),
        scatter_dimension=0,
        tiled=True,
    )
    stream = residual_in.astype(jnp.float32) + projected
    normed = (stream * lax.rsqrt(jnp.mean(stream * stream, axis=-1, keepdims=True) + 1e-06)).astype(
        jnp.bfloat16
    )
    context_count = lax.axis_size("ctx")
    head_groups = lax.axis_size("hd")
    expert_count = context_count * head_groups
    rows_here = normed.shape[0]
    slot_total = rows_here * TOP
    capacity = 2 * max(1, slot_total // expert_count)
    flat_ids = expert_ids.reshape(slot_total)
    onehot = (flat_ids[:, None] == jnp.arange(expert_count, dtype=jnp.int32)[None, :]).astype(
        jnp.int32
    )
    before = jnp.tril(jnp.ones((slot_total, slot_total), jnp.float32), -1)
    earlier = jnp.dot(
        before, onehot.astype(jnp.float32), precision=lax.Precision.HIGHEST
    ).astype(jnp.int32)
    position = jnp.sum(onehot * earlier, axis=1)
    target_row = flat_ids * capacity + position
    dispatch = (
        jnp.arange(expert_count * capacity, dtype=jnp.int32)[:, None] == target_row[None, :]
    ).astype(jnp.bfloat16)
    repeated = jnp.repeat(normed, TOP, axis=0)
    buffer = jnp.dot(dispatch, repeated, preferred_element_type=jnp.float32).astype(jnp.bfloat16)
    buffer = buffer.reshape(expert_count, capacity, model_width)
    slot_block = lax.all_to_all(buffer, ("ctx", "hd"), split_axis=0, concat_axis=0, tiled=True)
    sources, slot_count, feature_width = slot_block.shape
    flattened = slot_block.reshape(sources * slot_count, feature_width)
    gate_values = jnp.dot(flattened, w_gate[0], preferred_element_type=jnp.float32)
    up_values = jnp.dot(flattened, w_up[0], preferred_element_type=jnp.float32)
    hidden = (jax.nn.silu(gate_values) * up_values).astype(jnp.bfloat16)
    result = jnp.dot(hidden, w_down[0], preferred_element_type=jnp.float32).astype(jnp.bfloat16)
    returned_rows = lax.all_to_all(
        result.reshape(sources, slot_count, feature_width),
        ("ctx", "hd"),
        split_axis=0,
        concat_axis=0,
        tiled=True,
    )
    gathered = jnp.dot(
        dispatch.T,
        returned_rows.reshape(expert_count * capacity, model_width),
        preferred_element_type=jnp.float32,
    )
    weighted = gathered.reshape(rows_here, TOP, model_width) * gate_weights[:, :, None]
    mixture = jnp.sum(weighted, axis=1)
    return (stream + mixture).astype(jnp.bfloat16)


MESH = pl.DeviceIdType.MESH


def layer_kernel(
    ctxs,
    cores,
    q_ref,
    k_ref,
    v_ref,
    ow_ref,
    res_ref,
    ids_ref,
    gw_ref,
    wg_ref,
    wu_ref,
    wd_ref,
    out_ref,
    res_v,
    ids_v,
    gw_v,
    kraw,
    vraw,
    tmp,
    kd,
    vd,
    qbuf,
    qf,
    qh,
    w2,
    wg,
    wu,
    wd,
    numbuf,
    stbuf,
    numrecv,
    strecv,
    wst,
    wt,
    att,
    pjbuf,
    pjrecv,
    xbuf,
    xg,
    xs,
    ybuf,
    yrecv,
    load_sem,
    q_send,
    q_recv,
    ow_send,
    ow_recv,
    num_send,
    num_recv,
    st_send,
    st_recv,
    pj_send,
    pj_recv,
    x_send,
    x_recv,
    y_send,
    y_recv,
):
    mc = lax.axis_index("ctx")
    mh = lax.axis_index("hd")
    devices = ctxs * cores
    me = mc * cores + mh
    rows, width = res_ref.shape
    own, _, share_heads, head = q_ref.shape
    groups, positions, _ = kd.shape
    turns, pairs, _, pair_count = numbuf.shape[:4]
    tokens = own * ctxs
    half = tokens // cores
    rate = head ** (-0.5) * math.log2(math.e)

    def remote(src, dst, ssem, rsem, c, h):
        return pltpu.make_async_remote_copy(
            src_ref=src,
            dst_ref=dst,
            send_sem=ssem,
            recv_sem=rsem,
            device_id={"ctx": c, "hd": h},
            device_id_type=MESH,
        )

    def peer(step):
        c, bit = mc, 1
        while bit < ctxs:
            if step & bit:
                c = c + (1 - 2 * lax.rem(mc // bit, 2)) * bit
            bit *= 2
        return c

    ctx_peer = [peer(step) for step in range(ctxs)]
    core_peer = [mh, cores - 1 - mh]
    mz = mc // pairs
    half_turns = turns // groups
    steps = [(kc, kh) for kc in reversed(range(ctxs)) for kh in (1, 0)]

    def push(src, dst, ssem, rsem, c, h):
        other = c * cores + h

        @pl.when(other != me)
        def _():
            remote(src, dst, ssem, rsem, c, h).start()

        @pl.when(other == me)
        def _():
            pltpu.make_async_copy(src, dst, rsem).start()

    def sent(src, ssem):
        pltpu.make_async_copy(src, src, ssem).wait()

    def landed(dst, rsem):
        pltpu.make_async_copy(dst, dst, rsem).wait()

    drains = []
    loads = [
        pltpu.make_async_copy(a, b, load_sem.at[i])
        for i, (a, b) in enumerate(
            (
                (k_ref, kraw),
                (v_ref, vraw),
                (ow_ref, w2.at[mh]),
                (wg_ref, wg),
                (wu_ref, wu),
                (wd_ref, wd),
                (res_ref, res_v),
                (ids_ref, ids_v),
                (gw_ref, gw_v),
            )
        )
    ]
    barrier = pltpu.get_barrier_semaphore()
    for kc, kh in steps[:-1]:
        pl.semaphore_signal(
            barrier,
            inc=1,
            device_id={"ctx": ctx_peer[kc], "hd": core_peer[kh]},
            device_id_type=MESH,
        )
    for one in loads[:2] + loads[6:]:
        one.start()

    piece = tmp.shape[0]
    share = piece // groups

    def split(raw, store):
        @pl.loop(0, raw.shape[0] // piece)
        def _(i):
            tmp[...] = raw[pl.ds(pl.multiple_of(i * piece, piece), piece), :].astype(jnp.float32)
            for g in range(groups):
                store(g, i, tmp[pl.ds(g, share, stride=groups), :].astype(jnp.bfloat16))

    def store_k(g, i, value):
        kd[g, pl.ds(pl.multiple_of(i * share, share), share), :] = value

    def store_v(g, i, value):
        at = pl.ds(pl.multiple_of(i * share, share), share)
        vd[g, at, 0:head] = value
        vd[g, at, head : 2 * head] = jnp.ones_like(value)

    loads[0].wait()
    split(kraw, store_k)
    loads[1].wait()
    split(vraw, store_v)
    wst[...] = jnp.zeros_like(wst)
    for one in loads[6:]:
        one.wait()
    gates = []
    for e in range(devices):
        gates.append(jnp.sum(jnp.where(ids_v[...] == e, gw_v[...], 0.0), axis=1, keepdims=True))

    pl.semaphore_wait(barrier, devices - 1)

    def group_of(c, far):
        g = c // (ctxs // groups)
        return 1 - g if far else g

    for far in (1, 0):
        for kc in reversed(range(ctxs)):
            c = ctx_peer[kc]
            g = group_of(c, far)
            src, dst, rsem = q_ref.at[:, g], qbuf.at[mc, g], q_recv.at[mc, g]
            if kc:
                remote(src, dst, q_send.at[kc, far], rsem, c, mh).start()
            else:
                pltpu.make_async_copy(src, dst, rsem).start()
    ow_copy = remote(ow_ref, w2.at[mh], ow_send, ow_recv, mc, cores - 1 - mh)
    ow_copy.start()
    for one in loads[2:6]:
        one.start()

    def drain_q():
        for far in (1, 0):
            for kc in range(1, ctxs):
                sent(q_ref.at[:, 0], q_send.at[kc, far])

    drains.append(drain_q)
    block = pairs * pair_count * tokens
    pair_rows = pair_count * tokens
    lanes = lax.broadcasted_iota(jnp.int32, (pair_rows, head), 1)
    for far in (1, 0):
        g = group_of(mc, far)
        per = own * share_heads
        for c in range(ctxs):
            landed(qbuf.at[c, g], q_recv.at[c, g])
            qf[c * per : (c + 1) * per, :] = (
                qbuf[c, g].astype(jnp.float32).reshape(per, head)
            )
        for h in range(share_heads):
            qh[far, h * tokens : (h + 1) * tokens, :] = qf[
                pl.ds(h, tokens, stride=share_heads), :
            ].astype(jnp.bfloat16)
        for near in reversed(range(half_turns)):
            kz = far * half_turns + near
            turn = ctx_peer[kz * pairs] // pairs
            at = lax.rem(turn, half_turns) * block
            q = qh[far, pl.ds(pl.multiple_of(at, block), block), :]
            s = lax.dot_general(
                q, kd[g], (((1,), (1,)), ((), ())), preferred_element_type=jnp.float32
            )
            m = jnp.max(s, axis=1, keepdims=True)
            p = jnp.exp2((s - m) * rate).astype(jnp.bfloat16)
            o = jnp.dot(p, vd[g], preferred_element_type=jnp.float32)
            for j in range(pairs):
                c = turn * pairs + j
                base = j * pair_rows
                for b in range(cores):
                    for a in range(pair_count):
                        at = base + a * tokens + b * half
                        numbuf[kz, j, b, a] = o[at : at + half, 0:head].astype(jnp.bfloat16)
                rows_here = slice(base, base + pair_rows)
                stat = jnp.where(lanes == 0, m[rows_here], o[rows_here, head : 2 * head])
                stbuf[kz, j] = stat.T[0:2]
                for b in range(cores):
                    go = remote if kz else push
                    for src, dst, ssem, rsem in (
                        (stbuf.at[kz, j], strecv, st_send, st_recv),
                        (numbuf.at[kz, j, b], numrecv, num_send, num_recv),
                    ):
                        copy = go(
                            src, dst.at[mc, mh], ssem.at[kz, j, b], rsem.at[mc, mh], c, b
                        )
                        if kz:
                            copy.start()

    def drain_num():
        for kz in range(turns):
            for j in range(pairs):
                for b in range(cores):

                    def both(kz=kz, j=j, b=b):
                        sent(stbuf.at[kz, j], st_send.at[kz, j, b])
                        sent(numbuf.at[kz, j, b], num_send.at[kz, j, b])

                    if kz:
                        both()
                    else:
                        pl.when((mz * pairs + j) * cores + b != me)(both)

    drains.append(drain_num)
    for h in range(cores):
        peaks, totals = [], []
        for c in range(ctxs):
            landed(strecv.at[c, h], st_recv.at[c, h])
            peaks.append(strecv[c, h, 0:1, :])
            totals.append(strecv[c, h, 1:2, :])
        peaks = jnp.concatenate(peaks, axis=0)
        totals = jnp.concatenate(totals, axis=0)
        factor = jnp.exp2((peaks - jnp.max(peaks, axis=0, keepdims=True)) * rate)
        wst[h * ctxs : (h + 1) * ctxs, :] = factor / jnp.sum(
            totals * factor, axis=0, keepdims=True
        )
    wt[...] = wst[...].T
    for h in range(cores):
        for c in range(ctxs):
            landed(numrecv.at[c, h], num_recv.at[c, h])
        for a in range(pair_count):
            shares = wt[pl.ds(pl.multiple_of(a * tokens + mh * half, half), half), :]
            total = jnp.zeros((half, head), jnp.float32)
            for c in range(ctxs):
                at = h * ctxs + c
                total = total + numrecv[c, h, a].astype(jnp.float32) * shares[:, at : at + 1]
            at = (h * pair_count + a) * head
            att[:, at : at + head] = total.astype(jnp.bfloat16)

    loads[2].wait()
    ow_copy.wait()
    depth = w2.shape[1]
    projected = jnp.dot(att[:, 0:depth], w2[0], preferred_element_type=jnp.float32)
    for h in range(1, cores):
        projected = projected + jnp.dot(
            att[:, h * depth : (h + 1) * depth], w2[h], preferred_element_type=jnp.float32
        )
    targets = half // rows
    for j in range(targets):
        pjbuf[j] = projected[j * rows : (j + 1) * rows].astype(jnp.bfloat16)

    chips = targets // cores
    low = lax.rem(mc, chips)
    for kc in reversed(range(chips)):
        for kh in (1, 0):
            c = mh * chips + ctx_peer[kc] - (mc - low)
            h = core_peer[kh]
            j = (c - mh * chips) * cores + h
            go = remote if kc or kh else push
            k = kc * cores + kh
            copy = go(pjbuf.at[j], pjrecv.at[mc], pj_send.at[k], pj_recv.at[mc], c, h)
            if kc or kh:
                copy.start()

    def drain_pj():
        for k in range(1, targets):
            sent(pjbuf.at[0], pj_send.at[k])

        @pl.when(mh * chips != mc - low)
        def _():
            sent(pjbuf.at[0], pj_send.at[0])

    drains.append(drain_pj)
    stream = res_v[...].astype(jnp.float32)
    for c in range(ctxs):
        landed(pjrecv.at[c], pj_recv.at[c])
        stream = stream + pjrecv[c].astype(jnp.float32)
    square = jnp.mean(stream * stream, axis=-1, keepdims=True)
    xbuf[...] = (stream * lax.rsqrt(square + 1e-06)).astype(jnp.bfloat16)

    partner = core_peer[1]
    for kc in reversed(range(1, ctxs)):
        remote(
            xbuf, xg.at[me], x_send.at[kc * cores], x_recv.at[me], ctx_peer[kc], mh
        ).start()
    remote(xbuf, xg.at[me], x_send.at[1], x_recv.at[me], mc, partner).start()
    pltpu.make_async_copy(xbuf, xg.at[me], x_recv.at[me]).start()
    for kc in range(1, ctxs):
        came = ctx_peer[kc] * cores + mh
        landed(xg.at[came], x_recv.at[came])
        remote(
            xg.at[came],
            xg.at[came],
            x_send.at[kc * cores + 1],
            x_recv.at[came],
            mc,
            partner,
        ).start()

    def drain_x():
        for k in range(1, devices):
            sent(xbuf, x_send.at[k])

    drains.append(drain_x)
    for one in loads[3:6]:
        one.wait()
    landed(xg.at[me], x_recv.at[me])
    for c in range(ctxs):
        came = c * cores + partner
        landed(xg.at[came], x_recv.at[came])
    for d in range(devices):
        xs[d * rows : (d + 1) * rows, :] = xg[d].astype(jnp.float32)
    x = xs[...].astype(jnp.bfloat16)
    gate_values = jnp.dot(x, wg[...], preferred_element_type=jnp.float32)
    up_values = jnp.dot(x, wu[...], preferred_element_type=jnp.float32)
    hidden = (gate_values / (1.0 + jnp.exp(-gate_values)) * up_values).astype(jnp.bfloat16)
    result = jnp.dot(hidden, wd[...], preferred_element_type=jnp.float32)
    for d in range(devices):
        ybuf[d] = result[d * rows : (d + 1) * rows].astype(jnp.bfloat16)

    for kc, kh in steps:
        c, h = ctx_peer[kc], core_peer[kh]
        other = c * cores + h
        if kc or kh:
            remote(
                ybuf.at[other], yrecv.at[me], y_send.at[kc * cores + kh], y_recv.at[me], c, h
            ).start()
        else:
            pltpu.make_async_copy(ybuf.at[other], yrecv.at[me], y_recv.at[me]).start()

    def drain_y():
        for k in range(1, devices):
            sent(ybuf.at[0], y_send.at[k])

    drains.append(drain_y)
    mixture = jnp.zeros_like(stream)
    for d in range(devices):
        landed(yrecv.at[d], y_recv.at[d])
        mixture = mixture + yrecv[d].astype(jnp.float32) * gates[d]
    out_ref[...] = (stream + mixture).astype(out_ref.dtype)

    for drain in drains:
        drain()


def on_device(
    queries,
    prefix_keys,
    prefix_values,
    out_weight,
    residual_in,
    expert_ids,
    gate_weights,
    w_gate,
    w_up,
    w_down,
):
    ctxs, cores = lax.axis_size("ctx"), lax.axis_size("hd")
    devices = ctxs * cores
    own, heads, head = queries.shape
    positions, groups, _ = prefix_keys.shape
    depth, width = out_weight.shape
    rows = residual_in.shape[0]
    ffn = w_gate.shape[2]
    tokens = own * ctxs
    pair_count = heads // ctxs
    fits = (
        cores == 2
        and pair_count * ctxs == heads
        and pair_count * tokens == head
        and ctxs % 8 == 0
        and ctxs & (ctxs - 1) == 0
        and groups == 2
        and cores * ctxs <= head
    )
    if not fits:
        return on_device_general(
            queries,
            prefix_keys,
            prefix_values,
            out_weight,
            residual_in,
            expert_ids,
            gate_weights,
            w_gate,
            w_up,
            w_down,
        )
    half = tokens // cores
    any_spec = pl.BlockSpec(memory_space=pl.ANY)
    vmem_spec = pl.BlockSpec(memory_space=pltpu.VMEM)
    bf, f32 = jnp.bfloat16, jnp.float32
    dma = pltpu.SemaphoreType.DMA
    return pl.pallas_call(
        functools.partial(layer_kernel, ctxs, cores),
        out_shape=jax.ShapeDtypeStruct((rows, width), bf),
        in_specs=[any_spec] * 10,
        out_specs=vmem_spec,
        scratch_shapes=[
            pltpu.VMEM(residual_in.shape, bf),
            pltpu.VMEM(expert_ids.shape, expert_ids.dtype),
            pltpu.VMEM(gate_weights.shape, f32),
            pltpu.VMEM((positions * groups, head), bf),
            pltpu.VMEM((positions * groups, head), bf),
            pltpu.VMEM((256 * groups, head), f32),
            pltpu.VMEM((groups, positions, head), bf),
            pltpu.VMEM((groups, positions, 2 * head), bf),
            pltpu.VMEM((ctxs, groups, own, heads // groups, head), bf),
            pltpu.VMEM((tokens * heads // groups, head), f32),
            pltpu.VMEM((groups, heads // groups * tokens, head), bf),
            pltpu.VMEM((cores, depth, width), bf),
            pltpu.VMEM((width, ffn), bf),
            pltpu.VMEM((width, ffn), bf),
            pltpu.VMEM((ffn, width), bf),
            pltpu.VMEM((ctxs // 2, 2, cores, pair_count, half, head), bf),
            pltpu.VMEM((ctxs // 2, 2, 2, head), f32),
            pltpu.VMEM((ctxs, cores, pair_count, half, head), bf),
            pltpu.VMEM((ctxs, cores, 2, head), f32),
            pltpu.VMEM((head, head), f32),
            pltpu.VMEM((head, head), f32),
            pltpu.VMEM((half, cores * depth), bf),
            pltpu.VMEM((half // rows, rows, width), bf),
            pltpu.VMEM((ctxs, rows, width), bf),
            pltpu.VMEM((rows, width), bf),
            pltpu.VMEM((devices, rows, width), bf),
            pltpu.VMEM((devices * rows, width), f32),
            pltpu.VMEM((devices, rows, width), bf),
            pltpu.VMEM((devices, rows, width), bf),
            dma((9,)),
            dma((ctxs, groups)),
            dma((ctxs, groups)),
            dma,
            dma,
            dma((ctxs // 2, 2, cores)),
            dma((ctxs, cores)),
            dma((ctxs // 2, 2, cores)),
            dma((ctxs, cores)),
            dma((half // rows,)),
            dma((ctxs,)),
            dma((devices,)),
            dma((devices,)),
            dma((devices,)),
            dma((devices,)),
        ],
        compiler_params=pltpu.CompilerParams(
            collective_id=0, has_side_effects=True, vmem_limit_bytes=60 * 1024 * 1024
        ),
    )(
        queries.reshape(own, groups, heads // groups, head),
        prefix_keys.reshape(positions * groups, head),
        prefix_values.reshape(positions * groups, head),
        out_weight,
        residual_in,
        expert_ids,
        gate_weights,
        w_gate[0],
        w_up[0],
        w_down[0],
    )


def solution(mesh):
    placed = (
        P(("grp", "ctx"), "hd", None),
        P(("grp", "ctx"), "hd", None),
        P(("grp", "ctx"), "hd", None),
        P(("hd", "ctx"), None),
        P(("grp", "ctx", "hd"), None),
        P(("grp", "ctx", "hd"), None),
        P(("grp", "ctx", "hd"), None),
        P(("ctx", "hd"), None, None),
        P(("ctx", "hd"), None, None),
        P(("ctx", "hd"), None, None),
    )
    return jax.shard_map(
        on_device,
        mesh=mesh,
        in_specs=placed,
        out_specs=P(("grp", "ctx", "hd"), None),
        check_vma=False,
    )
```

```python
import jax
import jax.numpy as jnp
from jax import lax
from jax.experimental import pallas as pl
from jax.experimental.pallas import tpu as pltpu
from jax.sharding import PartitionSpec as P
import functools
import math

TOP = 8
KV_BLOCK = 512


NEG_START = -1e30


def local_attention(queries, prefix_keys, prefix_values):
    token_count, heads_local, head_width = queries.shape
    key_heads = prefix_keys.shape[1]
    grouped = heads_local // key_heads
    query_view = queries.reshape(token_count, key_heads, grouped, head_width)
    block_count = prefix_keys.shape[0] // KV_BLOCK
    key_blocks = prefix_keys.reshape(block_count, KV_BLOCK, key_heads, head_width)
    value_blocks = prefix_values.reshape(block_count, KV_BLOCK, key_heads, head_width)
    scaling = head_width ** (-0.5)

    def advance(running, pieces):
        peak_scores, totals, accumulated = running
        key_piece, value_piece = pieces
        scores = (
            jnp.einsum("sgjd,kgd->sgjk", query_view, key_piece, preferred_element_type=jnp.float32)
            * scaling
        )
        block_peak = jnp.max(scores, axis=-1)
        weights = jnp.exp(scores - block_peak[..., None]).astype(jnp.bfloat16)
        block_total = jnp.sum(weights.astype(jnp.float32), axis=-1)
        block_out = jnp.einsum(
            "sgjk,kgd->sgjd", weights, value_piece, preferred_element_type=jnp.float32
        )
        raised = jnp.maximum(peak_scores, block_peak)
        old_factor = jnp.exp(peak_scores - raised)
        new_factor = jnp.exp(block_peak - raised)
        totals = totals * old_factor + block_total * new_factor
        accumulated = accumulated * old_factor[..., None] + block_out * new_factor[..., None]
        return ((raised, totals, accumulated), None)

    start_state = (
        jnp.full((token_count, key_heads, grouped), NEG_START, jnp.float32),
        jnp.zeros((token_count, key_heads, grouped), jnp.float32),
        jnp.zeros((token_count, key_heads, grouped, head_width), jnp.float32),
    )
    final_state, leftover = lax.scan(advance, start_state, (key_blocks, value_blocks))
    peak_scores = final_state[0].reshape(token_count, heads_local)
    totals = final_state[1].reshape(token_count, heads_local)
    accumulated = final_state[2].reshape(token_count, heads_local, head_width)
    return (peak_scores, totals, accumulated)


def on_device_general(
    queries,
    prefix_keys,
    prefix_values,
    out_weight,
    residual_in,
    expert_ids,
    gate_weights,
    w_gate,
    w_up,
    w_down,
):
    every_query = lax.all_gather(queries, "ctx", axis=0, tiled=True)
    peak_scores, totals, accumulated = local_attention(every_query, prefix_keys, prefix_values)
    token_count, heads_local, head_width = accumulated.shape
    top_peak = lax.pmax(peak_scores, "ctx")
    factor = jnp.exp(peak_scores - top_peak)
    scaled_totals = totals * factor
    scaled_accum = (accumulated * factor[..., None]).reshape(token_count, heads_local * head_width)
    model_width = out_weight.shape[1]
    column_accum = lax.psum_scatter(
        scaled_accum.astype(jnp.bfloat16), "ctx", scatter_dimension=1, tiled=True
    ).astype(jnp.float32)
    all_totals = lax.psum(scaled_totals, "ctx")
    width_here = column_accum.shape[1]
    column_ids = lax.axis_index("ctx") * width_here + jnp.arange(width_here, dtype=jnp.int32)
    selector = (
        (column_ids // head_width)[None, :] == jnp.arange(heads_local, dtype=jnp.int32)[:, None]
    ).astype(jnp.float32)
    denominators = jnp.dot(all_totals, selector, precision=lax.Precision.HIGHEST)
    attended = (column_accum / denominators).astype(jnp.bfloat16)
    projected = lax.psum_scatter(
        jnp.dot(attended, out_weight, preferred_element_type=jnp.float32),
        ("ctx", "hd"),
        scatter_dimension=0,
        tiled=True,
    )
    stream = residual_in.astype(jnp.float32) + projected
    normed = (stream * lax.rsqrt(jnp.mean(stream * stream, axis=-1, keepdims=True) + 1e-06)).astype(
        jnp.bfloat16
    )
    context_count = lax.axis_size("ctx")
    head_groups = lax.axis_size("hd")
    expert_count = context_count * head_groups
    rows_here = normed.shape[0]
    slot_total = rows_here * TOP
    capacity = 2 * max(1, slot_total // expert_count)
    flat_ids = expert_ids.reshape(slot_total)
    onehot = (flat_ids[:, None] == jnp.arange(expert_count, dtype=jnp.int32)[None, :]).astype(
        jnp.int32
    )
    before = jnp.tril(jnp.ones((slot_total, slot_total), jnp.float32), -1)
    earlier = jnp.dot(
        before, onehot.astype(jnp.float32), precision=lax.Precision.HIGHEST
    ).astype(jnp.int32)
    position = jnp.sum(onehot * earlier, axis=1)
    target_row = flat_ids * capacity + position
    dispatch = (
        jnp.arange(expert_count * capacity, dtype=jnp.int32)[:, None] == target_row[None, :]
    ).astype(jnp.bfloat16)
    repeated = jnp.repeat(normed, TOP, axis=0)
    buffer = jnp.dot(dispatch, repeated, preferred_element_type=jnp.float32).astype(jnp.bfloat16)
    buffer = buffer.reshape(expert_count, capacity, model_width)
    slot_block = lax.all_to_all(buffer, ("ctx", "hd"), split_axis=0, concat_axis=0, tiled=True)
    sources, slot_count, feature_width = slot_block.shape
    flattened = slot_block.reshape(sources * slot_count, feature_width)
    gate_values = jnp.dot(flattened, w_gate[0], preferred_element_type=jnp.float32)
    up_values = jnp.dot(flattened, w_up[0], preferred_element_type=jnp.float32)
    hidden = (jax.nn.silu(gate_values) * up_values).astype(jnp.bfloat16)
    result = jnp.dot(hidden, w_down[0], preferred_element_type=jnp.float32).astype(jnp.bfloat16)
    returned_rows = lax.all_to_all(
        result.reshape(sources, slot_count, feature_width),
        ("ctx", "hd"),
        split_axis=0,
        concat_axis=0,
        tiled=True,
    )
    gathered = jnp.dot(
        dispatch.T,
        returned_rows.reshape(expert_count * capacity, model_width),
        preferred_element_type=jnp.float32,
    )
    weighted = gathered.reshape(rows_here, TOP, model_width) * gate_weights[:, :, None]
    mixture = jnp.sum(weighted, axis=1)
    return (stream + mixture).astype(jnp.bfloat16)


MESH = pl.DeviceIdType.MESH


def layer_kernel(
    ctxs,
    cores,
    q_ref,
    k_ref,
    v_ref,
    ow_ref,
    res_ref,
    ids_ref,
    gw_ref,
    wg_ref,
    wu_ref,
    wd_ref,
    out_ref,
    res_v,
    ids_v,
    gw_v,
    kraw,
    vraw,
    tmp,
    kd,
    vd,
    qbuf,
    qf,
    qh,
    w2,
    wg,
    wu,
    wd,
    numbuf,
    stbuf,
    numrecv,
    strecv,
    wst,
    wt,
    att,
    pjbuf,
    pjrecv,
    xbuf,
    xg,
    xs,
    gx,
    mine,
    give,
    take,
    ybuf,
    yrecv,
    load_sem,
    q_send,
    q_recv,
    ow_send,
    ow_recv,
    num_send,
    num_recv,
    st_send,
    st_recv,
    pj_send,
    pj_recv,
    x_send,
    x_recv,
    give_send,
    take_recv,
    y_send,
    y_recv,
):
    mc = lax.axis_index("ctx")
    mh = lax.axis_index("hd")
    devices = ctxs * cores
    me = mc * cores + mh
    rows, width = res_ref.shape
    own, groups, share_heads, head = q_ref.shape
    turns, targets_in_turn, pair_rows, _ = numbuf.shape
    tokens = own * ctxs
    half = tokens // cores
    pair_count = pair_rows // half
    rate = head ** (-0.5) * math.log2(math.e)

    def remote(src, dst, ssem, rsem, c, h):
        return pltpu.make_async_remote_copy(
            src_ref=src,
            dst_ref=dst,
            send_sem=ssem,
            recv_sem=rsem,
            device_id={"ctx": c, "hd": h},
            device_id_type=MESH,
        )

    def peer(step):
        c, bit = mc, 1
        while bit < ctxs:
            if step & bit:
                c = c + (1 - 2 * lax.rem(mc // bit, 2)) * bit
            bit *= 2
        return c

    ctx_peer = [peer(step) for step in range(ctxs)]
    core_peer = [mh, cores - 1 - mh]
    steps = [(kc, kh) for kc in reversed(range(ctxs)) for kh in (1, 0)]

    def push(src, dst, ssem, rsem, c, h):
        other = c * cores + h

        @pl.when(other != me)
        def _():
            remote(src, dst, ssem, rsem, c, h).start()

        @pl.when(other == me)
        def _():
            pltpu.make_async_copy(src, dst, rsem).start()

    def sent(src, ssem):
        pltpu.make_async_copy(src, src, ssem).wait()

    def landed(dst, rsem):
        pltpu.make_async_copy(dst, dst, rsem).wait()

    drains = []
    loads = [
        pltpu.make_async_copy(a, b, load_sem.at[i])
        for i, (a, b) in enumerate(
            (
                (k_ref, kraw),
                (v_ref, vraw),
                (ow_ref, w2.at[mh]),
                (wg_ref, wg),
                (wu_ref, wu),
                (wd_ref, wd),
                (res_ref, res_v),
                (ids_ref, ids_v),
                (gw_ref, gw_v),
            )
        )
    ]
    barrier = pltpu.get_barrier_semaphore()
    for kc, kh in steps[:-1]:
        pl.semaphore_signal(
            barrier,
            inc=1,
            device_id={"ctx": ctx_peer[kc], "hd": core_peer[kh]},
            device_id_type=MESH,
        )
    for one in loads[:2] + loads[6:]:
        one.start()

    pl.semaphore_wait(barrier, devices - 1)
    for kc in range(1, ctxs):
        remote(
            q_ref, qbuf.at[mc], q_send.at[kc], q_recv.at[mc], ctx_peer[kc], mh
        ).start()
    pltpu.make_async_copy(q_ref, qbuf.at[mc], q_recv.at[mc]).start()
    ow_copy = remote(ow_ref, w2.at[mh], ow_send, ow_recv, mc, cores - 1 - mh)
    ow_copy.start()
    for one in loads[2:6]:
        one.start()

    def drain_q():
        for kc in range(1, ctxs):
            sent(q_ref, q_send.at[kc])

    drains.append(drain_q)
    piece = tmp.shape[0]
    share = piece // groups

    def split(raw, store):
        @pl.loop(0, raw.shape[0] // piece)
        def _(i):
            tmp[...] = raw[pl.ds(pl.multiple_of(i * piece, piece), piece), :].astype(jnp.float32)
            for g in range(groups):
                store(g, i, tmp[pl.ds(g, share, stride=groups), :].astype(jnp.bfloat16))

    def store_k(g, i, value):
        kd[g, pl.ds(pl.multiple_of(i * share, share), share), :] = value

    def store_v(g, i, value):
        at = pl.ds(pl.multiple_of(i * share, share), share)
        vd[g, at, 0:head] = value
        vd[g, at, head : 2 * head] = jnp.ones_like(value)

    loads[0].wait()
    split(kraw, store_k)
    loads[1].wait()
    split(vraw, store_v)
    wst[...] = jnp.zeros_like(wst)
    for one in loads[6:]:
        one.wait()
    lane = lax.broadcasted_iota(jnp.int32, (rows, head), 1)
    offset = lane - lax.broadcasted_iota(jnp.int32, (rows, head), 0)
    spread = jnp.zeros((rows, head), jnp.float32)
    for e in range(devices):
        gate = jnp.sum(jnp.where(ids_v[...] == e, gw_v[...], 0.0), axis=1, keepdims=True)
        spread = spread + jnp.where(offset == e * rows, gate, 0.0)
    gates = jnp.sum(spread, axis=0, keepdims=True)

    sources = ctxs // cores
    here, there = mc // sources, mc // targets_in_turn
    lanes = lax.broadcasted_iota(jnp.int32, (2 * pair_rows, head), 1)
    for far in (0, 1):
        part = here if far == 0 else 1 - here
        per = own * share_heads
        for i in range(sources):
            c = part * sources + i
            landed(qbuf.at[c], q_recv.at[c])
            for g in range(groups):
                qf[g, i * per : (i + 1) * per, :] = (
                    qbuf[c, :, g].astype(jnp.float32).reshape(per, head)
                )
        for g in range(groups):
            for h in range(share_heads):
                qh[g, h * half : (h + 1) * half, :] = qf[
                    g, pl.ds(h, half, stride=share_heads), :
                ].astype(jnp.bfloat16)
        for near in (0, 1):
            turn = 2 * far + near
            g = there if near else 1 - there
            s = lax.dot_general(
                qh[g], kd[g], (((1,), (1,)), ((), ())), preferred_element_type=jnp.float32
            )
            m = jnp.max(s, axis=1, keepdims=True)
            p = jnp.exp2((s - m) * rate).astype(jnp.bfloat16)
            o = jnp.dot(p, vd[g], preferred_element_type=jnp.float32)
            for i in range(targets_in_turn):
                at = i * pair_rows
                numbuf[turn, i] = o[at : at + pair_rows, 0:head].astype(jnp.bfloat16)
                if i % 2 == 0:
                    both = slice(at, at + 2 * pair_rows)
                    stat = jnp.where(lanes == 0, m[both], o[both, head : 2 * head])
                    stbuf[turn, i // 2, 0:2] = stat.T[0:2]
                    stbuf[turn, i // 2, 2:3] = gates
            for i in range(targets_in_turn):
                c = g * targets_in_turn + i
                for src, dst, ssem, rsem in (
                    (stbuf.at[turn, i // 2], strecv, st_send, st_recv),
                    (numbuf.at[turn, i], numrecv, num_send, num_recv),
                ):
                    args = (src, dst.at[mc, mh], ssem.at[turn, i], rsem.at[mc, mh], c, part)
                    if near:
                        push(*args)
                    else:
                        remote(*args).start()

    def drain_num():
        for turn in range(turns):
            part = here if turn < 2 else 1 - here
            for i in range(targets_in_turn):

                def both(turn=turn, i=i):
                    sent(stbuf.at[turn, 0], st_send.at[turn, i])
                    sent(numbuf.at[turn, i], num_send.at[turn, i])

                if turn % 2 == 0:
                    both()
                else:
                    pl.when((there * targets_in_turn + i) * cores + part != me)(both)

    drains.append(drain_num)
    for h in range(cores):
        peaks, totals = [], []
        for c in range(ctxs):
            landed(strecv.at[c, h], st_recv.at[c, h])
            peaks.append(strecv[c, h, 0:1, :])
            totals.append(strecv[c, h, 1:2, :])
        peaks = jnp.concatenate(peaks, axis=0)
        totals = jnp.concatenate(totals, axis=0)
        factor = jnp.exp2((peaks - jnp.max(peaks, axis=0, keepdims=True)) * rate)
        wst[h * ctxs : (h + 1) * ctxs, :] = factor / jnp.sum(
            totals * factor, axis=0, keepdims=True
        )
    wt[...] = wst[...].T
    for h in range(cores):
        for c in range(ctxs):
            landed(numrecv.at[c, h], num_recv.at[c, h])
        for a in range(pair_count):
            at = lax.rem(mc, 2) * pair_rows + a * half
            shares = wt[pl.ds(pl.multiple_of(at, half), half), :]
            total = jnp.zeros((half, head), jnp.float32)
            for c in range(ctxs):
                at = h * ctxs + c
                total = total + numrecv[c, h, a * half : (a + 1) * half].astype(jnp.float32) * shares[:, at : at + 1]
            at = (h * pair_count + a) * head
            att[:, at : at + head] = total.astype(jnp.bfloat16)

    partner = core_peer[1]
    for h, core in enumerate((mh, partner)):
        for c in range(ctxs):
            at = (h * ctxs + c) * rows
            gx[at : at + rows, :] = jnp.broadcast_to(strecv[c, core, 2:3, :], (rows, head))
    row = lax.broadcasted_iota(jnp.int32, gx.shape, 0)
    lane = lax.broadcasted_iota(jnp.int32, gx.shape, 1)
    gate = jnp.sum(
        jnp.where(lane == me * rows + lax.rem(row, rows), gx[...], 0.0), axis=1, keepdims=True
    )

    loads[2].wait()
    ow_copy.wait()
    depth = w2.shape[1]
    projected = jnp.dot(att[:, 0:depth], w2[0], preferred_element_type=jnp.float32)
    for h in range(1, cores):
        projected = projected + jnp.dot(
            att[:, h * depth : (h + 1) * depth], w2[h], preferred_element_type=jnp.float32
        )
    targets = half // rows
    for j in range(targets):
        pjbuf[j] = projected[j * rows : (j + 1) * rows].astype(jnp.bfloat16)

    chips = targets // cores
    low = lax.rem(mc, chips)
    for kc in reversed(range(chips)):
        for kh in (1, 0):
            c = mh * chips + ctx_peer[kc] - (mc - low)
            h = core_peer[kh]
            j = (c - mh * chips) * cores + h
            go = remote if kc or kh else push
            k = kc * cores + kh
            copy = go(pjbuf.at[j], pjrecv.at[mc], pj_send.at[k], pj_recv.at[mc], c, h)
            if kc or kh:
                copy.start()

    def drain_pj():
        for k in range(1, targets):
            sent(pjbuf.at[0], pj_send.at[k])

        @pl.when(mh * chips != mc - low)
        def _():
            sent(pjbuf.at[0], pj_send.at[0])

    drains.append(drain_pj)
    stream = res_v[...].astype(jnp.float32)
    for c in range(ctxs):
        landed(pjrecv.at[c], pj_recv.at[c])
        stream = stream + pjrecv[c].astype(jnp.float32)
    square = jnp.mean(stream * stream, axis=-1, keepdims=True)
    xbuf[...] = (stream * lax.rsqrt(square + 1e-06)).astype(jnp.bfloat16)

    for kc in reversed(range(1, ctxs)):
        remote(
            xbuf, xg.at[me], x_send.at[kc * cores], x_recv.at[me], ctx_peer[kc], mh
        ).start()
    remote(xbuf, xg.at[me], x_send.at[1], x_recv.at[me], mc, partner).start()
    pltpu.make_async_copy(xbuf, xg.at[me], x_recv.at[me]).start()
    for kc in range(1, ctxs):
        came = ctx_peer[kc] * cores + mh
        landed(xg.at[came], x_recv.at[came])
        remote(
            xg.at[came],
            xg.at[came],
            x_send.at[kc * cores + 1],
            x_recv.at[came],
            mc,
            partner,
        ).start()

    def drain_x():
        for k in range(1, devices):
            sent(xbuf, x_send.at[k])

    drains.append(drain_x)
    for one in loads[3:6]:
        one.wait()
    landed(xg.at[me], x_recv.at[me])
    for c in range(ctxs):
        came = c * cores + partner
        landed(xg.at[came], x_recv.at[came])
    for h, core in enumerate((mh, partner)):
        for c in range(ctxs):
            at = (h * ctxs + c) * rows
            xs[at : at + rows, :] = xg[c * cores + core].astype(jnp.float32)
    x = xs[...].astype(jnp.bfloat16)
    gate_values = jnp.dot(x, wg[...], preferred_element_type=jnp.float32)
    up_values = jnp.dot(x, wu[...], preferred_element_type=jnp.float32)
    hidden = (gate_values / (1.0 + jnp.exp(-gate_values)) * up_values).astype(jnp.bfloat16)

    chunks, near_rows, cut = mine.shape
    for k in range(chunks):
        result = gate * jnp.dot(
            hidden, wd[:, k * cut : (k + 1) * cut], preferred_element_type=jnp.float32
        )
        mine[k] = result[0:near_rows]
        give[k] = result[near_rows:].astype(jnp.bfloat16)
        remote(give.at[k], take.at[k], give_send.at[k], take_recv.at[k], mc, partner).start()
    for k in range(chunks):
        landed(take.at[k], take_recv.at[k])
        total = mine[k] + take[k].astype(jnp.float32)
        for c in range(ctxs):
            ybuf[k, c] = total[c * rows : (c + 1) * rows].astype(jnp.bfloat16)
        for kc in reversed(range(1, ctxs)):
            c = ctx_peer[kc]
            remote(
                ybuf.at[k, c], yrecv.at[k, mc], y_send.at[k, kc], y_recv.at[k, mc], c, mh
            ).start()
        pltpu.make_async_copy(ybuf.at[k, mc], yrecv.at[k, mc], y_recv.at[k, mc]).start()

    def drain_y():
        for k in range(chunks):
            sent(give.at[k], give_send.at[k])
            for kc in range(1, ctxs):
                sent(ybuf.at[k, 0], y_send.at[k, kc])

    drains.append(drain_y)
    for k in range(chunks):
        mixture = stream[:, k * cut : (k + 1) * cut]
        for c in range(ctxs):
            landed(yrecv.at[k, c], y_recv.at[k, c])
            mixture = mixture + yrecv[k, c].astype(jnp.float32)
        out_ref[:, k * cut : (k + 1) * cut] = mixture.astype(out_ref.dtype)

    for drain in drains:
        drain()


def on_device(
    queries,
    prefix_keys,
    prefix_values,
    out_weight,
    residual_in,
    expert_ids,
    gate_weights,
    w_gate,
    w_up,
    w_down,
):
    ctxs, cores = lax.axis_size("ctx"), lax.axis_size("hd")
    devices = ctxs * cores
    own, heads, head = queries.shape
    positions, groups, _ = prefix_keys.shape
    depth, width = out_weight.shape
    rows = residual_in.shape[0]
    ffn = w_gate.shape[2]
    tokens = own * ctxs
    pair_count = heads // ctxs
    fits = (
        cores == 2
        and pair_count * ctxs == heads
        and pair_count * tokens == head
        and ctxs % 8 == 0
        and ctxs & (ctxs - 1) == 0
        and groups == 2
        and cores * ctxs <= head
        and devices * rows <= head
        and own * ctxs % (cores * 16) == 0
    )
    if not fits:
        return on_device_general(
            queries,
            prefix_keys,
            prefix_values,
            out_weight,
            residual_in,
            expert_ids,
            gate_weights,
            w_gate,
            w_up,
            w_down,
        )
    half = tokens // cores
    chunks = 2 if width % 256 == 0 else 1
    held = [
        pltpu.with_memory_space_constraint(a, pltpu.HBM)
        for a in (
            queries.reshape(own, groups, heads // groups, head),
            prefix_keys.reshape(positions * groups, head),
            prefix_values.reshape(positions * groups, head),
            out_weight,
            residual_in,
            expert_ids,
            gate_weights,
            w_gate[0],
            w_up[0],
            w_down[0],
        )
    ]
    any_spec = pl.BlockSpec(memory_space=pl.ANY)
    vmem_spec = pl.BlockSpec(memory_space=pltpu.VMEM)
    bf, f32 = jnp.bfloat16, jnp.float32
    dma = pltpu.SemaphoreType.DMA
    return pl.pallas_call(
        functools.partial(layer_kernel, ctxs, cores),
        out_shape=jax.ShapeDtypeStruct((rows, width), bf),
        in_specs=[any_spec] * 10,
        out_specs=vmem_spec,
        scratch_shapes=[
            pltpu.VMEM(residual_in.shape, bf),
            pltpu.VMEM(expert_ids.shape, expert_ids.dtype),
            pltpu.VMEM(gate_weights.shape, f32),
            pltpu.VMEM((positions * groups, head), bf),
            pltpu.VMEM((positions * groups, head), bf),
            pltpu.VMEM((256 * groups, head), f32),
            pltpu.VMEM((groups, positions, head), bf),
            pltpu.VMEM((groups, positions, 2 * head), bf),
            pltpu.VMEM((ctxs, own, groups, heads // groups, head), bf),
            pltpu.VMEM((groups, half * heads // groups, head), f32),
            pltpu.VMEM((groups, half * heads // groups, head), bf),
            pltpu.VMEM((cores, depth, width), bf),
            pltpu.VMEM((width, ffn), bf),
            pltpu.VMEM((width, ffn), bf),
            pltpu.VMEM((ffn, width), bf),
            pltpu.VMEM((cores * groups, ctxs // groups, pair_count * half, head), bf),
            pltpu.VMEM((cores * groups, ctxs // groups // 2, 3, head), f32),
            pltpu.VMEM((ctxs, cores, pair_count * half, head), bf),
            pltpu.VMEM((ctxs, cores, 3, head), f32),
            pltpu.VMEM((head, head), f32),
            pltpu.VMEM((head, head), f32),
            pltpu.VMEM((half, cores * depth), bf),
            pltpu.VMEM((half // rows, rows, width), bf),
            pltpu.VMEM((ctxs, rows, width), bf),
            pltpu.VMEM((rows, width), bf),
            pltpu.VMEM((devices, rows, width), bf),
            pltpu.VMEM((devices * rows, width), f32),
            pltpu.VMEM((devices * rows, head), f32),
            pltpu.VMEM((chunks, ctxs * rows, width // chunks), f32),
            pltpu.VMEM((chunks, ctxs * rows, width // chunks), bf),
            pltpu.VMEM((chunks, ctxs * rows, width // chunks), bf),
            pltpu.VMEM((chunks, ctxs, rows, width // chunks), bf),
            pltpu.VMEM((chunks, ctxs, rows, width // chunks), bf),
            dma((9,)),
            dma((ctxs,)),
            dma((ctxs,)),
            dma,
            dma,
            dma((cores * groups, ctxs // groups)),
            dma((ctxs, cores)),
            dma((cores * groups, ctxs // groups)),
            dma((ctxs, cores)),
            dma((half // rows,)),
            dma((ctxs,)),
            dma((devices,)),
            dma((devices,)),
            dma((chunks,)),
            dma((chunks,)),
            dma((chunks, ctxs)),
            dma((chunks, ctxs)),
        ],
        compiler_params=pltpu.CompilerParams(
            collective_id=0, has_side_effects=True, vmem_limit_bytes=32 * 1024 * 1024
        ),
    )(*held)


def solution(mesh):
    placed = (
        P(("grp", "ctx"), "hd", None),
        P(("grp", "ctx"), "hd", None),
        P(("grp", "ctx"), "hd", None),
        P(("hd", "ctx"), None),
        P(("grp", "ctx", "hd"), None),
        P(("grp", "ctx", "hd"), None),
        P(("grp", "ctx", "hd"), None),
        P(("ctx", "hd"), None, None),
        P(("ctx", "hd"), None, None),
        P(("ctx", "hd"), None, None),
    )
    return jax.shard_map(
        on_device,
        mesh=mesh,
        in_specs=placed,
        out_specs=P(("grp", "ctx", "hd"), None),
        check_vma=False,
    )
```

```python
import jax
import jax.numpy as jnp
from jax import lax
from jax.experimental import pallas as pl
from jax.experimental.pallas import tpu as pltpu
from jax.sharding import PartitionSpec as P
import functools
import math

TOP = 8
KV_BLOCK = 512


NEG_START = -1e30


def local_attention(queries, prefix_keys, prefix_values):
    token_count, heads_local, head_width = queries.shape
    key_heads = prefix_keys.shape[1]
    grouped = heads_local // key_heads
    query_view = queries.reshape(token_count, key_heads, grouped, head_width)
    block_count = prefix_keys.shape[0] // KV_BLOCK
    key_blocks = prefix_keys.reshape(block_count, KV_BLOCK, key_heads, head_width)
    value_blocks = prefix_values.reshape(block_count, KV_BLOCK, key_heads, head_width)
    scaling = head_width ** (-0.5)

    def advance(running, pieces):
        peak_scores, totals, accumulated = running
        key_piece, value_piece = pieces
        scores = (
            jnp.einsum("sgjd,kgd->sgjk", query_view, key_piece, preferred_element_type=jnp.float32)
            * scaling
        )
        block_peak = jnp.max(scores, axis=-1)
        weights = jnp.exp(scores - block_peak[..., None]).astype(jnp.bfloat16)
        block_total = jnp.sum(weights.astype(jnp.float32), axis=-1)
        block_out = jnp.einsum(
            "sgjk,kgd->sgjd", weights, value_piece, preferred_element_type=jnp.float32
        )
        raised = jnp.maximum(peak_scores, block_peak)
        old_factor = jnp.exp(peak_scores - raised)
        new_factor = jnp.exp(block_peak - raised)
        totals = totals * old_factor + block_total * new_factor
        accumulated = accumulated * old_factor[..., None] + block_out * new_factor[..., None]
        return ((raised, totals, accumulated), None)

    start_state = (
        jnp.full((token_count, key_heads, grouped), NEG_START, jnp.float32),
        jnp.zeros((token_count, key_heads, grouped), jnp.float32),
        jnp.zeros((token_count, key_heads, grouped, head_width), jnp.float32),
    )
    final_state, leftover = lax.scan(advance, start_state, (key_blocks, value_blocks))
    peak_scores = final_state[0].reshape(token_count, heads_local)
    totals = final_state[1].reshape(token_count, heads_local)
    accumulated = final_state[2].reshape(token_count, heads_local, head_width)
    return (peak_scores, totals, accumulated)


def on_device_general(
    queries,
    prefix_keys,
    prefix_values,
    out_weight,
    residual_in,
    expert_ids,
    gate_weights,
    w_gate,
    w_up,
    w_down,
):
    every_query = lax.all_gather(queries, "ctx", axis=0, tiled=True)
    peak_scores, totals, accumulated = local_attention(every_query, prefix_keys, prefix_values)
    token_count, heads_local, head_width = accumulated.shape
    top_peak = lax.pmax(peak_scores, "ctx")
    factor = jnp.exp(peak_scores - top_peak)
    scaled_totals = totals * factor
    scaled_accum = (accumulated * factor[..., None]).reshape(token_count, heads_local * head_width)
    model_width = out_weight.shape[1]
    column_accum = lax.psum_scatter(
        scaled_accum.astype(jnp.bfloat16), "ctx", scatter_dimension=1, tiled=True
    ).astype(jnp.float32)
    all_totals = lax.psum(scaled_totals, "ctx")
    width_here = column_accum.shape[1]
    column_ids = lax.axis_index("ctx") * width_here + jnp.arange(width_here, dtype=jnp.int32)
    selector = (
        (column_ids // head_width)[None, :] == jnp.arange(heads_local, dtype=jnp.int32)[:, None]
    ).astype(jnp.float32)
    denominators = jnp.dot(all_totals, selector, precision=lax.Precision.HIGHEST)
    attended = (column_accum / denominators).astype(jnp.bfloat16)
    projected = lax.psum_scatter(
        jnp.dot(attended, out_weight, preferred_element_type=jnp.float32),
        ("ctx", "hd"),
        scatter_dimension=0,
        tiled=True,
    )
    stream = residual_in.astype(jnp.float32) + projected
    normed = (stream * lax.rsqrt(jnp.mean(stream * stream, axis=-1, keepdims=True) + 1e-06)).astype(
        jnp.bfloat16
    )
    context_count = lax.axis_size("ctx")
    head_groups = lax.axis_size("hd")
    expert_count = context_count * head_groups
    rows_here = normed.shape[0]
    slot_total = rows_here * TOP
    capacity = 2 * max(1, slot_total // expert_count)
    flat_ids = expert_ids.reshape(slot_total)
    onehot = (flat_ids[:, None] == jnp.arange(expert_count, dtype=jnp.int32)[None, :]).astype(
        jnp.int32
    )
    before = jnp.tril(jnp.ones((slot_total, slot_total), jnp.float32), -1)
    earlier = jnp.dot(
        before, onehot.astype(jnp.float32), precision=lax.Precision.HIGHEST
    ).astype(jnp.int32)
    position = jnp.sum(onehot * earlier, axis=1)
    target_row = flat_ids * capacity + position
    dispatch = (
        jnp.arange(expert_count * capacity, dtype=jnp.int32)[:, None] == target_row[None, :]
    ).astype(jnp.bfloat16)
    repeated = jnp.repeat(normed, TOP, axis=0)
    buffer = jnp.dot(dispatch, repeated, preferred_element_type=jnp.float32).astype(jnp.bfloat16)
    buffer = buffer.reshape(expert_count, capacity, model_width)
    slot_block = lax.all_to_all(buffer, ("ctx", "hd"), split_axis=0, concat_axis=0, tiled=True)
    sources, slot_count, feature_width = slot_block.shape
    flattened = slot_block.reshape(sources * slot_count, feature_width)
    gate_values = jnp.dot(flattened, w_gate[0], preferred_element_type=jnp.float32)
    up_values = jnp.dot(flattened, w_up[0], preferred_element_type=jnp.float32)
    hidden = (jax.nn.silu(gate_values) * up_values).astype(jnp.bfloat16)
    result = jnp.dot(hidden, w_down[0], preferred_element_type=jnp.float32).astype(jnp.bfloat16)
    returned_rows = lax.all_to_all(
        result.reshape(sources, slot_count, feature_width),
        ("ctx", "hd"),
        split_axis=0,
        concat_axis=0,
        tiled=True,
    )
    gathered = jnp.dot(
        dispatch.T,
        returned_rows.reshape(expert_count * capacity, model_width),
        preferred_element_type=jnp.float32,
    )
    weighted = gathered.reshape(rows_here, TOP, model_width) * gate_weights[:, :, None]
    mixture = jnp.sum(weighted, axis=1)
    return (stream + mixture).astype(jnp.bfloat16)


MESH = pl.DeviceIdType.MESH


def layer_kernel(
    ctxs,
    cores,
    q_ref,
    k_ref,
    v_ref,
    ow_ref,
    res_ref,
    ids_ref,
    gw_ref,
    wg_ref,
    wu_ref,
    wd_ref,
    out_ref,
    q_v,
    res_v,
    ids_v,
    gw_v,
    kraw,
    vraw,
    tmp,
    kd,
    vd,
    qbuf,
    qf,
    qh,
    w2,
    wgu,
    wd,
    numbuf,
    stbuf,
    numrecv,
    strecv,
    wst,
    wt,
    att,
    pjbuf,
    pjrecv,
    xbuf,
    xg,
    xs,
    gx,
    mine,
    give,
    take,
    ybuf,
    yrecv,
    load_sem,
    q_send,
    q_recv,
    ow_send,
    ow_recv,
    num_send,
    num_recv,
    st_send,
    st_recv,
    pj_send,
    pj_recv,
    x_send,
    x_recv,
    give_send,
    take_recv,
    y_send,
    y_recv,
):
    mc = lax.axis_index("ctx")
    mh = lax.axis_index("hd")
    devices = ctxs * cores
    me = mc * cores + mh
    rows, width = res_ref.shape
    ffn = wd_ref.shape[0]
    own, groups, share_heads, head = q_ref.shape
    turns, targets_in_turn, pair_rows, _ = numbuf.shape
    tokens = own * ctxs
    half = tokens // cores
    pair_count = pair_rows // half
    rate = head ** (-0.5) * math.log2(math.e)

    def remote(src, dst, ssem, rsem, c, h):
        return pltpu.make_async_remote_copy(
            src_ref=src,
            dst_ref=dst,
            send_sem=ssem,
            recv_sem=rsem,
            device_id={"ctx": c, "hd": h},
            device_id_type=MESH,
        )

    def peer(step):
        c, bit = mc, 1
        while bit < ctxs:
            if step & bit:
                c = c + (1 - 2 * lax.rem(mc // bit, 2)) * bit
            bit *= 2
        return c

    ctx_peer = [peer(step) for step in range(ctxs)]
    core_peer = [mh, cores - 1 - mh]
    steps = [(kc, kh) for kc in reversed(range(ctxs)) for kh in (1, 0)]

    def push(src, dst, ssem, rsem, c, h):
        other = c * cores + h

        @pl.when(other != me)
        def _():
            remote(src, dst, ssem, rsem, c, h).start()

        @pl.when(other == me)
        def _():
            pltpu.make_async_copy(src, dst, rsem).start()

    def sent(src, ssem):
        pltpu.make_async_copy(src, src, ssem).wait()

    def landed(dst, rsem):
        pltpu.make_async_copy(dst, dst, rsem).wait()

    drains = []
    loads = [
        pltpu.make_async_copy(a, b, load_sem.at[i])
        for i, (a, b) in enumerate(
            (
                (k_ref, kraw),
                (v_ref, vraw),
                (ow_ref, w2.at[mh]),
                (wg_ref, wgu.at[:, 0:ffn]),
                (wu_ref, wgu.at[:, ffn : 2 * ffn]),
                (wd_ref, wd),
                (res_ref, res_v),
                (ids_ref, ids_v),
                (gw_ref, gw_v),
                (q_ref, q_v),
            )
        )
    ]
    barrier = pltpu.get_barrier_semaphore()
    for kc, kh in steps[:-1]:
        pl.semaphore_signal(
            barrier,
            inc=1,
            device_id={"ctx": ctx_peer[kc], "hd": core_peer[kh]},
            device_id_type=MESH,
        )
    for one in (loads[9], *loads[:2], *loads[6:9]):
        one.start()

    loads[9].wait()
    pl.semaphore_wait(barrier, devices - 1)
    for kc in range(1, ctxs):
        remote(
            q_v, qbuf.at[mc], q_send.at[kc], q_recv.at[mc], ctx_peer[kc], mh
        ).start()
    pltpu.make_async_copy(q_v, qbuf.at[mc], q_recv.at[mc]).start()
    ow_copy = remote(ow_ref, w2.at[mh], ow_send, ow_recv, mc, cores - 1 - mh)
    ow_copy.start()
    for one in loads[2:6]:
        one.start()

    def drain_q():
        for kc in range(1, ctxs):
            sent(q_v, q_send.at[kc])

    drains.append(drain_q)
    piece = tmp.shape[0]
    share = piece // groups

    def split(raw, store):
        @pl.loop(0, raw.shape[0] // piece)
        def _(i):
            tmp[...] = raw[pl.ds(pl.multiple_of(i * piece, piece), piece), :].astype(jnp.float32)
            for g in range(groups):
                store(g, i, tmp[pl.ds(g, share, stride=groups), :].astype(jnp.bfloat16))

    def store_k(g, i, value):
        kd[g, pl.ds(pl.multiple_of(i * share, share), share), :] = value

    def store_v(g, i, value):
        at = pl.ds(pl.multiple_of(i * share, share), share)
        vd[g, at, 0:head] = value
        vd[g, at, head : 2 * head] = jnp.ones_like(value)

    loads[0].wait()
    split(kraw, store_k)
    loads[1].wait()
    split(vraw, store_v)
    wst[...] = jnp.zeros_like(wst)
    for one in loads[6:9]:
        one.wait()
    lane = lax.broadcasted_iota(jnp.int32, (rows, head), 1)
    offset = lane - lax.broadcasted_iota(jnp.int32, (rows, head), 0)
    spread = jnp.zeros((rows, head), jnp.float32)
    for e in range(devices):
        gate = jnp.sum(jnp.where(ids_v[...] == e, gw_v[...], 0.0), axis=1, keepdims=True)
        spread = spread + jnp.where(offset == e * rows, gate, 0.0)
    gates = jnp.sum(spread, axis=0, keepdims=True)

    sources = ctxs // cores
    here, there = mc // sources, mc // targets_in_turn
    lanes = lax.broadcasted_iota(jnp.int32, (2 * pair_rows, head), 1)
    for far in (0, 1):
        part = here if far == 0 else 1 - here
        per = own * share_heads
        for i in range(sources):
            c = part * sources + i
            landed(qbuf.at[c], q_recv.at[c])
            for g in range(groups):
                qf[g, i * per : (i + 1) * per, :] = (
                    qbuf[c, :, g].astype(jnp.float32).reshape(per, head)
                )
        for g in range(groups):
            for h in range(share_heads):
                qh[g, h * half : (h + 1) * half, :] = qf[
                    g, pl.ds(h, half, stride=share_heads), :
                ].astype(jnp.bfloat16)
        for near in (0, 1):
            turn = 2 * far + near
            g = there if near else 1 - there
            s = lax.dot_general(
                qh[g], kd[g], (((1,), (1,)), ((), ())), preferred_element_type=jnp.float32
            )
            m = jnp.max(s, axis=1, keepdims=True)
            p = jnp.exp2((s - m) * rate).astype(jnp.bfloat16)
            o = jnp.dot(p, vd[g], preferred_element_type=jnp.float32)
            for i in range(targets_in_turn):
                at = i * pair_rows
                numbuf[turn, i] = o[at : at + pair_rows, 0:head].astype(jnp.bfloat16)
                if i % 2 == 0:
                    both = slice(at, at + 2 * pair_rows)
                    stat = jnp.where(lanes == 0, m[both], o[both, head : 2 * head])
                    stbuf[turn, i // 2, 0:2] = stat.T[0:2]
                    stbuf[turn, i // 2, 2:3] = gates
            for i in range(targets_in_turn):
                c = g * targets_in_turn + i
                for src, dst, ssem, rsem in (
                    (stbuf.at[turn, i // 2], strecv, st_send, st_recv),
                    (numbuf.at[turn, i], numrecv, num_send, num_recv),
                ):
                    args = (src, dst.at[mc, mh], ssem.at[turn, i], rsem.at[mc, mh], c, part)
                    if near:
                        push(*args)
                    else:
                        remote(*args).start()

    def drain_num():
        for turn in range(turns):
            part = here if turn < 2 else 1 - here
            for i in range(targets_in_turn):

                def both(turn=turn, i=i):
                    sent(stbuf.at[turn, 0], st_send.at[turn, i])
                    sent(numbuf.at[turn, i], num_send.at[turn, i])

                if turn % 2 == 0:
                    both()
                else:
                    pl.when((there * targets_in_turn + i) * cores + part != me)(both)

    drains.append(drain_num)
    for h in range(cores):
        peaks, totals = [], []
        for c in range(ctxs):
            landed(strecv.at[c, h], st_recv.at[c, h])
            peaks.append(strecv[c, h, 0:1, :])
            totals.append(strecv[c, h, 1:2, :])
        peaks = jnp.concatenate(peaks, axis=0)
        totals = jnp.concatenate(totals, axis=0)
        factor = jnp.exp2((peaks - jnp.max(peaks, axis=0, keepdims=True)) * rate)
        wst[h * ctxs : (h + 1) * ctxs, :] = factor / jnp.sum(
            totals * factor, axis=0, keepdims=True
        )
    wt[...] = wst[...].T
    for h in range(cores):
        for c in range(ctxs):
            landed(numrecv.at[c, h], num_recv.at[c, h])
        for a in range(pair_count):
            at = lax.rem(mc, 2) * pair_rows + a * half
            shares = wt[pl.ds(pl.multiple_of(at, half), half), :]
            total = jnp.zeros((half, head), jnp.float32)
            for c in range(ctxs):
                at = h * ctxs + c
                total = total + numrecv[c, h, a * half : (a + 1) * half].astype(jnp.float32) * shares[:, at : at + 1]
            at = (h * pair_count + a) * head
            att[:, at : at + head] = total.astype(jnp.bfloat16)

    partner = core_peer[1]
    for h, core in enumerate((partner, mh)):
        for c in range(ctxs):
            at = (h * ctxs + c) * rows
            gx[at : at + rows, :] = jnp.broadcast_to(strecv[c, core, 2:3, :], (rows, head))
    row = lax.broadcasted_iota(jnp.int32, gx.shape, 0)
    lane = lax.broadcasted_iota(jnp.int32, gx.shape, 1)
    gate = jnp.sum(
        jnp.where(lane == me * rows + lax.rem(row, rows), gx[...], 0.0), axis=1, keepdims=True
    )

    loads[2].wait()
    ow_copy.wait()
    projected = jnp.dot(
        att[...], w2[...].reshape(att.shape[1], width), preferred_element_type=jnp.float32
    )
    targets = half // rows
    for j in range(targets):
        pjbuf[j] = projected[j * rows : (j + 1) * rows].astype(jnp.bfloat16)

    chips = targets // cores
    low = lax.rem(mc, chips)
    for kc in reversed(range(chips)):
        for kh in (1, 0):
            c = mh * chips + ctx_peer[kc] - (mc - low)
            h = core_peer[kh]
            j = (c - mh * chips) * cores + h
            go = remote if kc or kh else push
            k = kc * cores + kh
            copy = go(pjbuf.at[j], pjrecv.at[mc], pj_send.at[k], pj_recv.at[mc], c, h)
            if kc or kh:
                copy.start()

    def drain_pj():
        for k in range(1, targets):
            sent(pjbuf.at[0], pj_send.at[k])

        @pl.when(mh * chips != mc - low)
        def _():
            sent(pjbuf.at[0], pj_send.at[0])

    drains.append(drain_pj)
    stream = res_v[...].astype(jnp.float32)
    for kc in range(ctxs):
        c = ctx_peer[kc]
        landed(pjrecv.at[c], pj_recv.at[c])
        stream = stream + pjrecv[c].astype(jnp.float32)
    square = jnp.mean(stream * stream, axis=-1, keepdims=True)
    xbuf[...] = (stream * lax.rsqrt(square + 1e-06)).astype(jnp.bfloat16)

    for kc in reversed(range(1, ctxs)):
        remote(
            xbuf, xg.at[me], x_send.at[kc * cores], x_recv.at[me], ctx_peer[kc], mh
        ).start()
    remote(xbuf, xg.at[me], x_send.at[1], x_recv.at[me], mc, partner).start()
    pltpu.make_async_copy(xbuf, xg.at[me], x_recv.at[me]).start()
    for kc in range(1, ctxs):
        came = ctx_peer[kc] * cores + mh
        landed(xg.at[came], x_recv.at[came])
        remote(
            xg.at[came],
            xg.at[came],
            x_send.at[kc * cores + 1],
            x_recv.at[came],
            mc,
            partner,
        ).start()

    def drain_x():
        for k in range(1, devices):
            sent(xbuf, x_send.at[k])

    drains.append(drain_x)
    for one in loads[3:6]:
        one.wait()
    landed(xg.at[me], x_recv.at[me])
    for c in range(ctxs):
        came = c * cores + partner
        landed(xg.at[came], x_recv.at[came])
    for h, core in enumerate((partner, mh)):
        for c in range(ctxs):
            at = (h * ctxs + c) * rows
            xs[at : at + rows, :] = xg[c * cores + core].astype(jnp.float32)
    x = xs[...].astype(jnp.bfloat16)
    both = jnp.dot(x, wgu[...], preferred_element_type=jnp.float32)
    gate_values, up_values = both[:, 0:ffn], both[:, ffn : 2 * ffn]
    hidden = (gate_values / (1.0 + jnp.exp(-gate_values)) * up_values).astype(jnp.bfloat16)

    near_rows = mine.shape[0]
    result = gate * jnp.dot(hidden, wd[...], preferred_element_type=jnp.float32)
    give[...] = result[near_rows:].astype(jnp.bfloat16)
    remote(give, take, give_send, take_recv, mc, partner).start()
    mine[...] = result[0:near_rows]
    landed(take, take_recv)
    total = mine[...] + take[...].astype(jnp.float32)
    for c in range(ctxs):
        ybuf[c] = total[c * rows : (c + 1) * rows].astype(jnp.bfloat16)
    for kc in reversed(range(ctxs)):
        c = ctx_peer[kc]
        remote(ybuf.at[c], yrecv.at[mc], y_send.at[kc], y_recv.at[mc], c, partner).start()

    def drain_y():
        sent(give, give_send)
        for kc in range(ctxs):
            sent(ybuf.at[0], y_send.at[kc])

    drains.append(drain_y)
    for kc in range(ctxs):
        c = ctx_peer[kc]
        landed(yrecv.at[c], y_recv.at[c])
        stream = stream + yrecv[c].astype(jnp.float32)
    out_ref[...] = stream.astype(out_ref.dtype)

    for drain in drains:
        drain()


def on_device(
    queries,
    prefix_keys,
    prefix_values,
    out_weight,
    residual_in,
    expert_ids,
    gate_weights,
    w_gate,
    w_up,
    w_down,
):
    ctxs, cores = lax.axis_size("ctx"), lax.axis_size("hd")
    devices = ctxs * cores
    own, heads, head = queries.shape
    positions, groups, _ = prefix_keys.shape
    depth, width = out_weight.shape
    rows = residual_in.shape[0]
    ffn = w_gate.shape[2]
    tokens = own * ctxs
    pair_count = heads // ctxs
    fits = (
        cores == 2
        and pair_count * ctxs == heads
        and pair_count * tokens == head
        and ctxs % 8 == 0
        and ctxs & (ctxs - 1) == 0
        and groups == 2
        and cores * ctxs <= head
        and devices * rows <= head
        and own * ctxs % (cores * 16) == 0
    )
    if not fits:
        return on_device_general(
            queries,
            prefix_keys,
            prefix_values,
            out_weight,
            residual_in,
            expert_ids,
            gate_weights,
            w_gate,
            w_up,
            w_down,
        )
    half = tokens // cores
    held = [
        pltpu.with_memory_space_constraint(a, pltpu.HBM)
        for a in (
            queries.reshape(own, groups, heads // groups, head),
            prefix_keys.reshape(positions * groups, head),
            prefix_values.reshape(positions * groups, head),
            out_weight,
            residual_in,
            expert_ids,
            gate_weights,
            w_gate[0],
            w_up[0],
            w_down[0],
        )
    ]
    any_spec = pl.BlockSpec(memory_space=pl.ANY)
    vmem_spec = pl.BlockSpec(memory_space=pltpu.VMEM)
    bf, f32 = jnp.bfloat16, jnp.float32
    dma = pltpu.SemaphoreType.DMA
    return pl.pallas_call(
        functools.partial(layer_kernel, ctxs, cores),
        out_shape=jax.ShapeDtypeStruct((rows, width), bf),
        in_specs=[any_spec] * 10,
        out_specs=vmem_spec,
        scratch_shapes=[
            pltpu.VMEM((own, groups, heads // groups, head), bf),
            pltpu.VMEM(residual_in.shape, bf),
            pltpu.VMEM(expert_ids.shape, expert_ids.dtype),
            pltpu.VMEM(gate_weights.shape, f32),
            pltpu.VMEM((positions * groups, head), bf),
            pltpu.VMEM((positions * groups, head), bf),
            pltpu.VMEM((256 * groups, head), f32),
            pltpu.VMEM((groups, positions, head), bf),
            pltpu.VMEM((groups, positions, 2 * head), bf),
            pltpu.VMEM((ctxs, own, groups, heads // groups, head), bf),
            pltpu.VMEM((groups, half * heads // groups, head), f32),
            pltpu.VMEM((groups, half * heads // groups, head), bf),
            pltpu.VMEM((cores, depth, width), bf),
            pltpu.VMEM((width, 2 * ffn), bf),
            pltpu.VMEM((ffn, width), bf),
            pltpu.VMEM((cores * groups, ctxs // groups, pair_count * half, head), bf),
            pltpu.VMEM((cores * groups, ctxs // groups // 2, 3, head), f32),
            pltpu.VMEM((ctxs, cores, pair_count * half, head), bf),
            pltpu.VMEM((ctxs, cores, 3, head), f32),
            pltpu.VMEM((head, head), f32),
            pltpu.VMEM((head, head), f32),
            pltpu.VMEM((half, cores * depth), bf),
            pltpu.VMEM((half // rows, rows, width), bf),
            pltpu.VMEM((ctxs, rows, width), bf),
            pltpu.VMEM((rows, width), bf),
            pltpu.VMEM((devices, rows, width), bf),
            pltpu.VMEM((devices * rows, width), f32),
            pltpu.VMEM((devices * rows, head), f32),
            pltpu.VMEM((ctxs * rows, width), f32),
            pltpu.VMEM((ctxs * rows, width), bf),
            pltpu.VMEM((ctxs * rows, width), bf),
            pltpu.VMEM((ctxs, rows, width), bf),
            pltpu.VMEM((ctxs, rows, width), bf),
            dma((10,)),
            dma((ctxs,)),
            dma((ctxs,)),
            dma,
            dma,
            dma((cores * groups, ctxs // groups)),
            dma((ctxs, cores)),
            dma((cores * groups, ctxs // groups)),
            dma((ctxs, cores)),
            dma((half // rows,)),
            dma((ctxs,)),
            dma((devices,)),
            dma((devices,)),
            dma,
            dma,
            dma((ctxs,)),
            dma((ctxs,)),
        ],
        compiler_params=pltpu.CompilerParams(
            collective_id=0, has_side_effects=True, vmem_limit_bytes=32 * 1024 * 1024
        ),
    )(*held)


def solution(mesh):
    placed = (
        P(("grp", "ctx"), "hd", None),
        P(("grp", "ctx"), "hd", None),
        P(("grp", "ctx"), "hd", None),
        P(("hd", "ctx"), None),
        P(("grp", "ctx", "hd"), None),
        P(("grp", "ctx", "hd"), None),
        P(("grp", "ctx", "hd"), None),
        P(("ctx", "hd"), None, None),
        P(("ctx", "hd"), None, None),
        P(("ctx", "hd"), None, None),
    )
    return jax.shard_map(
        on_device,
        mesh=mesh,
        in_specs=placed,
        out_specs=P(("grp", "ctx", "hd"), None),
        check_vma=False,
    )
```

```python
import jax
import jax.numpy as jnp
from jax import lax
from jax.experimental import pallas as pl
from jax.experimental.pallas import tpu as pltpu
from jax.sharding import PartitionSpec as P
import functools
import math

TOP = 8
KV_BLOCK = 512


NEG_START = -1e30


def local_attention(queries, prefix_keys, prefix_values):
    token_count, heads_local, head_width = queries.shape
    key_heads = prefix_keys.shape[1]
    grouped = heads_local // key_heads
    query_view = queries.reshape(token_count, key_heads, grouped, head_width)
    block_count = prefix_keys.shape[0] // KV_BLOCK
    key_blocks = prefix_keys.reshape(block_count, KV_BLOCK, key_heads, head_width)
    value_blocks = prefix_values.reshape(block_count, KV_BLOCK, key_heads, head_width)
    scaling = head_width ** (-0.5)

    def advance(running, pieces):
        peak_scores, totals, accumulated = running
        key_piece, value_piece = pieces
        scores = (
            jnp.einsum("sgjd,kgd->sgjk", query_view, key_piece, preferred_element_type=jnp.float32)
            * scaling
        )
        block_peak = jnp.max(scores, axis=-1)
        weights = jnp.exp(scores - block_peak[..., None]).astype(jnp.bfloat16)
        block_total = jnp.sum(weights.astype(jnp.float32), axis=-1)
        block_out = jnp.einsum(
            "sgjk,kgd->sgjd", weights, value_piece, preferred_element_type=jnp.float32
        )
        raised = jnp.maximum(peak_scores, block_peak)
        old_factor = jnp.exp(peak_scores - raised)
        new_factor = jnp.exp(block_peak - raised)
        totals = totals * old_factor + block_total * new_factor
        accumulated = accumulated * old_factor[..., None] + block_out * new_factor[..., None]
        return ((raised, totals, accumulated), None)

    start_state = (
        jnp.full((token_count, key_heads, grouped), NEG_START, jnp.float32),
        jnp.zeros((token_count, key_heads, grouped), jnp.float32),
        jnp.zeros((token_count, key_heads, grouped, head_width), jnp.float32),
    )
    final_state, leftover = lax.scan(advance, start_state, (key_blocks, value_blocks))
    peak_scores = final_state[0].reshape(token_count, heads_local)
    totals = final_state[1].reshape(token_count, heads_local)
    accumulated = final_state[2].reshape(token_count, heads_local, head_width)
    return (peak_scores, totals, accumulated)


def on_device_general(
    queries,
    prefix_keys,
    prefix_values,
    out_weight,
    residual_in,
    expert_ids,
    gate_weights,
    w_gate,
    w_up,
    w_down,
):
    every_query = lax.all_gather(queries, "ctx", axis=0, tiled=True)
    peak_scores, totals, accumulated = local_attention(every_query, prefix_keys, prefix_values)
    token_count, heads_local, head_width = accumulated.shape
    top_peak = lax.pmax(peak_scores, "ctx")
    factor = jnp.exp(peak_scores - top_peak)
    scaled_totals = totals * factor
    scaled_accum = (accumulated * factor[..., None]).reshape(token_count, heads_local * head_width)
    model_width = out_weight.shape[1]
    column_accum = lax.psum_scatter(
        scaled_accum.astype(jnp.bfloat16), "ctx", scatter_dimension=1, tiled=True
    ).astype(jnp.float32)
    all_totals = lax.psum(scaled_totals, "ctx")
    width_here = column_accum.shape[1]
    column_ids = lax.axis_index("ctx") * width_here + jnp.arange(width_here, dtype=jnp.int32)
    selector = (
        (column_ids // head_width)[None, :] == jnp.arange(heads_local, dtype=jnp.int32)[:, None]
    ).astype(jnp.float32)
    denominators = jnp.dot(all_totals, selector, precision=lax.Precision.HIGHEST)
    attended = (column_accum / denominators).astype(jnp.bfloat16)
    projected = lax.psum_scatter(
        jnp.dot(attended, out_weight, preferred_element_type=jnp.float32),
        ("ctx", "hd"),
        scatter_dimension=0,
        tiled=True,
    )
    stream = residual_in.astype(jnp.float32) + projected
    normed = (stream * lax.rsqrt(jnp.mean(stream * stream, axis=-1, keepdims=True) + 1e-06)).astype(
        jnp.bfloat16
    )
    context_count = lax.axis_size("ctx")
    head_groups = lax.axis_size("hd")
    expert_count = context_count * head_groups
    rows_here = normed.shape[0]
    slot_total = rows_here * TOP
    capacity = 2 * max(1, slot_total // expert_count)
    flat_ids = expert_ids.reshape(slot_total)
    onehot = (flat_ids[:, None] == jnp.arange(expert_count, dtype=jnp.int32)[None, :]).astype(
        jnp.int32
    )
    before = jnp.tril(jnp.ones((slot_total, slot_total), jnp.float32), -1)
    earlier = jnp.dot(
        before, onehot.astype(jnp.float32), precision=lax.Precision.HIGHEST
    ).astype(jnp.int32)
    position = jnp.sum(onehot * earlier, axis=1)
    target_row = flat_ids * capacity + position
    dispatch = (
        jnp.arange(expert_count * capacity, dtype=jnp.int32)[:, None] == target_row[None, :]
    ).astype(jnp.bfloat16)
    repeated = jnp.repeat(normed, TOP, axis=0)
    buffer = jnp.dot(dispatch, repeated, preferred_element_type=jnp.float32).astype(jnp.bfloat16)
    buffer = buffer.reshape(expert_count, capacity, model_width)
    slot_block = lax.all_to_all(buffer, ("ctx", "hd"), split_axis=0, concat_axis=0, tiled=True)
    sources, slot_count, feature_width = slot_block.shape
    flattened = slot_block.reshape(sources * slot_count, feature_width)
    gate_values = jnp.dot(flattened, w_gate[0], preferred_element_type=jnp.float32)
    up_values = jnp.dot(flattened, w_up[0], preferred_element_type=jnp.float32)
    hidden = (jax.nn.silu(gate_values) * up_values).astype(jnp.bfloat16)
    result = jnp.dot(hidden, w_down[0], preferred_element_type=jnp.float32).astype(jnp.bfloat16)
    returned_rows = lax.all_to_all(
        result.reshape(sources, slot_count, feature_width),
        ("ctx", "hd"),
        split_axis=0,
        concat_axis=0,
        tiled=True,
    )
    gathered = jnp.dot(
        dispatch.T,
        returned_rows.reshape(expert_count * capacity, model_width),
        preferred_element_type=jnp.float32,
    )
    weighted = gathered.reshape(rows_here, TOP, model_width) * gate_weights[:, :, None]
    mixture = jnp.sum(weighted, axis=1)
    return (stream + mixture).astype(jnp.bfloat16)


MESH = pl.DeviceIdType.MESH


def layer_kernel(
    ctxs,
    cores,
    q_ref,
    k_ref,
    v_ref,
    ow_ref,
    res_ref,
    ids_ref,
    gw_ref,
    wg_ref,
    wu_ref,
    wd_ref,
    out_ref,
    q_v,
    res_v,
    ids_v,
    gw_v,
    kraw,
    vraw,
    tmp,
    kd,
    vd,
    qbuf,
    qf,
    qs,
    w2,
    wgu,
    wd,
    numbuf,
    stbuf,
    numrecv,
    strecv,
    wst,
    wt,
    att,
    pjbuf,
    pjrecv,
    xbuf,
    xg,
    xs,
    gx,
    mine,
    give,
    take,
    lead,
    lead_out,
    lead_in,
    lead_sum,
    ybuf,
    yrecv,
    load_sem,
    q_send,
    q_recv,
    ow_send,
    ow_recv,
    num_send,
    num_recv,
    st_send,
    st_recv,
    pj_send,
    pj_recv,
    x_send,
    x_recv,
    give_send,
    take_recv,
    lead_send,
    lead_recv,
    lead_left,
    y_send,
    y_recv,
):
    mc = lax.axis_index("ctx")
    mh = lax.axis_index("hd")
    devices = ctxs * cores
    me = mc * cores + mh
    rows, width = res_ref.shape
    ffn = wd_ref.shape[0]
    own, groups, share_heads, head = q_ref.shape
    turns, targets_in_turn, pair_rows, _ = numbuf.shape
    tokens = own * ctxs
    half = tokens // cores
    pair_count = pair_rows // half
    rate = head ** (-0.5) * math.log2(math.e)

    def remote(src, dst, ssem, rsem, c, h):
        return pltpu.make_async_remote_copy(
            src_ref=src,
            dst_ref=dst,
            send_sem=ssem,
            recv_sem=rsem,
            device_id={"ctx": c, "hd": h},
            device_id_type=MESH,
        )

    def peer(step):
        c, bit = mc, 1
        while bit < ctxs:
            if step & bit:
                c = c + (1 - 2 * lax.rem(mc // bit, 2)) * bit
            bit *= 2
        return c

    ctx_peer = [peer(step) for step in range(ctxs)]
    core_peer = [mh, cores - 1 - mh]
    steps = [(kc, kh) for kc in reversed(range(ctxs)) for kh in (1, 0)]

    def push(src, dst, ssem, rsem, c, h):
        other = c * cores + h

        @pl.when(other != me)
        def _():
            remote(src, dst, ssem, rsem, c, h).start()

        @pl.when(other == me)
        def _():
            pltpu.make_async_copy(src, dst, rsem).start()

    def sent(src, ssem):
        pltpu.make_async_copy(src, src, ssem).wait()

    def landed(dst, rsem):
        pltpu.make_async_copy(dst, dst, rsem).wait()

    drains = []
    loads = [
        pltpu.make_async_copy(a, b, load_sem.at[i])
        for i, (a, b) in enumerate(
            (
                (k_ref, kraw),
                (v_ref, vraw),
                (ow_ref, w2.at[mh]),
                (wg_ref, wgu.at[:, 0:ffn]),
                (wu_ref, wgu.at[:, ffn : 2 * ffn]),
                (wd_ref, wd),
                (res_ref, res_v),
                (ids_ref, ids_v),
                (gw_ref, gw_v),
                (q_ref, q_v),
            )
        )
    ]
    barrier = pltpu.get_barrier_semaphore()
    for kc, kh in steps[:-1]:
        pl.semaphore_signal(
            barrier,
            inc=1,
            device_id={"ctx": ctx_peer[kc], "hd": core_peer[kh]},
            device_id_type=MESH,
        )
    for one in (loads[9], *loads[:2], *loads[6:9]):
        one.start()

    loads[9].wait()
    for g in range(groups):
        qf[g] = q_v[:, g].astype(jnp.float32).reshape(own * share_heads, head)
        for h in range(share_heads):
            qs[g, h * own : (h + 1) * own, :] = qf[
                g, pl.ds(h, own, stride=share_heads), :
            ].astype(jnp.bfloat16)
    pl.semaphore_wait(barrier, devices - 1)
    for kc in range(1, ctxs):
        remote(
            qs, qbuf.at[mc], q_send.at[kc], q_recv.at[mc], ctx_peer[kc], mh
        ).start()
    pltpu.make_async_copy(qs, qbuf.at[mc], q_recv.at[mc]).start()
    ow_copy = remote(ow_ref, w2.at[mh], ow_send, ow_recv, mc, cores - 1 - mh)
    ow_copy.start()
    for one in loads[2:6]:
        one.start()

    def drain_q():
        for kc in range(1, ctxs):
            sent(qs, q_send.at[kc])

    drains.append(drain_q)
    piece = tmp.shape[0]
    share = piece // groups

    def split(raw, store):
        @pl.loop(0, raw.shape[0] // piece)
        def _(i):
            tmp[...] = raw[pl.ds(pl.multiple_of(i * piece, piece), piece), :].astype(jnp.float32)
            for g in range(groups):
                store(g, i, tmp[pl.ds(g, share, stride=groups), :].astype(jnp.bfloat16))

    def store_k(g, i, value):
        kd[g, pl.ds(pl.multiple_of(i * share, share), share), :] = value

    def store_v(g, i, value):
        at = pl.ds(pl.multiple_of(i * share, share), share)
        vd[g, at, 0:head] = value
        vd[g, at, head : 2 * head] = jnp.ones_like(value)

    loads[0].wait()
    split(kraw, store_k)
    loads[1].wait()
    split(vraw, store_v)
    wst[...] = jnp.zeros_like(wst)
    for one in loads[6:9]:
        one.wait()
    lane = lax.broadcasted_iota(jnp.int32, (rows, head), 1)
    offset = lane - lax.broadcasted_iota(jnp.int32, (rows, head), 0)
    spread = jnp.zeros((rows, head), jnp.float32)
    for e in range(devices):
        gate = jnp.sum(jnp.where(ids_v[...] == e, gw_v[...], 0.0), axis=1, keepdims=True)
        spread = spread + jnp.where(offset == e * rows, gate, 0.0)
    gates = jnp.sum(spread, axis=0, keepdims=True)

    sources = ctxs // cores
    here, there = mc // sources, mc // targets_in_turn
    lanes = lax.broadcasted_iota(jnp.int32, (sources * own * share_heads, head), 1)
    for far in (0, 1):
        part = here if far == 0 else 1 - here
        for i in range(sources):
            c = part * sources + i
            landed(qbuf.at[c], q_recv.at[c])

        def rows_of(value, i):
            starts = [
                (n * share_heads + i * pair_count + a) * own
                for a in range(pair_count)
                for n in range(sources)
            ]
            return jnp.concatenate([value[at : at + own] for at in starts], axis=0)

        for near in (0, 1):
            turn = 2 * far + near
            g = there if near else 1 - there
            core = 1 if near == far else 0
            s = lax.dot_general(
                jnp.concatenate([qbuf[part * sources + i, g] for i in range(sources)], axis=0),
                kd[g],
                (((1,), (1,)), ((), ())), preferred_element_type=jnp.float32
            )
            m = jnp.max(s, axis=1, keepdims=True)
            p = jnp.exp2((s - m) * rate).astype(jnp.bfloat16)
            o = jnp.dot(p, vd[g], preferred_element_type=jnp.float32)
            stat = jnp.where(lanes == 0, m, o[:, head : 2 * head])
            for i in range(targets_in_turn):
                numbuf[turn, i] = rows_of(o[:, 0:head], i).astype(jnp.bfloat16)
                if i % 2 == 0:
                    both = jnp.concatenate([rows_of(stat, i), rows_of(stat, i + 1)], axis=0)
                    stbuf[turn, i // 2, 0:2] = both.T[0:2]
                    stbuf[turn, i // 2, 2:3] = gates
            for i in range(targets_in_turn):
                c = g * targets_in_turn + i
                for src, dst, ssem, rsem in (
                    (stbuf.at[turn, i // 2], strecv, st_send, st_recv),
                    (numbuf.at[turn, i], numrecv, num_send, num_recv),
                ):
                    args = (src, dst.at[mc, mh], ssem.at[turn, i], rsem.at[mc, mh], c, core)
                    if near:
                        push(*args)
                    else:
                        remote(*args).start()

    def drain_num():
        for turn in range(turns):
            core = turn // 2
            for i in range(targets_in_turn):

                def both(turn=turn, i=i):
                    sent(stbuf.at[turn, 0], st_send.at[turn, i])
                    sent(numbuf.at[turn, i], num_send.at[turn, i])

                if turn % 2 == 0:
                    both()
                else:
                    pl.when((there * targets_in_turn + i) * cores + core != me)(both)

    drains.append(drain_num)
    for h in range(cores):
        peaks, totals = [], []
        for c in range(ctxs):
            landed(strecv.at[c, h], st_recv.at[c, h])
            peaks.append(strecv[c, h, 0:1, :])
            totals.append(strecv[c, h, 1:2, :])
        peaks = jnp.concatenate(peaks, axis=0)
        totals = jnp.concatenate(totals, axis=0)
        factor = jnp.exp2((peaks - jnp.max(peaks, axis=0, keepdims=True)) * rate)
        wst[h * ctxs : (h + 1) * ctxs, :] = factor / jnp.sum(
            totals * factor, axis=0, keepdims=True
        )
    wt[...] = wst[...].T
    for h in reversed(range(cores)):
        for c in range(ctxs):
            landed(numrecv.at[c, h], num_recv.at[c, h])
        for a in range(pair_count):
            at = lax.rem(mc, 2) * pair_rows + a * half
            shares = wt[pl.ds(pl.multiple_of(at, half), half), :]
            total = jnp.zeros((half, head), jnp.float32)
            for c in range(ctxs):
                at = h * ctxs + c
                total = total + numrecv[c, h, a * half : (a + 1) * half].astype(jnp.float32) * shares[:, at : at + 1]
            at = (h * pair_count + a) * head
            att[:, at : at + head] = total.astype(jnp.bfloat16)

    partner = core_peer[1]
    for h, core in enumerate((partner, mh)):
        for c in range(ctxs):
            at = (h * ctxs + c) * rows
            gx[at : at + rows, :] = jnp.broadcast_to(strecv[c, core, 2:3, :], (rows, head))
    row = lax.broadcasted_iota(jnp.int32, gx.shape, 0)
    lane = lax.broadcasted_iota(jnp.int32, gx.shape, 1)
    gate = jnp.sum(
        jnp.where(lane == me * rows + lax.rem(row, rows), gx[...], 0.0), axis=1, keepdims=True
    )

    loads[2].wait()
    ow_copy.wait()
    projected = jnp.dot(
        att[...], w2[...].reshape(att.shape[1], width), preferred_element_type=jnp.float32
    )
    targets = half // rows
    for j in range(targets):
        pjbuf[j] = projected[j * rows : (j + 1) * rows].astype(jnp.bfloat16)

    chips = targets // cores
    low = lax.rem(mc, chips)
    away = mh
    base = (here + away - 2 * here * away) * chips
    for kc in reversed(range(chips)):
        for kh in (1, 0):
            c = base + ctx_peer[kc] - (mc - low)
            h = core_peer[kh]
            j = (c - base) * cores + h
            go = remote if kc or kh else push
            k = kc * cores + kh
            copy = go(pjbuf.at[j], pjrecv.at[mc], pj_send.at[k], pj_recv.at[mc], c, h)
            if kc or kh:
                copy.start()

    def drain_pj():
        for k in range(1, targets):
            sent(pjbuf.at[0], pj_send.at[k])

        @pl.when(base != mc - low)
        def _():
            sent(pjbuf.at[0], pj_send.at[0])

    drains.append(drain_pj)
    stream = res_v[...].astype(jnp.float32)
    for kc in range(ctxs):
        c = ctx_peer[kc]
        landed(pjrecv.at[c], pj_recv.at[c])
        stream = stream + pjrecv[c].astype(jnp.float32)
    square = jnp.mean(stream * stream, axis=-1, keepdims=True)
    xbuf[...] = (stream * lax.rsqrt(square + 1e-06)).astype(jnp.bfloat16)

    for kc in reversed(range(1, ctxs)):
        remote(
            xbuf, xg.at[me], x_send.at[kc * cores], x_recv.at[me], ctx_peer[kc], mh
        ).start()
    remote(xbuf, xg.at[me], x_send.at[1], x_recv.at[me], mc, partner).start()
    pltpu.make_async_copy(xbuf, xg.at[me], x_recv.at[me]).start()
    for kc in range(1, ctxs):
        came = ctx_peer[kc] * cores + mh
        landed(xg.at[came], x_recv.at[came])
        remote(
            xg.at[came],
            xg.at[came],
            x_send.at[kc * cores + 1],
            x_recv.at[came],
            mc,
            partner,
        ).start()

    def drain_x():
        for k in range(1, devices):
            sent(xbuf, x_send.at[k])

    drains.append(drain_x)
    for one in loads[3:6]:
        one.wait()
    landed(xg.at[me], x_recv.at[me])
    for c in range(ctxs):
        came = c * cores + partner
        landed(xg.at[came], x_recv.at[came])
    for h, core in enumerate((partner, mh)):
        for c in range(ctxs):
            at = (h * ctxs + c) * rows
            xs[at : at + rows, :] = xg[c * cores + core].astype(jnp.float32)
    x = xs[...].astype(jnp.bfloat16)
    both = jnp.dot(x, wgu[...], preferred_element_type=jnp.float32)
    gate_values, up_values = both[:, 0:ffn], both[:, ffn : 2 * ffn]
    hidden = (gate_values / (1.0 + jnp.exp(-gate_values)) * up_values).astype(jnp.bfloat16)

    near_rows = mine.shape[0]
    result = gate * jnp.dot(hidden, wd[...], preferred_element_type=jnp.float32)
    for b in range(cores):
        block = result[b * near_rows : b * near_rows + rows]
        lead[b] = block
        lead_out[b] = block.astype(jnp.bfloat16)

    @pl.when(mh == 0)
    def _():
        remote(lead_out, lead_in, lead_send, lead_recv, mc, partner).start()

    give[...] = result[near_rows:].astype(jnp.bfloat16)
    remote(give, take, give_send, take_recv, mc, partner).start()
    mine[...] = result[0:near_rows]

    @pl.when(mh == 1)
    def _():
        landed(lead_in, lead_recv)
        for b in range(cores):
            lead_sum[b] = (lead[b] + lead_in[1 - b].astype(jnp.float32)).astype(jnp.bfloat16)
        for b in range(cores):
            push(lead_sum.at[b], yrecv.at[mc], lead_left.at[b], y_recv.at[mc], 0, b)

    landed(take, take_recv)
    total = mine[...] + take[...].astype(jnp.float32)
    for c in range(1, ctxs):
        ybuf[c] = total[c * rows : (c + 1) * rows].astype(jnp.bfloat16)
    for c in range(1, ctxs):
        remote(ybuf.at[c], yrecv.at[mc], y_send.at[c], y_recv.at[mc], c, partner).start()

    def drain_y():
        sent(give, give_send)
        for c in range(1, ctxs):
            sent(ybuf.at[0], y_send.at[c])

        @pl.when(mh == 0)
        def _():
            sent(lead_out, lead_send)

        @pl.when(mh == 1)
        def _():
            for b in range(cores):
                pl.when(me != b)(lambda b=b: sent(lead_sum.at[b], lead_left.at[b]))

    drains.append(drain_y)
    for kc in range(ctxs):
        c = ctx_peer[kc]
        landed(yrecv.at[c], y_recv.at[c])
        stream = stream + yrecv[c].astype(jnp.float32)
    out_ref[...] = stream.astype(out_ref.dtype)

    for drain in drains:
        drain()


def on_device(
    queries,
    prefix_keys,
    prefix_values,
    out_weight,
    residual_in,
    expert_ids,
    gate_weights,
    w_gate,
    w_up,
    w_down,
):
    ctxs, cores = lax.axis_size("ctx"), lax.axis_size("hd")
    devices = ctxs * cores
    own, heads, head = queries.shape
    positions, groups, _ = prefix_keys.shape
    depth, width = out_weight.shape
    rows = residual_in.shape[0]
    ffn = w_gate.shape[2]
    tokens = own * ctxs
    pair_count = heads // ctxs
    fits = (
        cores == 2
        and pair_count * ctxs == heads
        and pair_count * tokens == head
        and ctxs % 8 == 0
        and ctxs & (ctxs - 1) == 0
        and groups == 2
        and cores * ctxs <= head
        and devices * rows <= head
        and own * ctxs % (cores * 16) == 0
    )
    if not fits:
        return on_device_general(
            queries,
            prefix_keys,
            prefix_values,
            out_weight,
            residual_in,
            expert_ids,
            gate_weights,
            w_gate,
            w_up,
            w_down,
        )
    half = tokens // cores
    held = [
        pltpu.with_memory_space_constraint(a, pltpu.HBM)
        for a in (
            queries.reshape(own, groups, heads // groups, head),
            prefix_keys.reshape(positions * groups, head),
            prefix_values.reshape(positions * groups, head),
            out_weight,
            residual_in,
            expert_ids,
            gate_weights,
            w_gate[0],
            w_up[0],
            w_down[0],
        )
    ]
    any_spec = pl.BlockSpec(memory_space=pl.ANY)
    vmem_spec = pl.BlockSpec(memory_space=pltpu.VMEM)
    bf, f32 = jnp.bfloat16, jnp.float32
    dma = pltpu.SemaphoreType.DMA
    return pl.pallas_call(
        functools.partial(layer_kernel, ctxs, cores),
        out_shape=jax.ShapeDtypeStruct((rows, width), bf),
        in_specs=[any_spec] * 10,
        out_specs=vmem_spec,
        scratch_shapes=[
            pltpu.VMEM((own, groups, heads // groups, head), bf),
            pltpu.VMEM(residual_in.shape, bf),
            pltpu.VMEM(expert_ids.shape, expert_ids.dtype),
            pltpu.VMEM(gate_weights.shape, f32),
            pltpu.VMEM((positions * groups, head), bf),
            pltpu.VMEM((positions * groups, head), bf),
            pltpu.VMEM((256 * groups, head), f32),
            pltpu.VMEM((groups, positions, head), bf),
            pltpu.VMEM((groups, positions, 2 * head), bf),
            pltpu.VMEM((ctxs, groups, own * heads // groups, head), bf),
            pltpu.VMEM((groups, own * heads // groups, head), f32),
            pltpu.VMEM((groups, own * heads // groups, head), bf),
            pltpu.VMEM((cores, depth, width), bf),
            pltpu.VMEM((width, 2 * ffn), bf),
            pltpu.VMEM((ffn, width), bf),
            pltpu.VMEM((cores * groups, ctxs // groups, pair_count * half, head), bf),
            pltpu.VMEM((cores * groups, ctxs // groups // 2, 3, head), f32),
            pltpu.VMEM((ctxs, cores, pair_count * half, head), bf),
            pltpu.VMEM((ctxs, cores, 3, head), f32),
            pltpu.VMEM((head, head), f32),
            pltpu.VMEM((head, head), f32),
            pltpu.VMEM((half, cores * depth), bf),
            pltpu.VMEM((half // rows, rows, width), bf),
            pltpu.VMEM((ctxs, rows, width), bf),
            pltpu.VMEM((rows, width), bf),
            pltpu.VMEM((devices, rows, width), bf),
            pltpu.VMEM((devices * rows, width), f32),
            pltpu.VMEM((devices * rows, head), f32),
            pltpu.VMEM((ctxs * rows, width), f32),
            pltpu.VMEM((ctxs * rows, width), bf),
            pltpu.VMEM((ctxs * rows, width), bf),
            pltpu.VMEM((cores, rows, width), f32),
            pltpu.VMEM((cores, rows, width), bf),
            pltpu.VMEM((cores, rows, width), bf),
            pltpu.VMEM((cores, rows, width), bf),
            pltpu.VMEM((ctxs, rows, width), bf),
            pltpu.VMEM((ctxs, rows, width), bf),
            dma((10,)),
            dma((ctxs,)),
            dma((ctxs,)),
            dma,
            dma,
            dma((cores * groups, ctxs // groups)),
            dma((ctxs, cores)),
            dma((cores * groups, ctxs // groups)),
            dma((ctxs, cores)),
            dma((half // rows,)),
            dma((ctxs,)),
            dma((devices,)),
            dma((devices,)),
            dma,
            dma,
            dma,
            dma,
            dma((cores,)),
            dma((ctxs,)),
            dma((ctxs,)),
        ],
        compiler_params=pltpu.CompilerParams(
            collective_id=0, has_side_effects=True, vmem_limit_bytes=32 * 1024 * 1024
        ),
    )(*held)


def solution(mesh):
    placed = (
        P(("grp", "ctx"), "hd", None),
        P(("grp", "ctx"), "hd", None),
        P(("grp", "ctx"), "hd", None),
        P(("hd", "ctx"), None),
        P(("grp", "ctx", "hd"), None),
        P(("grp", "ctx", "hd"), None),
        P(("grp", "ctx", "hd"), None),
        P(("ctx", "hd"), None, None),
        P(("ctx", "hd"), None, None),
        P(("ctx", "hd"), None, None),
    )
    return jax.shard_map(
        on_device,
        mesh=mesh,
        in_specs=placed,
        out_specs=P(("grp", "ctx", "hd"), None),
        check_vma=False,
    )
```

```python
import jax
import jax.numpy as jnp
from jax import lax
from jax.experimental import pallas as pl
from jax.experimental.pallas import tpu as pltpu
from jax.sharding import PartitionSpec as P
import functools
import math

TOP = 8
KV_BLOCK = 512


NEG_START = -1e30


def local_attention(queries, prefix_keys, prefix_values):
    token_count, heads_local, head_width = queries.shape
    key_heads = prefix_keys.shape[1]
    grouped = heads_local // key_heads
    query_view = queries.reshape(token_count, key_heads, grouped, head_width)
    block_count = prefix_keys.shape[0] // KV_BLOCK
    key_blocks = prefix_keys.reshape(block_count, KV_BLOCK, key_heads, head_width)
    value_blocks = prefix_values.reshape(block_count, KV_BLOCK, key_heads, head_width)
    scaling = head_width ** (-0.5)

    def advance(running, pieces):
        peak_scores, totals, accumulated = running
        key_piece, value_piece = pieces
        scores = (
            jnp.einsum("sgjd,kgd->sgjk", query_view, key_piece, preferred_element_type=jnp.float32)
            * scaling
        )
        block_peak = jnp.max(scores, axis=-1)
        weights = jnp.exp(scores - block_peak[..., None]).astype(jnp.bfloat16)
        block_total = jnp.sum(weights.astype(jnp.float32), axis=-1)
        block_out = jnp.einsum(
            "sgjk,kgd->sgjd", weights, value_piece, preferred_element_type=jnp.float32
        )
        raised = jnp.maximum(peak_scores, block_peak)
        old_factor = jnp.exp(peak_scores - raised)
        new_factor = jnp.exp(block_peak - raised)
        totals = totals * old_factor + block_total * new_factor
        accumulated = accumulated * old_factor[..., None] + block_out * new_factor[..., None]
        return ((raised, totals, accumulated), None)

    start_state = (
        jnp.full((token_count, key_heads, grouped), NEG_START, jnp.float32),
        jnp.zeros((token_count, key_heads, grouped), jnp.float32),
        jnp.zeros((token_count, key_heads, grouped, head_width), jnp.float32),
    )
    final_state, leftover = lax.scan(advance, start_state, (key_blocks, value_blocks))
    peak_scores = final_state[0].reshape(token_count, heads_local)
    totals = final_state[1].reshape(token_count, heads_local)
    accumulated = final_state[2].reshape(token_count, heads_local, head_width)
    return (peak_scores, totals, accumulated)


def on_device_general(
    queries,
    prefix_keys,
    prefix_values,
    out_weight,
    residual_in,
    expert_ids,
    gate_weights,
    w_gate,
    w_up,
    w_down,
):
    every_query = lax.all_gather(queries, "ctx", axis=0, tiled=True)
    peak_scores, totals, accumulated = local_attention(every_query, prefix_keys, prefix_values)
    token_count, heads_local, head_width = accumulated.shape
    top_peak = lax.pmax(peak_scores, "ctx")
    factor = jnp.exp(peak_scores - top_peak)
    scaled_totals = totals * factor
    scaled_accum = (accumulated * factor[..., None]).reshape(token_count, heads_local * head_width)
    model_width = out_weight.shape[1]
    column_accum = lax.psum_scatter(
        scaled_accum.astype(jnp.bfloat16), "ctx", scatter_dimension=1, tiled=True
    ).astype(jnp.float32)
    all_totals = lax.psum(scaled_totals, "ctx")
    width_here = column_accum.shape[1]
    column_ids = lax.axis_index("ctx") * width_here + jnp.arange(width_here, dtype=jnp.int32)
    selector = (
        (column_ids // head_width)[None, :] == jnp.arange(heads_local, dtype=jnp.int32)[:, None]
    ).astype(jnp.float32)
    denominators = jnp.dot(all_totals, selector, precision=lax.Precision.HIGHEST)
    attended = (column_accum / denominators).astype(jnp.bfloat16)
    projected = lax.psum_scatter(
        jnp.dot(attended, out_weight, preferred_element_type=jnp.float32),
        ("ctx", "hd"),
        scatter_dimension=0,
        tiled=True,
    )
    stream = residual_in.astype(jnp.float32) + projected
    normed = (stream * lax.rsqrt(jnp.mean(stream * stream, axis=-1, keepdims=True) + 1e-06)).astype(
        jnp.bfloat16
    )
    context_count = lax.axis_size("ctx")
    head_groups = lax.axis_size("hd")
    expert_count = context_count * head_groups
    rows_here = normed.shape[0]
    slot_total = rows_here * TOP
    capacity = 2 * max(1, slot_total // expert_count)
    flat_ids = expert_ids.reshape(slot_total)
    onehot = (flat_ids[:, None] == jnp.arange(expert_count, dtype=jnp.int32)[None, :]).astype(
        jnp.int32
    )
    before = jnp.tril(jnp.ones((slot_total, slot_total), jnp.float32), -1)
    earlier = jnp.dot(
        before, onehot.astype(jnp.float32), precision=lax.Precision.HIGHEST
    ).astype(jnp.int32)
    position = jnp.sum(onehot * earlier, axis=1)
    target_row = flat_ids * capacity + position
    dispatch = (
        jnp.arange(expert_count * capacity, dtype=jnp.int32)[:, None] == target_row[None, :]
    ).astype(jnp.bfloat16)
    repeated = jnp.repeat(normed, TOP, axis=0)
    buffer = jnp.dot(dispatch, repeated, preferred_element_type=jnp.float32).astype(jnp.bfloat16)
    buffer = buffer.reshape(expert_count, capacity, model_width)
    slot_block = lax.all_to_all(buffer, ("ctx", "hd"), split_axis=0, concat_axis=0, tiled=True)
    sources, slot_count, feature_width = slot_block.shape
    flattened = slot_block.reshape(sources * slot_count, feature_width)
    gate_values = jnp.dot(flattened, w_gate[0], preferred_element_type=jnp.float32)
    up_values = jnp.dot(flattened, w_up[0], preferred_element_type=jnp.float32)
    hidden = (jax.nn.silu(gate_values) * up_values).astype(jnp.bfloat16)
    result = jnp.dot(hidden, w_down[0], preferred_element_type=jnp.float32).astype(jnp.bfloat16)
    returned_rows = lax.all_to_all(
        result.reshape(sources, slot_count, feature_width),
        ("ctx", "hd"),
        split_axis=0,
        concat_axis=0,
        tiled=True,
    )
    gathered = jnp.dot(
        dispatch.T,
        returned_rows.reshape(expert_count * capacity, model_width),
        preferred_element_type=jnp.float32,
    )
    weighted = gathered.reshape(rows_here, TOP, model_width) * gate_weights[:, :, None]
    mixture = jnp.sum(weighted, axis=1)
    return (stream + mixture).astype(jnp.bfloat16)


MESH = pl.DeviceIdType.MESH


def layer_kernel(
    ctxs,
    cores,
    q_ref,
    k_ref,
    v_ref,
    ow_ref,
    res_ref,
    ids_ref,
    gw_ref,
    wg_ref,
    wu_ref,
    wd_ref,
    out_ref,
    q_v,
    res_v,
    ids_v,
    gw_v,
    kraw,
    vraw,
    tmp,
    kd,
    vd,
    qbuf,
    qf,
    qs,
    w2,
    wgu,
    wd,
    numbuf,
    stbuf,
    numrecv,
    strecv,
    wst,
    wt,
    att,
    pjbuf,
    pjrecv,
    xbuf,
    xg,
    xs,
    gx,
    mine,
    give,
    take,
    lead,
    lead_out,
    lead_in,
    lead_sum,
    ybuf,
    yrecv,
    load_sem,
    q_send,
    q_recv,
    ow_send,
    ow_recv,
    num_send,
    num_recv,
    st_send,
    st_recv,
    pj_send,
    pj_recv,
    x_send,
    x_recv,
    give_send,
    take_recv,
    lead_send,
    lead_recv,
    lead_left,
    y_send,
    y_recv,
    late,
):
    mc = lax.axis_index("ctx")
    mh = lax.axis_index("hd")
    devices = ctxs * cores
    me = mc * cores + mh
    rows, width = res_ref.shape
    ffn = wd_ref.shape[0]
    own, groups, share_heads, head = q_ref.shape
    turns, targets_in_turn, pair_rows, _ = numbuf.shape
    tokens = own * ctxs
    half = tokens // cores
    pair_count = pair_rows // half
    rate = head ** (-0.5) * math.log2(math.e)

    def remote(src, dst, ssem, rsem, c, h):
        return pltpu.make_async_remote_copy(
            src_ref=src,
            dst_ref=dst,
            send_sem=ssem,
            recv_sem=rsem,
            device_id={"ctx": c, "hd": h},
            device_id_type=MESH,
        )

    def peer(step):
        c, bit = mc, 1
        while bit < ctxs:
            if step & bit:
                c = c + (1 - 2 * lax.rem(mc // bit, 2)) * bit
            bit *= 2
        return c

    ctx_peer = [peer(step) for step in range(ctxs)]
    core_peer = [mh, cores - 1 - mh]
    steps = [(kc, kh) for kc in reversed(range(ctxs)) for kh in (1, 0)]

    def push(src, dst, ssem, rsem, c, h):
        other = c * cores + h

        @pl.when(other != me)
        def _():
            remote(src, dst, ssem, rsem, c, h).start()

        @pl.when(other == me)
        def _():
            pltpu.make_async_copy(src, dst, rsem).start()

    def sent(src, ssem):
        pltpu.make_async_copy(src, src, ssem).wait()

    def landed(dst, rsem):
        pltpu.make_async_copy(dst, dst, rsem).wait()

    drains = []
    loads = [
        pltpu.make_async_copy(a, b, load_sem.at[i])
        for i, (a, b) in enumerate(
            (
                (k_ref, kraw),
                (v_ref, vraw),
                (ow_ref, w2.at[mh]),
                (wg_ref, wgu.at[:, 0:ffn]),
                (wu_ref, wgu.at[:, ffn : 2 * ffn]),
                (wd_ref, wd),
                (res_ref, res_v),
                (ids_ref, ids_v),
                (gw_ref, gw_v),
                (q_ref, q_v),
            )
        )
    ]
    barrier = pltpu.get_barrier_semaphore()

    last = ctxs - 1

    def greet(sem, kc, kh):
        pl.semaphore_signal(
            sem,
            inc=1,
            device_id={"ctx": ctx_peer[kc], "hd": core_peer[kh]},
            device_id_type=MESH,
        )

    @pl.when(mc != last)
    def _():
        for kc, kh in steps[:-2]:
            greet(barrier, kc, kh)

    greet(barrier, 0, 1)
    for one in (loads[9], *loads[:2], *loads[6:9]):
        one.start()

    loads[9].wait()
    for g in range(groups):
        qf[g] = q_v[:, g].astype(jnp.float32).reshape(own * share_heads, head)
        for h in range(share_heads):
            qs[g, h * own : (h + 1) * own, :] = qf[
                g, pl.ds(h, own, stride=share_heads), :
            ].astype(jnp.bfloat16)
    pl.semaphore_wait(barrier, devices - 1 - cores + cores * (mc // last))

    @pl.when(mc == last)
    def _():
        for kc, kh in steps[:-2]:
            greet(late, kc, kh)

    def send_q(c, sem):
        remote(qs, qbuf.at[mc], sem, q_recv.at[mc], c, mh).start()

    for kc in range(1, ctxs):
        pl.when(ctx_peer[kc] != last)(lambda kc=kc: send_q(ctx_peer[kc], q_send.at[kc]))
    pltpu.make_async_copy(qs, qbuf.at[mc], q_recv.at[mc]).start()
    ow_copy = remote(ow_ref, w2.at[mh], ow_send, ow_recv, mc, cores - 1 - mh)
    ow_copy.start()
    for one in loads[2:6]:
        one.start()

    def drain_q():
        for kc in range(1, ctxs):
            pl.when(ctx_peer[kc] != last)(lambda kc=kc: sent(qs, q_send.at[kc]))
        pl.when(mc != last)(lambda: sent(qs, q_send.at[0]))

    drains.append(drain_q)
    piece = tmp.shape[0]
    share = piece // groups

    def split(raw, store):
        @pl.loop(0, raw.shape[0] // piece)
        def _(i):
            tmp[...] = raw[pl.ds(pl.multiple_of(i * piece, piece), piece), :].astype(jnp.float32)
            for g in range(groups):
                store(g, i, tmp[pl.ds(g, share, stride=groups), :].astype(jnp.bfloat16))

    def store_k(g, i, value):
        kd[g, pl.ds(pl.multiple_of(i * share, share), share), :] = value

    def store_v(g, i, value):
        at = pl.ds(pl.multiple_of(i * share, share), share)
        vd[g, at, 0:head] = value
        vd[g, at, head : 2 * head] = jnp.ones_like(value)

    loads[0].wait()
    split(kraw, store_k)
    loads[1].wait()
    split(vraw, store_v)

    @pl.when(mc != last)
    def _():
        pl.semaphore_wait(late, cores)
        send_q(last, q_send.at[0])

    wst[...] = jnp.zeros_like(wst)
    for one in loads[6:9]:
        one.wait()
    lane = lax.broadcasted_iota(jnp.int32, (rows, head), 1)
    offset = lane - lax.broadcasted_iota(jnp.int32, (rows, head), 0)
    spread = jnp.zeros((rows, head), jnp.float32)
    for e in range(devices):
        gate = jnp.sum(jnp.where(ids_v[...] == e, gw_v[...], 0.0), axis=1, keepdims=True)
        spread = spread + jnp.where(offset == e * rows, gate, 0.0)
    gates = jnp.sum(spread, axis=0, keepdims=True)

    sources = ctxs // cores
    here, there = mc // sources, mc // targets_in_turn
    lanes = lax.broadcasted_iota(jnp.int32, (sources * own * share_heads, head), 1)
    for far in (0, 1):
        part = here if far == 0 else 1 - here
        for i in range(sources):
            c = part * sources + i
            landed(qbuf.at[c], q_recv.at[c])

        def rows_of(value, i):
            starts = [
                (n * share_heads + i * pair_count + a) * own
                for a in range(pair_count)
                for n in range(sources)
            ]
            return jnp.concatenate([value[at : at + own] for at in starts], axis=0)

        for near in (0, 1):
            turn = 2 * far + near
            g = there if near else 1 - there
            core = 1 if near == far else 0
            s = lax.dot_general(
                jnp.concatenate([qbuf[part * sources + i, g] for i in range(sources)], axis=0),
                kd[g],
                (((1,), (1,)), ((), ())), preferred_element_type=jnp.float32
            )
            m = jnp.max(s, axis=1, keepdims=True)
            p = jnp.exp2((s - m) * rate).astype(jnp.bfloat16)
            o = jnp.dot(p, vd[g], preferred_element_type=jnp.float32)
            stat = jnp.where(lanes == 0, m, o[:, head : 2 * head])
            for i in range(targets_in_turn):
                numbuf[turn, i] = rows_of(o[:, 0:head], i).astype(jnp.bfloat16)
                if i % 2 == 0:
                    both = jnp.concatenate([rows_of(stat, i), rows_of(stat, i + 1)], axis=0)
                    stbuf[turn, i // 2, 0:2] = both.T[0:2]
                    stbuf[turn, i // 2, 2:3] = gates
            for i in range(targets_in_turn):
                c = g * targets_in_turn + i
                for src, dst, ssem, rsem in (
                    (stbuf.at[turn, i // 2], strecv, st_send, st_recv),
                    (numbuf.at[turn, i], numrecv, num_send, num_recv),
                ):
                    args = (src, dst.at[mc, mh], ssem.at[turn, i], rsem.at[mc, mh], c, core)
                    if near:
                        push(*args)
                    else:
                        remote(*args).start()

    def drain_num():
        for turn in range(turns):
            core = turn // 2
            for i in range(targets_in_turn):

                def both(turn=turn, i=i):
                    sent(stbuf.at[turn, 0], st_send.at[turn, i])
                    sent(numbuf.at[turn, i], num_send.at[turn, i])

                if turn % 2 == 0:
                    both()
                else:
                    pl.when((there * targets_in_turn + i) * cores + core != me)(both)

    drains.append(drain_num)
    for h in range(cores):
        peaks, totals = [], []
        for c in range(ctxs):
            landed(strecv.at[c, h], st_recv.at[c, h])
            peaks.append(strecv[c, h, 0:1, :])
            totals.append(strecv[c, h, 1:2, :])
        peaks = jnp.concatenate(peaks, axis=0)
        totals = jnp.concatenate(totals, axis=0)
        factor = jnp.exp2((peaks - jnp.max(peaks, axis=0, keepdims=True)) * rate)
        wst[h * ctxs : (h + 1) * ctxs, :] = factor / jnp.sum(
            totals * factor, axis=0, keepdims=True
        )
    wt[...] = wst[...].T
    for h in reversed(range(cores)):
        for c in range(ctxs):
            landed(numrecv.at[c, h], num_recv.at[c, h])
        for a in range(pair_count):
            at = lax.rem(mc, 2) * pair_rows + a * half
            shares = wt[pl.ds(pl.multiple_of(at, half), half), :]
            total = jnp.zeros((half, head), jnp.float32)
            for c in range(ctxs):
                at = h * ctxs + c
                total = total + numrecv[c, h, a * half : (a + 1) * half].astype(jnp.float32) * shares[:, at : at + 1]
            at = (h * pair_count + a) * head
            att[:, at : at + head] = total.astype(jnp.bfloat16)

    partner = core_peer[1]
    for h, core in enumerate((partner, mh)):
        for c in range(ctxs):
            at = (h * ctxs + c) * rows
            gx[at : at + rows, :] = jnp.broadcast_to(strecv[c, core, 2:3, :], (rows, head))
    row = lax.broadcasted_iota(jnp.int32, gx.shape, 0)
    lane = lax.broadcasted_iota(jnp.int32, gx.shape, 1)
    gate = jnp.sum(
        jnp.where(lane == me * rows + lax.rem(row, rows), gx[...], 0.0), axis=1, keepdims=True
    )

    loads[2].wait()
    ow_copy.wait()
    projected = jnp.dot(
        att[...], w2[...].reshape(att.shape[1], width), preferred_element_type=jnp.float32
    )
    targets = half // rows
    for j in range(targets):
        pjbuf[j] = projected[j * rows : (j + 1) * rows].astype(jnp.bfloat16)

    chips = targets // cores
    low = lax.rem(mc, chips)
    away = mh
    base = (here + away - 2 * here * away) * chips
    for kc in reversed(range(chips)):
        for kh in (1, 0):
            c = base + ctx_peer[kc] - (mc - low)
            h = core_peer[kh]
            j = (c - base) * cores + h
            go = remote if kc or kh else push
            k = kc * cores + kh
            copy = go(pjbuf.at[j], pjrecv.at[mc], pj_send.at[k], pj_recv.at[mc], c, h)
            if kc or kh:
                copy.start()

    def drain_pj():
        for k in range(1, targets):
            sent(pjbuf.at[0], pj_send.at[k])

        @pl.when(base != mc - low)
        def _():
            sent(pjbuf.at[0], pj_send.at[0])

    drains.append(drain_pj)
    stream = res_v[...].astype(jnp.float32)
    for kc in range(ctxs):
        c = ctx_peer[kc]
        landed(pjrecv.at[c], pj_recv.at[c])
        stream = stream + pjrecv[c].astype(jnp.float32)
    square = jnp.mean(stream * stream, axis=-1, keepdims=True)
    xbuf[...] = (stream * lax.rsqrt(square + 1e-06)).astype(jnp.bfloat16)

    for kc in reversed(range(1, ctxs)):
        remote(
            xbuf, xg.at[me], x_send.at[kc * cores], x_recv.at[me], ctx_peer[kc], mh
        ).start()
    remote(xbuf, xg.at[me], x_send.at[1], x_recv.at[me], mc, partner).start()
    pltpu.make_async_copy(xbuf, xg.at[me], x_recv.at[me]).start()
    for kc in range(1, ctxs):
        came = ctx_peer[kc] * cores + mh
        landed(xg.at[came], x_recv.at[came])
        remote(
            xg.at[came],
            xg.at[came],
            x_send.at[kc * cores + 1],
            x_recv.at[came],
            mc,
            partner,
        ).start()

    def drain_x():
        for k in range(1, devices):
            sent(xbuf, x_send.at[k])

    drains.append(drain_x)
    for one in loads[3:6]:
        one.wait()
    landed(xg.at[me], x_recv.at[me])
    for c in range(ctxs):
        came = c * cores + partner
        landed(xg.at[came], x_recv.at[came])
    for h, core in enumerate((partner, mh)):
        for c in range(ctxs):
            at = (h * ctxs + c) * rows
            xs[at : at + rows, :] = xg[c * cores + core].astype(jnp.float32)
    x = xs[...].astype(jnp.bfloat16)
    both = jnp.dot(x, wgu[...], preferred_element_type=jnp.float32)
    gate_values, up_values = both[:, 0:ffn], both[:, ffn : 2 * ffn]
    hidden = (gate_values / (1.0 + jnp.exp(-gate_values)) * up_values).astype(jnp.bfloat16)

    near_rows = mine.shape[0]
    result = gate * jnp.dot(hidden, wd[...], preferred_element_type=jnp.float32)
    for b in range(cores):
        block = result[b * near_rows : b * near_rows + rows]
        lead[b] = block
        lead_out[b] = block.astype(jnp.bfloat16)

    @pl.when(mh == 0)
    def _():
        remote(lead_out, lead_in, lead_send, lead_recv, mc, partner).start()

    give[...] = result[near_rows:].astype(jnp.bfloat16)
    remote(give, take, give_send, take_recv, mc, partner).start()
    mine[...] = result[0:near_rows]

    @pl.when(mh == 1)
    def _():
        landed(lead_in, lead_recv)
        for b in range(cores):
            lead_sum[b] = (lead[b] + lead_in[1 - b].astype(jnp.float32)).astype(jnp.bfloat16)
        for b in range(cores):
            push(lead_sum.at[b], yrecv.at[mc], lead_left.at[b], y_recv.at[mc], 0, b)

    landed(take, take_recv)
    total = mine[...] + take[...].astype(jnp.float32)
    for c in range(1, ctxs):
        ybuf[c] = total[c * rows : (c + 1) * rows].astype(jnp.bfloat16)
    for c in range(1, ctxs):
        remote(ybuf.at[c], yrecv.at[mc], y_send.at[c], y_recv.at[mc], c, partner).start()

    def drain_y():
        sent(give, give_send)
        for c in range(1, ctxs):
            sent(ybuf.at[0], y_send.at[c])

        @pl.when(mh == 0)
        def _():
            sent(lead_out, lead_send)

        @pl.when(mh == 1)
        def _():
            for b in range(cores):
                pl.when(me != b)(lambda b=b: sent(lead_sum.at[b], lead_left.at[b]))

    drains.append(drain_y)
    for kc in range(ctxs):
        c = ctx_peer[kc]
        landed(yrecv.at[c], y_recv.at[c])
        stream = stream + yrecv[c].astype(jnp.float32)
    out_ref[...] = stream.astype(out_ref.dtype)

    for drain in drains:
        drain()


def on_device(
    queries,
    prefix_keys,
    prefix_values,
    out_weight,
    residual_in,
    expert_ids,
    gate_weights,
    w_gate,
    w_up,
    w_down,
):
    ctxs, cores = lax.axis_size("ctx"), lax.axis_size("hd")
    devices = ctxs * cores
    own, heads, head = queries.shape
    positions, groups, _ = prefix_keys.shape
    depth, width = out_weight.shape
    rows = residual_in.shape[0]
    ffn = w_gate.shape[2]
    tokens = own * ctxs
    pair_count = heads // ctxs
    fits = (
        cores == 2
        and pair_count * ctxs == heads
        and pair_count * tokens == head
        and ctxs % 8 == 0
        and ctxs & (ctxs - 1) == 0
        and groups == 2
        and cores * ctxs <= head
        and devices * rows <= head
        and own * ctxs % (cores * 16) == 0
    )
    if not fits:
        return on_device_general(
            queries,
            prefix_keys,
            prefix_values,
            out_weight,
            residual_in,
            expert_ids,
            gate_weights,
            w_gate,
            w_up,
            w_down,
        )
    half = tokens // cores
    held = [
        pltpu.with_memory_space_constraint(a, pltpu.HBM)
        for a in (
            queries.reshape(own, groups, heads // groups, head),
            prefix_keys.reshape(positions * groups, head),
            prefix_values.reshape(positions * groups, head),
            out_weight,
            residual_in,
            expert_ids,
            gate_weights,
            w_gate[0],
            w_up[0],
            w_down[0],
        )
    ]
    any_spec = pl.BlockSpec(memory_space=pl.ANY)
    vmem_spec = pl.BlockSpec(memory_space=pltpu.VMEM)
    bf, f32 = jnp.bfloat16, jnp.float32
    dma = pltpu.SemaphoreType.DMA
    return pl.pallas_call(
        functools.partial(layer_kernel, ctxs, cores),
        out_shape=jax.ShapeDtypeStruct((rows, width), bf),
        in_specs=[any_spec] * 10,
        out_specs=vmem_spec,
        scratch_shapes=[
            pltpu.VMEM((own, groups, heads // groups, head), bf),
            pltpu.VMEM(residual_in.shape, bf),
            pltpu.VMEM(expert_ids.shape, expert_ids.dtype),
            pltpu.VMEM(gate_weights.shape, f32),
            pltpu.VMEM((positions * groups, head), bf),
            pltpu.VMEM((positions * groups, head), bf),
            pltpu.VMEM((256 * groups, head), f32),
            pltpu.VMEM((groups, positions, head), bf),
            pltpu.VMEM((groups, positions, 2 * head), bf),
            pltpu.VMEM((ctxs, groups, own * heads // groups, head), bf),
            pltpu.VMEM((groups, own * heads // groups, head), f32),
            pltpu.VMEM((groups, own * heads // groups, head), bf),
            pltpu.VMEM((cores, depth, width), bf),
            pltpu.VMEM((width, 2 * ffn), bf),
            pltpu.VMEM((ffn, width), bf),
            pltpu.VMEM((cores * groups, ctxs // groups, pair_count * half, head), bf),
            pltpu.VMEM((cores * groups, ctxs // groups // 2, 3, head), f32),
            pltpu.VMEM((ctxs, cores, pair_count * half, head), bf),
            pltpu.VMEM((ctxs, cores, 3, head), f32),
            pltpu.VMEM((head, head), f32),
            pltpu.VMEM((head, head), f32),
            pltpu.VMEM((half, cores * depth), bf),
            pltpu.VMEM((half // rows, rows, width), bf),
            pltpu.VMEM((ctxs, rows, width), bf),
            pltpu.VMEM((rows, width), bf),
            pltpu.VMEM((devices, rows, width), bf),
            pltpu.VMEM((devices * rows, width), f32),
            pltpu.VMEM((devices * rows, head), f32),
            pltpu.VMEM((ctxs * rows, width), f32),
            pltpu.VMEM((ctxs * rows, width), bf),
            pltpu.VMEM((ctxs * rows, width), bf),
            pltpu.VMEM((cores, rows, width), f32),
            pltpu.VMEM((cores, rows, width), bf),
            pltpu.VMEM((cores, rows, width), bf),
            pltpu.VMEM((cores, rows, width), bf),
            pltpu.VMEM((ctxs, rows, width), bf),
            pltpu.VMEM((ctxs, rows, width), bf),
            dma((10,)),
            dma((ctxs,)),
            dma((ctxs,)),
            dma,
            dma,
            dma((cores * groups, ctxs // groups)),
            dma((ctxs, cores)),
            dma((cores * groups, ctxs // groups)),
            dma((ctxs, cores)),
            dma((half // rows,)),
            dma((ctxs,)),
            dma((devices,)),
            dma((devices,)),
            dma,
            dma,
            dma,
            dma,
            dma((cores,)),
            dma((ctxs,)),
            dma((ctxs,)),
            pltpu.SemaphoreType.REGULAR,
        ],
        compiler_params=pltpu.CompilerParams(
            collective_id=0, has_side_effects=True, vmem_limit_bytes=32 * 1024 * 1024
        ),
    )(*held)


def solution(mesh):
    placed = (
        P(("grp", "ctx"), "hd", None),
        P(("grp", "ctx"), "hd", None),
        P(("grp", "ctx"), "hd", None),
        P(("hd", "ctx"), None),
        P(("grp", "ctx", "hd"), None),
        P(("grp", "ctx", "hd"), None),
        P(("grp", "ctx", "hd"), None),
        P(("ctx", "hd"), None, None),
        P(("ctx", "hd"), None, None),
        P(("ctx", "hd"), None, None),
    )
    return jax.shard_map(
        on_device,
        mesh=mesh,
        in_specs=placed,
        out_specs=P(("grp", "ctx", "hd"), None),
        check_vma=False,
    )
```

```python
import jax
import jax.numpy as jnp
from jax import lax
from jax.experimental import pallas as pl
from jax.experimental.pallas import tpu as pltpu
from jax.sharding import PartitionSpec as P
import functools
import math

TOP = 8
KV_BLOCK = 512


NEG_START = -1e30


def local_attention(queries, prefix_keys, prefix_values):
    token_count, heads_local, head_width = queries.shape
    key_heads = prefix_keys.shape[1]
    grouped = heads_local // key_heads
    query_view = queries.reshape(token_count, key_heads, grouped, head_width)
    block_count = prefix_keys.shape[0] // KV_BLOCK
    key_blocks = prefix_keys.reshape(block_count, KV_BLOCK, key_heads, head_width)
    value_blocks = prefix_values.reshape(block_count, KV_BLOCK, key_heads, head_width)
    scaling = head_width ** (-0.5)

    def advance(running, pieces):
        peak_scores, totals, accumulated = running
        key_piece, value_piece = pieces
        scores = (
            jnp.einsum("sgjd,kgd->sgjk", query_view, key_piece, preferred_element_type=jnp.float32)
            * scaling
        )
        block_peak = jnp.max(scores, axis=-1)
        weights = jnp.exp(scores - block_peak[..., None]).astype(jnp.bfloat16)
        block_total = jnp.sum(weights.astype(jnp.float32), axis=-1)
        block_out = jnp.einsum(
            "sgjk,kgd->sgjd", weights, value_piece, preferred_element_type=jnp.float32
        )
        raised = jnp.maximum(peak_scores, block_peak)
        old_factor = jnp.exp(peak_scores - raised)
        new_factor = jnp.exp(block_peak - raised)
        totals = totals * old_factor + block_total * new_factor
        accumulated = accumulated * old_factor[..., None] + block_out * new_factor[..., None]
        return ((raised, totals, accumulated), None)

    start_state = (
        jnp.full((token_count, key_heads, grouped), NEG_START, jnp.float32),
        jnp.zeros((token_count, key_heads, grouped), jnp.float32),
        jnp.zeros((token_count, key_heads, grouped, head_width), jnp.float32),
    )
    final_state, leftover = lax.scan(advance, start_state, (key_blocks, value_blocks))
    peak_scores = final_state[0].reshape(token_count, heads_local)
    totals = final_state[1].reshape(token_count, heads_local)
    accumulated = final_state[2].reshape(token_count, heads_local, head_width)
    return (peak_scores, totals, accumulated)


def on_device_general(
    queries,
    prefix_keys,
    prefix_values,
    out_weight,
    residual_in,
    expert_ids,
    gate_weights,
    w_gate,
    w_up,
    w_down,
):
    every_query = lax.all_gather(queries, "ctx", axis=0, tiled=True)
    peak_scores, totals, accumulated = local_attention(every_query, prefix_keys, prefix_values)
    token_count, heads_local, head_width = accumulated.shape
    top_peak = lax.pmax(peak_scores, "ctx")
    factor = jnp.exp(peak_scores - top_peak)
    scaled_totals = totals * factor
    scaled_accum = (accumulated * factor[..., None]).reshape(token_count, heads_local * head_width)
    model_width = out_weight.shape[1]
    column_accum = lax.psum_scatter(
        scaled_accum.astype(jnp.bfloat16), "ctx", scatter_dimension=1, tiled=True
    ).astype(jnp.float32)
    all_totals = lax.psum(scaled_totals, "ctx")
    width_here = column_accum.shape[1]
    column_ids = lax.axis_index("ctx") * width_here + jnp.arange(width_here, dtype=jnp.int32)
    selector = (
        (column_ids // head_width)[None, :] == jnp.arange(heads_local, dtype=jnp.int32)[:, None]
    ).astype(jnp.float32)
    denominators = jnp.dot(all_totals, selector, precision=lax.Precision.HIGHEST)
    attended = (column_accum / denominators).astype(jnp.bfloat16)
    projected = lax.psum_scatter(
        jnp.dot(attended, out_weight, preferred_element_type=jnp.float32),
        ("ctx", "hd"),
        scatter_dimension=0,
        tiled=True,
    )
    stream = residual_in.astype(jnp.float32) + projected
    normed = (stream * lax.rsqrt(jnp.mean(stream * stream, axis=-1, keepdims=True) + 1e-06)).astype(
        jnp.bfloat16
    )
    context_count = lax.axis_size("ctx")
    head_groups = lax.axis_size("hd")
    expert_count = context_count * head_groups
    rows_here = normed.shape[0]
    slot_total = rows_here * TOP
    capacity = 2 * max(1, slot_total // expert_count)
    flat_ids = expert_ids.reshape(slot_total)
    onehot = (flat_ids[:, None] == jnp.arange(expert_count, dtype=jnp.int32)[None, :]).astype(
        jnp.int32
    )
    before = jnp.tril(jnp.ones((slot_total, slot_total), jnp.float32), -1)
    earlier = jnp.dot(
        before, onehot.astype(jnp.float32), precision=lax.Precision.HIGHEST
    ).astype(jnp.int32)
    position = jnp.sum(onehot * earlier, axis=1)
    target_row = flat_ids * capacity + position
    dispatch = (
        jnp.arange(expert_count * capacity, dtype=jnp.int32)[:, None] == target_row[None, :]
    ).astype(jnp.bfloat16)
    repeated = jnp.repeat(normed, TOP, axis=0)
    buffer = jnp.dot(dispatch, repeated, preferred_element_type=jnp.float32).astype(jnp.bfloat16)
    buffer = buffer.reshape(expert_count, capacity, model_width)
    slot_block = lax.all_to_all(buffer, ("ctx", "hd"), split_axis=0, concat_axis=0, tiled=True)
    sources, slot_count, feature_width = slot_block.shape
    flattened = slot_block.reshape(sources * slot_count, feature_width)
    gate_values = jnp.dot(flattened, w_gate[0], preferred_element_type=jnp.float32)
    up_values = jnp.dot(flattened, w_up[0], preferred_element_type=jnp.float32)
    hidden = (jax.nn.silu(gate_values) * up_values).astype(jnp.bfloat16)
    result = jnp.dot(hidden, w_down[0], preferred_element_type=jnp.float32).astype(jnp.bfloat16)
    returned_rows = lax.all_to_all(
        result.reshape(sources, slot_count, feature_width),
        ("ctx", "hd"),
        split_axis=0,
        concat_axis=0,
        tiled=True,
    )
    gathered = jnp.dot(
        dispatch.T,
        returned_rows.reshape(expert_count * capacity, model_width),
        preferred_element_type=jnp.float32,
    )
    weighted = gathered.reshape(rows_here, TOP, model_width) * gate_weights[:, :, None]
    mixture = jnp.sum(weighted, axis=1)
    return (stream + mixture).astype(jnp.bfloat16)


MESH = pl.DeviceIdType.MESH


def layer_kernel(
    ctxs,
    cores,
    q_ref,
    k_ref,
    v_ref,
    ow_ref,
    res_ref,
    ids_ref,
    gw_ref,
    wg_ref,
    wu_ref,
    wd_ref,
    out_ref,
    q_v,
    res_v,
    ids_v,
    gw_v,
    kraw,
    vraw,
    tmp,
    kd,
    vd,
    qbuf,
    qf,
    qs,
    w2,
    wgu,
    wd,
    numbuf,
    stbuf,
    numrecv,
    strecv,
    wst,
    wt,
    att,
    pjbuf,
    pjrecv,
    xbuf,
    xg,
    xs,
    gx,
    mine,
    give,
    take,
    lead,
    lead_out,
    lead_in,
    lead_sum,
    ybuf,
    yrecv,
    load_sem,
    q_send,
    q_recv,
    ow_send,
    ow_recv,
    num_send,
    num_recv,
    st_send,
    st_recv,
    pj_send,
    pj_recv,
    x_send,
    x_recv,
    give_send,
    take_recv,
    lead_send,
    lead_recv,
    lead_left,
    y_send,
    y_recv,
    late,
):
    mc = lax.axis_index("ctx")
    mh = lax.axis_index("hd")
    devices = ctxs * cores
    me = mc * cores + mh
    rows, width = res_ref.shape
    ffn = wd_ref.shape[0]
    own, groups, share_heads, head = q_ref.shape
    turns, targets_in_turn, pair_rows, _ = numbuf.shape
    tokens = own * ctxs
    half = tokens // cores
    pair_count = pair_rows // half
    rate = head ** (-0.5) * math.log2(math.e)

    def remote(src, dst, ssem, rsem, c, h):
        return pltpu.make_async_remote_copy(
            src_ref=src,
            dst_ref=dst,
            send_sem=ssem,
            recv_sem=rsem,
            device_id={"ctx": c, "hd": h},
            device_id_type=MESH,
        )

    def peer(step):
        c, bit = mc, 1
        while bit < ctxs:
            if step & bit:
                c = c + (1 - 2 * lax.rem(mc // bit, 2)) * bit
            bit *= 2
        return c

    ctx_peer = [peer(step) for step in range(ctxs)]
    core_peer = [mh, cores - 1 - mh]
    steps = [(kc, kh) for kc in reversed(range(ctxs)) for kh in (1, 0)]

    def push(src, dst, ssem, rsem, c, h):
        other = c * cores + h

        @pl.when(other != me)
        def _():
            remote(src, dst, ssem, rsem, c, h).start()

        @pl.when(other == me)
        def _():
            pltpu.make_async_copy(src, dst, rsem).start()

    def sent(src, ssem):
        pltpu.make_async_copy(src, src, ssem).wait()

    def landed(dst, rsem):
        pltpu.make_async_copy(dst, dst, rsem).wait()

    drains = []
    loads = [
        pltpu.make_async_copy(a, b, load_sem.at[i])
        for i, (a, b) in enumerate(
            (
                (k_ref, kraw),
                (v_ref, vraw),
                (ow_ref, w2.at[mh]),
                (wg_ref, wgu.at[:, 0:ffn]),
                (wu_ref, wgu.at[:, ffn : 2 * ffn]),
                (wd_ref, wd),
                (res_ref, res_v),
                (ids_ref, ids_v),
                (gw_ref, gw_v),
                (q_ref, q_v),
            )
        )
    ]
    barrier = pltpu.get_barrier_semaphore()

    last = ctxs - 1

    def greet(sem, kc, kh):
        pl.semaphore_signal(
            sem,
            inc=1,
            device_id={"ctx": ctx_peer[kc], "hd": core_peer[kh]},
            device_id_type=MESH,
        )

    @pl.when(mc != last)
    def _():
        for kc, kh in steps[:-2]:
            greet(barrier, kc, kh)

    greet(barrier, 0, 1)
    for one in (loads[9], *loads[:2], *loads[6:9]):
        one.start()

    loads[9].wait()
    for g in range(groups):
        qf[g] = q_v[:, g].astype(jnp.float32).reshape(own * share_heads, head)
        for h in range(share_heads):
            qs[g, h * own : (h + 1) * own, :] = qf[
                g, pl.ds(h, own, stride=share_heads), :
            ].astype(jnp.bfloat16)
    pl.semaphore_wait(barrier, devices - 1 - cores + cores * (mc // last))

    @pl.when(mc == last)
    def _():
        for kc, kh in steps[:-2]:
            greet(late, kc, kh)

    def send_q(c, sem):
        remote(qs, qbuf.at[mc], sem, q_recv.at[mc], c, mh).start()

    for kc in range(1, ctxs):
        pl.when(ctx_peer[kc] != last)(lambda kc=kc: send_q(ctx_peer[kc], q_send.at[kc]))
    pltpu.make_async_copy(qs, qbuf.at[mc], q_recv.at[mc]).start()
    ow_copy = remote(ow_ref, w2.at[mh], ow_send, ow_recv, mc, cores - 1 - mh)
    ow_copy.start()
    for one in loads[2:6]:
        one.start()

    def drain_q():
        for kc in range(1, ctxs):
            pl.when(ctx_peer[kc] != last)(lambda kc=kc: sent(qs, q_send.at[kc]))
        pl.when(mc != last)(lambda: sent(qs, q_send.at[0]))

    drains.append(drain_q)
    piece = tmp.shape[0]
    share = piece // groups

    def split(raw, store):
        @pl.loop(0, raw.shape[0] // piece)
        def _(i):
            tmp[...] = raw[pl.ds(pl.multiple_of(i * piece, piece), piece), :].astype(jnp.float32)
            for g in range(groups):
                store(g, i, tmp[pl.ds(g, share, stride=groups), :].astype(jnp.bfloat16))

    def store_k(g, i, value):
        kd[g, pl.ds(pl.multiple_of(i * share, share), share), :] = value

    def store_v(g, i, value):
        at = pl.ds(pl.multiple_of(i * share, share), share)
        vd[g, at, 0:head] = value
        vd[g, at, head : 2 * head] = jnp.ones_like(value)

    loads[0].wait()
    split(kraw, store_k)

    @pl.when(mc != last)
    def _():
        pl.semaphore_wait(late, cores)
        send_q(last, q_send.at[0])

    loads[1].wait()
    split(vraw, store_v)

    wst[...] = jnp.zeros_like(wst)
    for one in loads[6:9]:
        one.wait()
    lane = lax.broadcasted_iota(jnp.int32, (rows, head), 1)
    offset = lane - lax.broadcasted_iota(jnp.int32, (rows, head), 0)
    spread = jnp.zeros((rows, head), jnp.float32)
    for e in range(devices):
        gate = jnp.sum(jnp.where(ids_v[...] == e, gw_v[...], 0.0), axis=1, keepdims=True)
        spread = spread + jnp.where(offset == e * rows, gate, 0.0)
    gates = jnp.sum(spread, axis=0, keepdims=True)

    sources = ctxs // cores
    here, there = mc // sources, mc // targets_in_turn
    lanes = lax.broadcasted_iota(jnp.int32, (sources * own * share_heads, head), 1)
    for far in (0, 1):
        part = here if far == 0 else 1 - here
        for i in range(sources):
            c = part * sources + i
            landed(qbuf.at[c], q_recv.at[c])

        def rows_of(value, i):
            starts = [
                (n * share_heads + i * pair_count + a) * own
                for a in range(pair_count)
                for n in range(sources)
            ]
            return jnp.concatenate([value[at : at + own] for at in starts], axis=0)

        for near in (0, 1):
            turn = 2 * far + near
            g = there if near else 1 - there
            core = 1 if near == far else 0
            s = lax.dot_general(
                jnp.concatenate([qbuf[part * sources + i, g] for i in range(sources)], axis=0),
                kd[g],
                (((1,), (1,)), ((), ())), preferred_element_type=jnp.float32
            )
            m = jnp.max(s, axis=1, keepdims=True)
            p = jnp.exp2((s - m) * rate).astype(jnp.bfloat16)
            o = jnp.dot(p, vd[g], preferred_element_type=jnp.float32)
            stat = jnp.where(lanes == 0, m, o[:, head : 2 * head])
            for i in range(targets_in_turn):
                numbuf[turn, i] = rows_of(o[:, 0:head], i).astype(jnp.bfloat16)
                if i % 2 == 0:
                    both = jnp.concatenate([rows_of(stat, i), rows_of(stat, i + 1)], axis=0)
                    stbuf[turn, i // 2, 0:2] = both.T[0:2]
                    stbuf[turn, i // 2, 2:3] = gates
            for i in range(targets_in_turn):
                c = g * targets_in_turn + i
                for src, dst, ssem, rsem in (
                    (stbuf.at[turn, i // 2], strecv, st_send, st_recv),
                    (numbuf.at[turn, i], numrecv, num_send, num_recv),
                ):
                    args = (src, dst.at[mc, mh], ssem.at[turn, i], rsem.at[mc, mh], c, core)
                    if near:
                        push(*args)
                    else:
                        remote(*args).start()

    def drain_num():
        for turn in range(turns):
            core = turn // 2
            for i in range(targets_in_turn):

                def both(turn=turn, i=i):
                    sent(stbuf.at[turn, 0], st_send.at[turn, i])
                    sent(numbuf.at[turn, i], num_send.at[turn, i])

                if turn % 2 == 0:
                    both()
                else:
                    pl.when((there * targets_in_turn + i) * cores + core != me)(both)

    drains.append(drain_num)
    for h in range(cores):
        peaks, totals = [], []
        for c in range(ctxs):
            landed(strecv.at[c, h], st_recv.at[c, h])
            peaks.append(strecv[c, h, 0:1, :])
            totals.append(strecv[c, h, 1:2, :])
        peaks = jnp.concatenate(peaks, axis=0)
        totals = jnp.concatenate(totals, axis=0)
        factor = jnp.exp2((peaks - jnp.max(peaks, axis=0, keepdims=True)) * rate)
        wst[h * ctxs : (h + 1) * ctxs, :] = factor / jnp.sum(
            totals * factor, axis=0, keepdims=True
        )
    wt[...] = wst[...].T
    for h in reversed(range(cores)):
        for c in range(ctxs):
            landed(numrecv.at[c, h], num_recv.at[c, h])
        for a in range(pair_count):
            at = lax.rem(mc, 2) * pair_rows + a * half
            shares = wt[pl.ds(pl.multiple_of(at, half), half), :]
            total = jnp.zeros((half, head), jnp.float32)
            for c in range(ctxs):
                at = h * ctxs + c
                total = total + numrecv[c, h, a * half : (a + 1) * half].astype(jnp.float32) * shares[:, at : at + 1]
            at = (h * pair_count + a) * head
            att[:, at : at + head] = total.astype(jnp.bfloat16)

    partner = core_peer[1]
    for h, core in enumerate((partner, mh)):
        for c in range(ctxs):
            at = (h * ctxs + c) * rows
            gx[at : at + rows, :] = jnp.broadcast_to(strecv[c, core, 2:3, :], (rows, head))
    row = lax.broadcasted_iota(jnp.int32, gx.shape, 0)
    lane = lax.broadcasted_iota(jnp.int32, gx.shape, 1)
    gate = jnp.sum(
        jnp.where(lane == me * rows + lax.rem(row, rows), gx[...], 0.0), axis=1, keepdims=True
    )

    loads[2].wait()
    ow_copy.wait()
    projected = jnp.dot(
        att[...], w2[...].reshape(att.shape[1], width), preferred_element_type=jnp.float32
    )
    targets = half // rows
    for j in range(targets):
        pjbuf[j] = projected[j * rows : (j + 1) * rows].astype(jnp.bfloat16)

    chips = targets // cores
    low = lax.rem(mc, chips)
    away = mh
    base = (here + away - 2 * here * away) * chips
    for kc in reversed(range(chips)):
        for kh in (1, 0):
            c = base + ctx_peer[kc] - (mc - low)
            h = core_peer[kh]
            j = (c - base) * cores + h
            go = remote if kc or kh else push
            k = kc * cores + kh
            copy = go(pjbuf.at[j], pjrecv.at[mc], pj_send.at[k], pj_recv.at[mc], c, h)
            if kc or kh:
                copy.start()

    def drain_pj():
        for k in range(1, targets):
            sent(pjbuf.at[0], pj_send.at[k])

        @pl.when(base != mc - low)
        def _():
            sent(pjbuf.at[0], pj_send.at[0])

    drains.append(drain_pj)
    stream = res_v[...].astype(jnp.float32)
    for kc in range(ctxs):
        c = ctx_peer[kc]
        landed(pjrecv.at[c], pj_recv.at[c])
        stream = stream + pjrecv[c].astype(jnp.float32)
    square = jnp.mean(stream * stream, axis=-1, keepdims=True)
    xbuf[...] = (stream * lax.rsqrt(square + 1e-06)).astype(jnp.bfloat16)

    for kc in reversed(range(1, ctxs)):
        remote(
            xbuf, xg.at[me], x_send.at[kc * cores], x_recv.at[me], ctx_peer[kc], mh
        ).start()
    remote(xbuf, xg.at[me], x_send.at[1], x_recv.at[me], mc, partner).start()
    pltpu.make_async_copy(xbuf, xg.at[me], x_recv.at[me]).start()
    for kc in range(1, ctxs):
        came = ctx_peer[kc] * cores + mh
        landed(xg.at[came], x_recv.at[came])
        remote(
            xg.at[came],
            xg.at[came],
            x_send.at[kc * cores + 1],
            x_recv.at[came],
            mc,
            partner,
        ).start()

    def drain_x():
        for k in range(1, devices):
            sent(xbuf, x_send.at[k])

    drains.append(drain_x)
    for one in loads[3:6]:
        one.wait()
    landed(xg.at[me], x_recv.at[me])
    for c in range(ctxs):
        came = c * cores + partner
        landed(xg.at[came], x_recv.at[came])
    for h, core in enumerate((partner, mh)):
        for c in range(ctxs):
            at = (h * ctxs + c) * rows
            xs[at : at + rows, :] = xg[c * cores + core].astype(jnp.float32)
    x = xs[...].astype(jnp.bfloat16)
    both = jnp.dot(x, wgu[...], preferred_element_type=jnp.float32)
    gate_values, up_values = both[:, 0:ffn], both[:, ffn : 2 * ffn]
    hidden = (gate_values / (1.0 + jnp.exp(-gate_values)) * up_values).astype(jnp.bfloat16)

    near_rows = mine.shape[0]
    result = gate * jnp.dot(hidden, wd[...], preferred_element_type=jnp.float32)
    for b in range(cores):
        block = result[b * near_rows : b * near_rows + rows]
        lead[b] = block
        lead_out[b] = block.astype(jnp.bfloat16)

    @pl.when(mh == 0)
    def _():
        remote(lead_out, lead_in, lead_send, lead_recv, mc, partner).start()

    give[...] = result[near_rows:].astype(jnp.bfloat16)
    remote(give, take, give_send, take_recv, mc, partner).start()
    mine[...] = result[0:near_rows]

    @pl.when(mh == 1)
    def _():
        landed(lead_in, lead_recv)
        for b in range(cores):
            lead_sum[b] = (lead[b] + lead_in[1 - b].astype(jnp.float32)).astype(jnp.bfloat16)
        for b in range(cores):
            push(lead_sum.at[b], yrecv.at[mc], lead_left.at[b], y_recv.at[mc], 0, b)

    landed(take, take_recv)
    total = mine[...] + take[...].astype(jnp.float32)
    for c in range(1, ctxs):
        ybuf[c] = total[c * rows : (c + 1) * rows].astype(jnp.bfloat16)
    for c in range(1, ctxs):
        remote(ybuf.at[c], yrecv.at[mc], y_send.at[c], y_recv.at[mc], c, partner).start()

    def drain_y():
        sent(give, give_send)
        for c in range(1, ctxs):
            sent(ybuf.at[0], y_send.at[c])

        @pl.when(mh == 0)
        def _():
            sent(lead_out, lead_send)

        @pl.when(mh == 1)
        def _():
            for b in range(cores):
                pl.when(me != b)(lambda b=b: sent(lead_sum.at[b], lead_left.at[b]))

    drains.append(drain_y)
    for drain in drains:
        drain()
    for kc in range(ctxs):
        c = ctx_peer[kc]
        landed(yrecv.at[c], y_recv.at[c])
        stream = stream + yrecv[c].astype(jnp.float32)
    out_ref[...] = stream.astype(out_ref.dtype)


def on_device(
    queries,
    prefix_keys,
    prefix_values,
    out_weight,
    residual_in,
    expert_ids,
    gate_weights,
    w_gate,
    w_up,
    w_down,
):
    ctxs, cores = lax.axis_size("ctx"), lax.axis_size("hd")
    devices = ctxs * cores
    own, heads, head = queries.shape
    positions, groups, _ = prefix_keys.shape
    depth, width = out_weight.shape
    rows = residual_in.shape[0]
    ffn = w_gate.shape[2]
    tokens = own * ctxs
    pair_count = heads // ctxs
    fits = (
        cores == 2
        and pair_count * ctxs == heads
        and pair_count * tokens == head
        and ctxs % 8 == 0
        and ctxs & (ctxs - 1) == 0
        and groups == 2
        and cores * ctxs <= head
        and devices * rows <= head
        and own * ctxs % (cores * 16) == 0
    )
    if not fits:
        return on_device_general(
            queries,
            prefix_keys,
            prefix_values,
            out_weight,
            residual_in,
            expert_ids,
            gate_weights,
            w_gate,
            w_up,
            w_down,
        )
    half = tokens // cores
    held = [
        pltpu.with_memory_space_constraint(a, pltpu.HBM)
        for a in (
            queries.reshape(own, groups, heads // groups, head),
            prefix_keys.reshape(positions * groups, head),
            prefix_values.reshape(positions * groups, head),
            out_weight,
            residual_in,
            expert_ids,
            gate_weights,
            w_gate[0],
            w_up[0],
            w_down[0],
        )
    ]
    any_spec = pl.BlockSpec(memory_space=pl.ANY)
    vmem_spec = pl.BlockSpec(memory_space=pltpu.VMEM)
    bf, f32 = jnp.bfloat16, jnp.float32
    dma = pltpu.SemaphoreType.DMA
    return pl.pallas_call(
        functools.partial(layer_kernel, ctxs, cores),
        out_shape=jax.ShapeDtypeStruct((rows, width), bf),
        in_specs=[any_spec] * 10,
        out_specs=vmem_spec,
        scratch_shapes=[
            pltpu.VMEM((own, groups, heads // groups, head), bf),
            pltpu.VMEM(residual_in.shape, bf),
            pltpu.VMEM(expert_ids.shape, expert_ids.dtype),
            pltpu.VMEM(gate_weights.shape, f32),
            pltpu.VMEM((positions * groups, head), bf),
            pltpu.VMEM((positions * groups, head), bf),
            pltpu.VMEM((256 * groups, head), f32),
            pltpu.VMEM((groups, positions, head), bf),
            pltpu.VMEM((groups, positions, 2 * head), bf),
            pltpu.VMEM((ctxs, groups, own * heads // groups, head), bf),
            pltpu.VMEM((groups, own * heads // groups, head), f32),
            pltpu.VMEM((groups, own * heads // groups, head), bf),
            pltpu.VMEM((cores, depth, width), bf),
            pltpu.VMEM((width, 2 * ffn), bf),
            pltpu.VMEM((ffn, width), bf),
            pltpu.VMEM((cores * groups, ctxs // groups, pair_count * half, head), bf),
            pltpu.VMEM((cores * groups, ctxs // groups // 2, 3, head), f32),
            pltpu.VMEM((ctxs, cores, pair_count * half, head), bf),
            pltpu.VMEM((ctxs, cores, 3, head), f32),
            pltpu.VMEM((head, head), f32),
            pltpu.VMEM((head, head), f32),
            pltpu.VMEM((half, cores * depth), bf),
            pltpu.VMEM((half // rows, rows, width), bf),
            pltpu.VMEM((ctxs, rows, width), bf),
            pltpu.VMEM((rows, width), bf),
            pltpu.VMEM((devices, rows, width), bf),
            pltpu.VMEM((devices * rows, width), f32),
            pltpu.VMEM((devices * rows, head), f32),
            pltpu.VMEM((ctxs * rows, width), f32),
            pltpu.VMEM((ctxs * rows, width), bf),
            pltpu.VMEM((ctxs * rows, width), bf),
            pltpu.VMEM((cores, rows, width), f32),
            pltpu.VMEM((cores, rows, width), bf),
            pltpu.VMEM((cores, rows, width), bf),
            pltpu.VMEM((cores, rows, width), bf),
            pltpu.VMEM((ctxs, rows, width), bf),
            pltpu.VMEM((ctxs, rows, width), bf),
            dma((10,)),
            dma((ctxs,)),
            dma((ctxs,)),
            dma,
            dma,
            dma((cores * groups, ctxs // groups)),
            dma((ctxs, cores)),
            dma((cores * groups, ctxs // groups)),
            dma((ctxs, cores)),
            dma((half // rows,)),
            dma((ctxs,)),
            dma((devices,)),
            dma((devices,)),
            dma,
            dma,
            dma,
            dma,
            dma((cores,)),
            dma((ctxs,)),
            dma((ctxs,)),
            pltpu.SemaphoreType.REGULAR,
        ],
        compiler_params=pltpu.CompilerParams(
            collective_id=0, has_side_effects=True, vmem_limit_bytes=32 * 1024 * 1024
        ),
    )(*held)


def solution(mesh):
    placed = (
        P(("grp", "ctx"), "hd", None),
        P(("grp", "ctx"), "hd", None),
        P(("grp", "ctx"), "hd", None),
        P(("hd", "ctx"), None),
        P(("grp", "ctx", "hd"), None),
        P(("grp", "ctx", "hd"), None),
        P(("grp", "ctx", "hd"), None),
        P(("ctx", "hd"), None, None),
        P(("ctx", "hd"), None, None),
        P(("ctx", "hd"), None, None),
    )
    return jax.shard_map(
        on_device,
        mesh=mesh,
        in_specs=placed,
        out_specs=P(("grp", "ctx", "hd"), None),
        check_vma=False,
    )
```

```python
import jax
import jax.numpy as jnp
from jax import lax
from jax.experimental import pallas as pl
from jax.experimental.pallas import tpu as pltpu
from jax.sharding import PartitionSpec as P
import functools
import math

TOP = 8
KV_BLOCK = 512


NEG_START = -1e30


def local_attention(queries, prefix_keys, prefix_values):
    token_count, heads_local, head_width = queries.shape
    key_heads = prefix_keys.shape[1]
    grouped = heads_local // key_heads
    query_view = queries.reshape(token_count, key_heads, grouped, head_width)
    block_count = prefix_keys.shape[0] // KV_BLOCK
    key_blocks = prefix_keys.reshape(block_count, KV_BLOCK, key_heads, head_width)
    value_blocks = prefix_values.reshape(block_count, KV_BLOCK, key_heads, head_width)
    scaling = head_width ** (-0.5)

    def advance(running, pieces):
        peak_scores, totals, accumulated = running
        key_piece, value_piece = pieces
        scores = (
            jnp.einsum("sgjd,kgd->sgjk", query_view, key_piece, preferred_element_type=jnp.float32)
            * scaling
        )
        block_peak = jnp.max(scores, axis=-1)
        weights = jnp.exp(scores - block_peak[..., None]).astype(jnp.bfloat16)
        block_total = jnp.sum(weights.astype(jnp.float32), axis=-1)
        block_out = jnp.einsum(
            "sgjk,kgd->sgjd", weights, value_piece, preferred_element_type=jnp.float32
        )
        raised = jnp.maximum(peak_scores, block_peak)
        old_factor = jnp.exp(peak_scores - raised)
        new_factor = jnp.exp(block_peak - raised)
        totals = totals * old_factor + block_total * new_factor
        accumulated = accumulated * old_factor[..., None] + block_out * new_factor[..., None]
        return ((raised, totals, accumulated), None)

    start_state = (
        jnp.full((token_count, key_heads, grouped), NEG_START, jnp.float32),
        jnp.zeros((token_count, key_heads, grouped), jnp.float32),
        jnp.zeros((token_count, key_heads, grouped, head_width), jnp.float32),
    )
    final_state, leftover = lax.scan(advance, start_state, (key_blocks, value_blocks))
    peak_scores = final_state[0].reshape(token_count, heads_local)
    totals = final_state[1].reshape(token_count, heads_local)
    accumulated = final_state[2].reshape(token_count, heads_local, head_width)
    return (peak_scores, totals, accumulated)


def on_device_general(
    queries,
    prefix_keys,
    prefix_values,
    out_weight,
    residual_in,
    expert_ids,
    gate_weights,
    w_gate,
    w_up,
    w_down,
):
    every_query = lax.all_gather(queries, "ctx", axis=0, tiled=True)
    peak_scores, totals, accumulated = local_attention(every_query, prefix_keys, prefix_values)
    token_count, heads_local, head_width = accumulated.shape
    top_peak = lax.pmax(peak_scores, "ctx")
    factor = jnp.exp(peak_scores - top_peak)
    scaled_totals = totals * factor
    scaled_accum = (accumulated * factor[..., None]).reshape(token_count, heads_local * head_width)
    model_width = out_weight.shape[1]
    column_accum = lax.psum_scatter(
        scaled_accum.astype(jnp.bfloat16), "ctx", scatter_dimension=1, tiled=True
    ).astype(jnp.float32)
    all_totals = lax.psum(scaled_totals, "ctx")
    width_here = column_accum.shape[1]
    column_ids = lax.axis_index("ctx") * width_here + jnp.arange(width_here, dtype=jnp.int32)
    selector = (
        (column_ids // head_width)[None, :] == jnp.arange(heads_local, dtype=jnp.int32)[:, None]
    ).astype(jnp.float32)
    denominators = jnp.dot(all_totals, selector, precision=lax.Precision.HIGHEST)
    attended = (column_accum / denominators).astype(jnp.bfloat16)
    projected = lax.psum_scatter(
        jnp.dot(attended, out_weight, preferred_element_type=jnp.float32),
        ("ctx", "hd"),
        scatter_dimension=0,
        tiled=True,
    )
    stream = residual_in.astype(jnp.float32) + projected
    normed = (stream * lax.rsqrt(jnp.mean(stream * stream, axis=-1, keepdims=True) + 1e-06)).astype(
        jnp.bfloat16
    )
    context_count = lax.axis_size("ctx")
    head_groups = lax.axis_size("hd")
    expert_count = context_count * head_groups
    rows_here = normed.shape[0]
    slot_total = rows_here * TOP
    capacity = 2 * max(1, slot_total // expert_count)
    flat_ids = expert_ids.reshape(slot_total)
    onehot = (flat_ids[:, None] == jnp.arange(expert_count, dtype=jnp.int32)[None, :]).astype(
        jnp.int32
    )
    before = jnp.tril(jnp.ones((slot_total, slot_total), jnp.float32), -1)
    earlier = jnp.dot(
        before, onehot.astype(jnp.float32), precision=lax.Precision.HIGHEST
    ).astype(jnp.int32)
    position = jnp.sum(onehot * earlier, axis=1)
    target_row = flat_ids * capacity + position
    dispatch = (
        jnp.arange(expert_count * capacity, dtype=jnp.int32)[:, None] == target_row[None, :]
    ).astype(jnp.bfloat16)
    repeated = jnp.repeat(normed, TOP, axis=0)
    buffer = jnp.dot(dispatch, repeated, preferred_element_type=jnp.float32).astype(jnp.bfloat16)
    buffer = buffer.reshape(expert_count, capacity, model_width)
    slot_block = lax.all_to_all(buffer, ("ctx", "hd"), split_axis=0, concat_axis=0, tiled=True)
    sources, slot_count, feature_width = slot_block.shape
    flattened = slot_block.reshape(sources * slot_count, feature_width)
    gate_values = jnp.dot(flattened, w_gate[0], preferred_element_type=jnp.float32)
    up_values = jnp.dot(flattened, w_up[0], preferred_element_type=jnp.float32)
    hidden = (jax.nn.silu(gate_values) * up_values).astype(jnp.bfloat16)
    result = jnp.dot(hidden, w_down[0], preferred_element_type=jnp.float32).astype(jnp.bfloat16)
    returned_rows = lax.all_to_all(
        result.reshape(sources, slot_count, feature_width),
        ("ctx", "hd"),
        split_axis=0,
        concat_axis=0,
        tiled=True,
    )
    gathered = jnp.dot(
        dispatch.T,
        returned_rows.reshape(expert_count * capacity, model_width),
        preferred_element_type=jnp.float32,
    )
    weighted = gathered.reshape(rows_here, TOP, model_width) * gate_weights[:, :, None]
    mixture = jnp.sum(weighted, axis=1)
    return (stream + mixture).astype(jnp.bfloat16)


MESH = pl.DeviceIdType.MESH


def layer_kernel(
    ctxs,
    cores,
    q_ref,
    k_ref,
    v_ref,
    ow_ref,
    res_ref,
    ids_ref,
    gw_ref,
    wg_ref,
    wu_ref,
    wd_ref,
    out_ref,
    q_v,
    res_v,
    ids_v,
    gw_v,
    kraw,
    vraw,
    tmp,
    kd,
    vd,
    qbuf,
    qf,
    qs,
    w2,
    wgu,
    wd,
    numbuf,
    stbuf,
    numrecv,
    strecv,
    wst,
    wt,
    att,
    pjbuf,
    pjrecv,
    xbuf,
    xg,
    xs,
    gx,
    mine,
    give,
    take,
    lead,
    lead_out,
    lead_in,
    lead_sum,
    ybuf,
    yrecv,
    load_sem,
    q_send,
    q_recv,
    ow_send,
    ow_recv,
    num_send,
    num_recv,
    st_send,
    st_recv,
    pj_send,
    pj_recv,
    x_send,
    x_recv,
    give_send,
    take_recv,
    lead_send,
    lead_recv,
    lead_left,
    y_send,
    y_recv,
    late,
):
    mc = lax.axis_index("ctx")
    mh = lax.axis_index("hd")
    devices = ctxs * cores
    me = mc * cores + mh
    rows, width = res_ref.shape
    ffn = wd_ref.shape[0]
    own, groups, share_heads, head = q_ref.shape
    turns, targets_in_turn, pair_rows, _ = numbuf.shape
    tokens = own * ctxs
    half = tokens // cores
    pair_count = pair_rows // half
    rate = head ** (-0.5) * math.log2(math.e)

    def remote(src, dst, ssem, rsem, c, h):
        return pltpu.make_async_remote_copy(
            src_ref=src,
            dst_ref=dst,
            send_sem=ssem,
            recv_sem=rsem,
            device_id={"ctx": c, "hd": h},
            device_id_type=MESH,
        )

    def peer(step):
        c, bit = mc, 1
        while bit < ctxs:
            if step & bit:
                c = c + (1 - 2 * lax.rem(mc // bit, 2)) * bit
            bit *= 2
        return c

    ctx_peer = [peer(step) for step in range(ctxs)]
    core_peer = [mh, cores - 1 - mh]
    steps = [(kc, kh) for kc in reversed(range(ctxs)) for kh in (1, 0)]

    def push(src, dst, ssem, rsem, c, h):
        other = c * cores + h

        @pl.when(other != me)
        def _():
            remote(src, dst, ssem, rsem, c, h).start()

        @pl.when(other == me)
        def _():
            pltpu.make_async_copy(src, dst, rsem).start()

    def sent(src, ssem):
        pltpu.make_async_copy(src, src, ssem).wait()

    def landed(dst, rsem):
        pltpu.make_async_copy(dst, dst, rsem).wait()

    drains = []
    loads = [
        pltpu.make_async_copy(a, b, load_sem.at[i])
        for i, (a, b) in enumerate(
            (
                (k_ref, kraw),
                (v_ref, vraw),
                (ow_ref, w2.at[mh]),
                (wg_ref, wgu.at[:, 0:ffn]),
                (wu_ref, wgu.at[:, ffn : 2 * ffn]),
                (wd_ref, wd),
                (res_ref, res_v),
                (ids_ref, ids_v),
                (gw_ref, gw_v),
                (q_ref, q_v),
            )
        )
    ]
    barrier = pltpu.get_barrier_semaphore()

    last = ctxs - 1

    def greet(sem, kc, kh):
        pl.semaphore_signal(
            sem,
            inc=1,
            device_id={"ctx": ctx_peer[kc], "hd": core_peer[kh]},
            device_id_type=MESH,
        )

    @pl.when(mc != last)
    def _():
        for kc, kh in steps[:-2]:
            greet(barrier, kc, kh)

    greet(barrier, 0, 1)
    for one in (loads[9], *loads[:2], *loads[6:9]):
        one.start()

    loads[9].wait()
    for g in range(groups):
        qf[g] = q_v[:, g].astype(jnp.float32).reshape(own * share_heads, head)
        for h in range(share_heads):
            qs[g, h * own : (h + 1) * own, :] = qf[
                g, pl.ds(h, own, stride=share_heads), :
            ].astype(jnp.bfloat16)
    pl.semaphore_wait(barrier, devices - 1 - cores + cores * (mc // last))

    @pl.when(mc == last)
    def _():
        for kc, kh in steps[:-2]:
            greet(late, kc, kh)

    def send_q(c, sem):
        remote(qs, qbuf.at[mc], sem, q_recv.at[mc], c, mh).start()

    for kc in range(1, ctxs):
        pl.when(ctx_peer[kc] != last)(lambda kc=kc: send_q(ctx_peer[kc], q_send.at[kc]))
    pltpu.make_async_copy(qs, qbuf.at[mc], q_recv.at[mc]).start()
    ow_copy = remote(ow_ref, w2.at[mh], ow_send, ow_recv, mc, cores - 1 - mh)
    ow_copy.start()
    for one in loads[2:6]:
        one.start()

    def drain_q():
        for kc in range(1, ctxs):
            pl.when(ctx_peer[kc] != last)(lambda kc=kc: sent(qs, q_send.at[kc]))
        pl.when(mc != last)(lambda: sent(qs, q_send.at[0]))

    drains.append(drain_q)
    piece = tmp.shape[0]
    share = piece // groups

    def split(raw, store):
        @pl.loop(0, raw.shape[0] // piece)
        def _(i):
            tmp[...] = raw[pl.ds(pl.multiple_of(i * piece, piece), piece), :].astype(jnp.float32)
            for g in range(groups):
                store(g, i, tmp[pl.ds(g, share, stride=groups), :].astype(jnp.bfloat16))

    def store_k(g, i, value):
        kd[g, pl.ds(pl.multiple_of(i * share, share), share), :] = value

    def store_v(g, i, value):
        at = pl.ds(pl.multiple_of(i * share, share), share)
        vd[g, at, 0:head] = value
        vd[g, at, head : 2 * head] = jnp.ones_like(value)

    loads[0].wait()
    split(kraw, store_k)

    @pl.when(mc != last)
    def _():
        pl.semaphore_wait(late, cores)
        send_q(last, q_send.at[0])

    loads[1].wait()
    split(vraw, store_v)

    wst[...] = jnp.zeros_like(wst)
    for one in loads[6:9]:
        one.wait()
    lane = lax.broadcasted_iota(jnp.int32, (rows, head), 1)
    offset = lane - lax.broadcasted_iota(jnp.int32, (rows, head), 0)
    spread = jnp.zeros((rows, head), jnp.float32)
    for e in range(devices):
        gate = jnp.sum(jnp.where(ids_v[...] == e, gw_v[...], 0.0), axis=1, keepdims=True)
        spread = spread + jnp.where(offset == e * rows, gate, 0.0)
    gates = jnp.sum(spread, axis=0, keepdims=True)

    sources = ctxs // cores
    here, there = mc // sources, mc // targets_in_turn
    lanes = lax.broadcasted_iota(jnp.int32, (sources * own * share_heads, head), 1)
    for far in (0, 1):
        part = here if far == 0 else 1 - here
        for i in range(sources):
            c = part * sources + i
            landed(qbuf.at[c], q_recv.at[c])

        def rows_of(value, i):
            starts = [
                (n * share_heads + i * pair_count + a) * own
                for a in range(pair_count)
                for n in range(sources)
            ]
            return jnp.concatenate([value[at : at + own] for at in starts], axis=0)

        for near in (0, 1):
            turn = 2 * far + near
            g = there if near else 1 - there
            core = 1 if near == far else 0
            s = lax.dot_general(
                jnp.concatenate([qbuf[part * sources + i, g] for i in range(sources)], axis=0),
                kd[g],
                (((1,), (1,)), ((), ())), preferred_element_type=jnp.float32
            )
            m = jnp.max(s, axis=1, keepdims=True)
            p = jnp.exp2((s - m) * rate).astype(jnp.bfloat16)
            o = jnp.dot(p, vd[g], preferred_element_type=jnp.float32)
            stat = jnp.where(lanes == 0, m, o[:, head : 2 * head])
            for i in range(targets_in_turn):
                numbuf[turn, i] = rows_of(o[:, 0:head], i).astype(jnp.bfloat16)
                if i % 2 == 0:
                    both = jnp.concatenate([rows_of(stat, i), rows_of(stat, i + 1)], axis=0)
                    stbuf[turn, i // 2, 0:2] = both.T[0:2]
                    stbuf[turn, i // 2, 2:3] = gates
            for i in range(targets_in_turn):
                c = g * targets_in_turn + i
                for src, dst, ssem, rsem in (
                    (stbuf.at[turn, i // 2], strecv, st_send, st_recv),
                    (numbuf.at[turn, i], numrecv, num_send, num_recv),
                ):
                    args = (src, dst.at[mc, mh], ssem.at[turn, i], rsem.at[mc, mh], c, core)
                    if near:
                        push(*args)
                    else:
                        remote(*args).start()

    def drain_num():
        for turn in range(turns):
            core = turn // 2
            for i in range(targets_in_turn):

                def both(turn=turn, i=i):
                    sent(stbuf.at[turn, 0], st_send.at[turn, i])
                    sent(numbuf.at[turn, i], num_send.at[turn, i])

                if turn % 2 == 0:
                    both()
                else:
                    pl.when((there * targets_in_turn + i) * cores + core != me)(both)

    drains.append(drain_num)
    for h in range(cores):
        peaks, totals = [], []
        for c in range(ctxs):
            landed(strecv.at[c, h], st_recv.at[c, h])
            peaks.append(strecv[c, h, 0:1, :])
            totals.append(strecv[c, h, 1:2, :])
        peaks = jnp.concatenate(peaks, axis=0)
        totals = jnp.concatenate(totals, axis=0)
        factor = jnp.exp2((peaks - jnp.max(peaks, axis=0, keepdims=True)) * rate)
        wst[h * ctxs : (h + 1) * ctxs, :] = factor / jnp.sum(
            totals * factor, axis=0, keepdims=True
        )
    wt[...] = wst[...].T
    for h in reversed(range(cores)):
        for c in range(ctxs):
            landed(numrecv.at[c, h], num_recv.at[c, h])
        for a in range(pair_count):
            at = lax.rem(mc, 2) * pair_rows + a * half
            shares = wt[pl.ds(pl.multiple_of(at, half), half), :]
            total = jnp.zeros((half, head), jnp.float32)
            for c in range(ctxs):
                at = h * ctxs + c
                total = total + numrecv[c, h, a * half : (a + 1) * half].astype(jnp.float32) * shares[:, at : at + 1]
            at = (h * pair_count + a) * head
            att[:, at : at + head] = total.astype(jnp.bfloat16)

    partner = core_peer[1]
    loads[2].wait()
    ow_copy.wait()
    projected = jnp.dot(
        att[...], w2[...].reshape(att.shape[1], width), preferred_element_type=jnp.float32
    )
    targets = half // rows
    for j in range(targets):
        pjbuf[j] = projected[j * rows : (j + 1) * rows].astype(jnp.bfloat16)

    chips = targets // cores
    low = lax.rem(mc, chips)
    away = mh
    base = (here + away - 2 * here * away) * chips
    for kc in reversed(range(chips)):
        for kh in (1, 0):
            c = base + ctx_peer[kc] - (mc - low)
            h = core_peer[kh]
            j = (c - base) * cores + h
            go = remote if kc or kh else push
            k = kc * cores + kh
            copy = go(pjbuf.at[j], pjrecv.at[mc], pj_send.at[k], pj_recv.at[mc], c, h)
            if kc or kh:
                copy.start()

    def drain_pj():
        for k in range(1, targets):
            sent(pjbuf.at[0], pj_send.at[k])

        @pl.when(base != mc - low)
        def _():
            sent(pjbuf.at[0], pj_send.at[0])

    drains.append(drain_pj)
    for h, core in enumerate((partner, mh)):
        for c in range(ctxs):
            at = (h * ctxs + c) * rows
            gx[at : at + rows, :] = jnp.broadcast_to(strecv[c, core, 2:3, :], (rows, head))
    row = lax.broadcasted_iota(jnp.int32, gx.shape, 0)
    lane = lax.broadcasted_iota(jnp.int32, gx.shape, 1)
    gate = jnp.sum(
        jnp.where(lane == me * rows + lax.rem(row, rows), gx[...], 0.0), axis=1, keepdims=True
    )

    stream = res_v[...].astype(jnp.float32)
    for kc in range(ctxs):
        c = ctx_peer[kc]
        landed(pjrecv.at[c], pj_recv.at[c])
        stream = stream + pjrecv[c].astype(jnp.float32)
    square = jnp.mean(stream * stream, axis=-1, keepdims=True)
    xbuf[...] = (stream * lax.rsqrt(square + 1e-06)).astype(jnp.bfloat16)

    for kc in reversed(range(1, ctxs)):
        remote(
            xbuf, xg.at[me], x_send.at[kc * cores], x_recv.at[me], ctx_peer[kc], mh
        ).start()
    remote(xbuf, xg.at[me], x_send.at[1], x_recv.at[me], mc, partner).start()
    pltpu.make_async_copy(xbuf, xg.at[me], x_recv.at[me]).start()
    for kc in range(1, ctxs):
        came = ctx_peer[kc] * cores + mh
        landed(xg.at[came], x_recv.at[came])
        remote(
            xg.at[came],
            xg.at[came],
            x_send.at[kc * cores + 1],
            x_recv.at[came],
            mc,
            partner,
        ).start()

    def drain_x():
        for k in range(1, devices):
            sent(xbuf, x_send.at[k])

    drains.append(drain_x)
    for one in loads[3:6]:
        one.wait()
    landed(xg.at[me], x_recv.at[me])
    for c in range(ctxs):
        at = (ctxs + c) * rows
        xs[at : at + rows, :] = xg[c * cores + mh].astype(jnp.float32)
    for c in range(ctxs):
        came = c * cores + partner
        landed(xg.at[came], x_recv.at[came])
        xs[c * rows : (c + 1) * rows, :] = xg[came].astype(jnp.float32)
    x = xs[...].astype(jnp.bfloat16)
    both = jnp.dot(x, wgu[...], preferred_element_type=jnp.float32)
    gate_values, up_values = both[:, 0:ffn], both[:, ffn : 2 * ffn]
    hidden = (gate_values / (1.0 + jnp.exp(-gate_values)) * up_values).astype(jnp.bfloat16)

    near_rows = mine.shape[0]
    result = gate * jnp.dot(hidden, wd[...], preferred_element_type=jnp.float32)
    for b in range(cores):
        block = result[b * near_rows : b * near_rows + rows]
        lead[b] = block
        lead_out[b] = block.astype(jnp.bfloat16)

    @pl.when(mh == 0)
    def _():
        remote(lead_out, lead_in, lead_send, lead_recv, mc, partner).start()

    give[...] = result[near_rows:].astype(jnp.bfloat16)
    remote(give, take, give_send, take_recv, mc, partner).start()

    @pl.when(mh == 1)
    def _():
        landed(lead_in, lead_recv)
        for b in range(cores):
            lead_sum[b] = (lead[b] + lead_in[1 - b].astype(jnp.float32)).astype(jnp.bfloat16)
        for b in range(cores):
            push(lead_sum.at[b], yrecv.at[mc], lead_left.at[b], y_recv.at[mc], 0, b)

    landed(take, take_recv)
    total = result[0:near_rows] + take[...].astype(jnp.float32)
    for c in range(1, ctxs):
        ybuf[c] = total[c * rows : (c + 1) * rows].astype(jnp.bfloat16)
    for c in range(1, ctxs):
        remote(ybuf.at[c], yrecv.at[mc], y_send.at[c], y_recv.at[mc], c, partner).start()

    def drain_y():
        sent(give, give_send)
        for c in range(1, ctxs):
            sent(ybuf.at[0], y_send.at[c])

        @pl.when(mh == 0)
        def _():
            sent(lead_out, lead_send)

        @pl.when(mh == 1)
        def _():
            for b in range(cores):
                pl.when(me != b)(lambda b=b: sent(lead_sum.at[b], lead_left.at[b]))

    drains.append(drain_y)
    for drain in drains:
        drain()
    for kc in range(ctxs):
        c = ctx_peer[kc]
        landed(yrecv.at[c], y_recv.at[c])
        stream = stream + yrecv[c].astype(jnp.float32)
    out_ref[...] = stream.astype(out_ref.dtype)


def on_device(
    queries,
    prefix_keys,
    prefix_values,
    out_weight,
    residual_in,
    expert_ids,
    gate_weights,
    w_gate,
    w_up,
    w_down,
):
    ctxs, cores = lax.axis_size("ctx"), lax.axis_size("hd")
    devices = ctxs * cores
    own, heads, head = queries.shape
    positions, groups, _ = prefix_keys.shape
    depth, width = out_weight.shape
    rows = residual_in.shape[0]
    ffn = w_gate.shape[2]
    tokens = own * ctxs
    pair_count = heads // ctxs
    fits = (
        cores == 2
        and pair_count * ctxs == heads
        and pair_count * tokens == head
        and ctxs % 8 == 0
        and ctxs & (ctxs - 1) == 0
        and groups == 2
        and cores * ctxs <= head
        and devices * rows <= head
        and own * ctxs % (cores * 16) == 0
    )
    if not fits:
        return on_device_general(
            queries,
            prefix_keys,
            prefix_values,
            out_weight,
            residual_in,
            expert_ids,
            gate_weights,
            w_gate,
            w_up,
            w_down,
        )
    half = tokens // cores
    held = [
        pltpu.with_memory_space_constraint(a, pltpu.HBM)
        for a in (
            queries.reshape(own, groups, heads // groups, head),
            prefix_keys.reshape(positions * groups, head),
            prefix_values.reshape(positions * groups, head),
            out_weight,
            residual_in,
            expert_ids,
            gate_weights,
            w_gate[0],
            w_up[0],
            w_down[0],
        )
    ]
    any_spec = pl.BlockSpec(memory_space=pl.ANY)
    vmem_spec = pl.BlockSpec(memory_space=pltpu.VMEM)
    bf, f32 = jnp.bfloat16, jnp.float32
    dma = pltpu.SemaphoreType.DMA
    return pl.pallas_call(
        functools.partial(layer_kernel, ctxs, cores),
        out_shape=jax.ShapeDtypeStruct((rows, width), bf),
        in_specs=[any_spec] * 10,
        out_specs=vmem_spec,
        scratch_shapes=[
            pltpu.VMEM((own, groups, heads // groups, head), bf),
            pltpu.VMEM(residual_in.shape, bf),
            pltpu.VMEM(expert_ids.shape, expert_ids.dtype),
            pltpu.VMEM(gate_weights.shape, f32),
            pltpu.VMEM((positions * groups, head), bf),
            pltpu.VMEM((positions * groups, head), bf),
            pltpu.VMEM((256 * groups, head), f32),
            pltpu.VMEM((groups, positions, head), bf),
            pltpu.VMEM((groups, positions, 2 * head), bf),
            pltpu.VMEM((ctxs, groups, own * heads // groups, head), bf),
            pltpu.VMEM((groups, own * heads // groups, head), f32),
            pltpu.VMEM((groups, own * heads // groups, head), bf),
            pltpu.VMEM((cores, depth, width), bf),
            pltpu.VMEM((width, 2 * ffn), bf),
            pltpu.VMEM((ffn, width), bf),
            pltpu.VMEM((cores * groups, ctxs // groups, pair_count * half, head), bf),
            pltpu.VMEM((cores * groups, ctxs // groups // 2, 3, head), f32),
            pltpu.VMEM((ctxs, cores, pair_count * half, head), bf),
            pltpu.VMEM((ctxs, cores, 3, head), f32),
            pltpu.VMEM((head, head), f32),
            pltpu.VMEM((head, head), f32),
            pltpu.VMEM((half, cores * depth), bf),
            pltpu.VMEM((half // rows, rows, width), bf),
            pltpu.VMEM((ctxs, rows, width), bf),
            pltpu.VMEM((rows, width), bf),
            pltpu.VMEM((devices, rows, width), bf),
            pltpu.VMEM((devices * rows, width), f32),
            pltpu.VMEM((devices * rows, head), f32),
            pltpu.VMEM((ctxs * rows, width), f32),
            pltpu.VMEM((ctxs * rows, width), bf),
            pltpu.VMEM((ctxs * rows, width), bf),
            pltpu.VMEM((cores, rows, width), f32),
            pltpu.VMEM((cores, rows, width), bf),
            pltpu.VMEM((cores, rows, width), bf),
            pltpu.VMEM((cores, rows, width), bf),
            pltpu.VMEM((ctxs, rows, width), bf),
            pltpu.VMEM((ctxs, rows, width), bf),
            dma((10,)),
            dma((ctxs,)),
            dma((ctxs,)),
            dma,
            dma,
            dma((cores * groups, ctxs // groups)),
            dma((ctxs, cores)),
            dma((cores * groups, ctxs // groups)),
            dma((ctxs, cores)),
            dma((half // rows,)),
            dma((ctxs,)),
            dma((devices,)),
            dma((devices,)),
            dma,
            dma,
            dma,
            dma,
            dma((cores,)),
            dma((ctxs,)),
            dma((ctxs,)),
            pltpu.SemaphoreType.REGULAR,
        ],
        compiler_params=pltpu.CompilerParams(
            collective_id=0, has_side_effects=True, vmem_limit_bytes=32 * 1024 * 1024
        ),
    )(*held)


def solution(mesh):
    placed = (
        P(("grp", "ctx"), "hd", None),
        P(("grp", "ctx"), "hd", None),
        P(("grp", "ctx"), "hd", None),
        P(("hd", "ctx"), None),
        P(("grp", "ctx", "hd"), None),
        P(("grp", "ctx", "hd"), None),
        P(("grp", "ctx", "hd"), None),
        P(("ctx", "hd"), None, None),
        P(("ctx", "hd"), None, None),
        P(("ctx", "hd"), None, None),
    )
    return jax.shard_map(
        on_device,
        mesh=mesh,
        in_specs=placed,
        out_specs=P(("grp", "ctx", "hd"), None),
        check_vma=False,
    )
```

```python
import jax
import jax.numpy as jnp
from jax import lax
from jax.experimental import pallas as pl
from jax.experimental.pallas import tpu as pltpu
from jax.sharding import PartitionSpec as P
import functools
import math

TOP = 8
KV_BLOCK = 512


NEG_START = -1e30


def local_attention(queries, prefix_keys, prefix_values):
    token_count, heads_local, head_width = queries.shape
    key_heads = prefix_keys.shape[1]
    grouped = heads_local // key_heads
    query_view = queries.reshape(token_count, key_heads, grouped, head_width)
    block_count = prefix_keys.shape[0] // KV_BLOCK
    key_blocks = prefix_keys.reshape(block_count, KV_BLOCK, key_heads, head_width)
    value_blocks = prefix_values.reshape(block_count, KV_BLOCK, key_heads, head_width)
    scaling = head_width ** (-0.5)

    def advance(running, pieces):
        peak_scores, totals, accumulated = running
        key_piece, value_piece = pieces
        scores = (
            jnp.einsum("sgjd,kgd->sgjk", query_view, key_piece, preferred_element_type=jnp.float32)
            * scaling
        )
        block_peak = jnp.max(scores, axis=-1)
        weights = jnp.exp(scores - block_peak[..., None]).astype(jnp.bfloat16)
        block_total = jnp.sum(weights.astype(jnp.float32), axis=-1)
        block_out = jnp.einsum(
            "sgjk,kgd->sgjd", weights, value_piece, preferred_element_type=jnp.float32
        )
        raised = jnp.maximum(peak_scores, block_peak)
        old_factor = jnp.exp(peak_scores - raised)
        new_factor = jnp.exp(block_peak - raised)
        totals = totals * old_factor + block_total * new_factor
        accumulated = accumulated * old_factor[..., None] + block_out * new_factor[..., None]
        return ((raised, totals, accumulated), None)

    start_state = (
        jnp.full((token_count, key_heads, grouped), NEG_START, jnp.float32),
        jnp.zeros((token_count, key_heads, grouped), jnp.float32),
        jnp.zeros((token_count, key_heads, grouped, head_width), jnp.float32),
    )
    final_state, leftover = lax.scan(advance, start_state, (key_blocks, value_blocks))
    peak_scores = final_state[0].reshape(token_count, heads_local)
    totals = final_state[1].reshape(token_count, heads_local)
    accumulated = final_state[2].reshape(token_count, heads_local, head_width)
    return (peak_scores, totals, accumulated)


def on_device_general(
    queries,
    prefix_keys,
    prefix_values,
    out_weight,
    residual_in,
    expert_ids,
    gate_weights,
    w_gate,
    w_up,
    w_down,
):
    every_query = lax.all_gather(queries, "ctx", axis=0, tiled=True)
    peak_scores, totals, accumulated = local_attention(every_query, prefix_keys, prefix_values)
    token_count, heads_local, head_width = accumulated.shape
    top_peak = lax.pmax(peak_scores, "ctx")
    factor = jnp.exp(peak_scores - top_peak)
    scaled_totals = totals * factor
    scaled_accum = (accumulated * factor[..., None]).reshape(token_count, heads_local * head_width)
    model_width = out_weight.shape[1]
    column_accum = lax.psum_scatter(
        scaled_accum.astype(jnp.bfloat16), "ctx", scatter_dimension=1, tiled=True
    ).astype(jnp.float32)
    all_totals = lax.psum(scaled_totals, "ctx")
    width_here = column_accum.shape[1]
    column_ids = lax.axis_index("ctx") * width_here + jnp.arange(width_here, dtype=jnp.int32)
    selector = (
        (column_ids // head_width)[None, :] == jnp.arange(heads_local, dtype=jnp.int32)[:, None]
    ).astype(jnp.float32)
    denominators = jnp.dot(all_totals, selector, precision=lax.Precision.HIGHEST)
    attended = (column_accum / denominators).astype(jnp.bfloat16)
    projected = lax.psum_scatter(
        jnp.dot(attended, out_weight, preferred_element_type=jnp.float32),
        ("ctx", "hd"),
        scatter_dimension=0,
        tiled=True,
    )
    stream = residual_in.astype(jnp.float32) + projected
    normed = (stream * lax.rsqrt(jnp.mean(stream * stream, axis=-1, keepdims=True) + 1e-06)).astype(
        jnp.bfloat16
    )
    context_count = lax.axis_size("ctx")
    head_groups = lax.axis_size("hd")
    expert_count = context_count * head_groups
    rows_here = normed.shape[0]
    slot_total = rows_here * TOP
    capacity = 2 * max(1, slot_total // expert_count)
    flat_ids = expert_ids.reshape(slot_total)
    onehot = (flat_ids[:, None] == jnp.arange(expert_count, dtype=jnp.int32)[None, :]).astype(
        jnp.int32
    )
    before = jnp.tril(jnp.ones((slot_total, slot_total), jnp.float32), -1)
    earlier = jnp.dot(
        before, onehot.astype(jnp.float32), precision=lax.Precision.HIGHEST
    ).astype(jnp.int32)
    position = jnp.sum(onehot * earlier, axis=1)
    target_row = flat_ids * capacity + position
    dispatch = (
        jnp.arange(expert_count * capacity, dtype=jnp.int32)[:, None] == target_row[None, :]
    ).astype(jnp.bfloat16)
    repeated = jnp.repeat(normed, TOP, axis=0)
    buffer = jnp.dot(dispatch, repeated, preferred_element_type=jnp.float32).astype(jnp.bfloat16)
    buffer = buffer.reshape(expert_count, capacity, model_width)
    slot_block = lax.all_to_all(buffer, ("ctx", "hd"), split_axis=0, concat_axis=0, tiled=True)
    sources, slot_count, feature_width = slot_block.shape
    flattened = slot_block.reshape(sources * slot_count, feature_width)
    gate_values = jnp.dot(flattened, w_gate[0], preferred_element_type=jnp.float32)
    up_values = jnp.dot(flattened, w_up[0], preferred_element_type=jnp.float32)
    hidden = (jax.nn.silu(gate_values) * up_values).astype(jnp.bfloat16)
    result = jnp.dot(hidden, w_down[0], preferred_element_type=jnp.float32).astype(jnp.bfloat16)
    returned_rows = lax.all_to_all(
        result.reshape(sources, slot_count, feature_width),
        ("ctx", "hd"),
        split_axis=0,
        concat_axis=0,
        tiled=True,
    )
    gathered = jnp.dot(
        dispatch.T,
        returned_rows.reshape(expert_count * capacity, model_width),
        preferred_element_type=jnp.float32,
    )
    weighted = gathered.reshape(rows_here, TOP, model_width) * gate_weights[:, :, None]
    mixture = jnp.sum(weighted, axis=1)
    return (stream + mixture).astype(jnp.bfloat16)


MESH = pl.DeviceIdType.MESH


def layer_kernel(
    ctxs,
    cores,
    q_ref,
    k_ref,
    v_ref,
    ow_ref,
    res_ref,
    ids_ref,
    gw_ref,
    wg_ref,
    wu_ref,
    wd_ref,
    out_ref,
    q_v,
    res_v,
    ids_v,
    gw_v,
    kraw,
    vraw,
    tmp,
    kd,
    vd,
    qbuf,
    qf,
    qs,
    w2,
    wgu,
    wd,
    numbuf,
    stbuf,
    numrecv,
    strecv,
    wst,
    wt,
    att,
    pjbuf,
    pjrecv,
    xbuf,
    xg,
    xs,
    gx,
    mine,
    give,
    take,
    lead,
    lead_out,
    lead_in,
    lead_sum,
    ybuf,
    yrecv,
    load_sem,
    q_send,
    q_recv,
    ow_send,
    ow_recv,
    num_send,
    num_recv,
    st_send,
    st_recv,
    pj_send,
    pj_recv,
    x_send,
    x_recv,
    give_send,
    take_recv,
    lead_send,
    lead_recv,
    lead_left,
    y_send,
    y_recv,
    late,
):
    mc = lax.axis_index("ctx")
    mh = lax.axis_index("hd")
    devices = ctxs * cores
    me = mc * cores + mh
    rows, width = res_ref.shape
    ffn = wd_ref.shape[0]
    own, groups, share_heads, head = q_ref.shape
    turns, targets_in_turn, pair_rows, _ = numbuf.shape
    tokens = own * ctxs
    half = tokens // cores
    pair_count = pair_rows // half
    rate = head ** (-0.5) * math.log2(math.e)

    def remote(src, dst, ssem, rsem, c, h):
        return pltpu.make_async_remote_copy(
            src_ref=src,
            dst_ref=dst,
            send_sem=ssem,
            recv_sem=rsem,
            device_id={"ctx": c, "hd": h},
            device_id_type=MESH,
        )

    def peer(step):
        c, bit = mc, 1
        while bit < ctxs:
            if step & bit:
                c = c + (1 - 2 * lax.rem(mc // bit, 2)) * bit
            bit *= 2
        return c

    ctx_peer = [peer(step) for step in range(ctxs)]
    core_peer = [mh, cores - 1 - mh]
    steps = [(kc, kh) for kc in reversed(range(ctxs)) for kh in (1, 0)]

    def push(src, dst, ssem, rsem, c, h):
        other = c * cores + h

        @pl.when(other != me)
        def _():
            remote(src, dst, ssem, rsem, c, h).start()

        @pl.when(other == me)
        def _():
            pltpu.make_async_copy(src, dst, rsem).start()

    def sent(src, ssem):
        pltpu.make_async_copy(src, src, ssem).wait()

    def landed(dst, rsem):
        pltpu.make_async_copy(dst, dst, rsem).wait()

    drains = []
    loads = [
        pltpu.make_async_copy(a, b, load_sem.at[i])
        for i, (a, b) in enumerate(
            (
                (k_ref, kraw),
                (v_ref, vraw),
                (ow_ref, w2.at[mh]),
                (wg_ref, wgu.at[:, 0:ffn]),
                (wu_ref, wgu.at[:, ffn : 2 * ffn]),
                (wd_ref, wd),
                (res_ref, res_v),
                (ids_ref, ids_v),
                (gw_ref, gw_v),
                (q_ref, q_v),
            )
        )
    ]
    barrier = pltpu.get_barrier_semaphore()

    last = ctxs - 1

    def greet(sem, kc, kh):
        pl.semaphore_signal(
            sem,
            inc=1,
            device_id={"ctx": ctx_peer[kc], "hd": core_peer[kh]},
            device_id_type=MESH,
        )

    @pl.when(mc != last)
    def _():
        for kc, kh in steps[:-2]:
            greet(barrier, kc, kh)

    greet(barrier, 0, 1)
    for one in (loads[9], *loads[:2], *loads[6:9]):
        one.start()

    loads[9].wait()
    for g in range(groups):
        qf[g] = q_v[:, g].astype(jnp.float32).reshape(own * share_heads, head)
        for h in range(share_heads):
            qs[g, h * own : (h + 1) * own, :] = qf[
                g, pl.ds(h, own, stride=share_heads), :
            ].astype(jnp.bfloat16)
    pl.semaphore_wait(barrier, devices - 1 - cores + cores * (mc // last))

    @pl.when(mc == last)
    def _():
        for kc, kh in steps[:-2]:
            greet(late, kc, kh)

    def send_q(c, sem):
        remote(qs, qbuf.at[mc], sem, q_recv.at[mc], c, mh).start()

    for kc in range(1, ctxs):
        pl.when(ctx_peer[kc] != last)(lambda kc=kc: send_q(ctx_peer[kc], q_send.at[kc]))
    pltpu.make_async_copy(qs, qbuf.at[mc], q_recv.at[mc]).start()
    ow_copy = remote(ow_ref, w2.at[mh], ow_send, ow_recv, mc, cores - 1 - mh)
    ow_copy.start()
    for one in loads[2:6]:
        one.start()

    def drain_q():
        for kc in range(1, ctxs):
            pl.when(ctx_peer[kc] != last)(lambda kc=kc: sent(qs, q_send.at[kc]))
        pl.when(mc != last)(lambda: sent(qs, q_send.at[0]))

    drains.append(drain_q)
    piece = tmp.shape[0]
    share = piece // groups

    def split(raw, store):
        @pl.loop(0, raw.shape[0] // piece)
        def _(i):
            tmp[...] = raw[pl.ds(pl.multiple_of(i * piece, piece), piece), :].astype(jnp.float32)
            for g in range(groups):
                store(g, i, tmp[pl.ds(g, share, stride=groups), :].astype(jnp.bfloat16))

    def store_k(g, i, value):
        kd[g, pl.ds(pl.multiple_of(i * share, share), share), :] = value

    def store_v(g, i, value):
        at = pl.ds(pl.multiple_of(i * share, share), share)
        vd[g, at, 0:head] = value
        vd[g, at, head : 2 * head] = jnp.ones_like(value)

    loads[0].wait()
    split(kraw, store_k)

    @pl.when(mc != last)
    def _():
        pl.semaphore_wait(late, cores)
        send_q(last, q_send.at[0])

    loads[1].wait()
    split(vraw, store_v)

    wst[...] = jnp.zeros_like(wst)
    for one in loads[6:9]:
        one.wait()
    lane = lax.broadcasted_iota(jnp.int32, (rows, head), 1)
    offset = lane - lax.broadcasted_iota(jnp.int32, (rows, head), 0)
    spread = jnp.zeros((rows, head), jnp.float32)
    for e in range(devices):
        gate = jnp.sum(jnp.where(ids_v[...] == e, gw_v[...], 0.0), axis=1, keepdims=True)
        spread = spread + jnp.where(offset == e * rows, gate, 0.0)
    gates = jnp.sum(spread, axis=0, keepdims=True)

    sources = ctxs // cores
    here, there = mc // sources, mc // targets_in_turn
    lanes = lax.broadcasted_iota(jnp.int32, (sources * own * share_heads, head), 1)
    for far in (0, 1):
        part = here if far == 0 else 1 - here
        for i in range(sources):
            c = part * sources + i
            landed(qbuf.at[c], q_recv.at[c])

        def rows_of(value, i):
            starts = [
                (n * share_heads + i * pair_count + a) * own
                for a in range(pair_count)
                for n in range(sources)
            ]
            return jnp.concatenate([value[at : at + own] for at in starts], axis=0)

        for near in (0, 1):
            turn = 2 * far + near
            g = there if near else 1 - there
            core = 1 if near == far else 0
            s = lax.dot_general(
                jnp.concatenate([qbuf[part * sources + i, g] for i in range(sources)], axis=0),
                kd[g],
                (((1,), (1,)), ((), ())), preferred_element_type=jnp.float32
            )
            m = jnp.max(s, axis=1, keepdims=True)
            p = jnp.exp2((s - m) * rate).astype(jnp.bfloat16)
            o = jnp.dot(p, vd[g], preferred_element_type=jnp.float32)
            stat = jnp.where(lanes == 0, m, o[:, head : 2 * head])
            for i in range(targets_in_turn):
                numbuf[turn, i] = rows_of(o[:, 0:head], i).astype(jnp.bfloat16)
                if i % 2 == 0:
                    both = jnp.concatenate([rows_of(stat, i), rows_of(stat, i + 1)], axis=0)
                    stbuf[turn, i // 2, 0:2] = both.T[0:2]
                    stbuf[turn, i // 2, 2:3] = gates
            for i in range(targets_in_turn):
                c = g * targets_in_turn + i
                for src, dst, ssem, rsem in (
                    (stbuf.at[turn, i // 2], strecv, st_send, st_recv),
                    (numbuf.at[turn, i], numrecv, num_send, num_recv),
                ):
                    args = (src, dst.at[mc, mh], ssem.at[turn, i], rsem.at[mc, mh], c, core)
                    if near:
                        push(*args)
                    else:
                        remote(*args).start()

    def drain_num():
        for turn in range(turns):
            core = turn // 2
            for i in range(targets_in_turn):

                def both(turn=turn, i=i):
                    sent(stbuf.at[turn, 0], st_send.at[turn, i])
                    sent(numbuf.at[turn, i], num_send.at[turn, i])

                if turn % 2 == 0:
                    both()
                else:
                    pl.when((there * targets_in_turn + i) * cores + core != me)(both)

    drains.append(drain_num)
    for h in reversed(range(cores)):
        peaks, totals = [], []
        for c in range(ctxs):
            landed(strecv.at[c, h], st_recv.at[c, h])
            peaks.append(strecv[c, h, 0:1, :])
            totals.append(strecv[c, h, 1:2, :])
        peaks = jnp.concatenate(peaks, axis=0)
        totals = jnp.concatenate(totals, axis=0)
        factor = jnp.exp2((peaks - jnp.max(peaks, axis=0, keepdims=True)) * rate)
        wst[h * ctxs : (h + 1) * ctxs, :] = factor / jnp.sum(
            totals * factor, axis=0, keepdims=True
        )
    wt[...] = wst[...].T
    for h in reversed(range(cores)):
        for c in range(ctxs):
            landed(numrecv.at[c, h], num_recv.at[c, h])
        for a in range(pair_count):
            at = lax.rem(mc, 2) * pair_rows + a * half
            shares = wt[pl.ds(pl.multiple_of(at, half), half), :]
            total = jnp.zeros((half, head), jnp.float32)
            for c in range(ctxs):
                at = h * ctxs + c
                total = total + numrecv[c, h, a * half : (a + 1) * half].astype(jnp.float32) * shares[:, at : at + 1]
            at = (h * pair_count + a) * head
            att[:, at : at + head] = total.astype(jnp.bfloat16)

    partner = core_peer[1]
    loads[2].wait()
    ow_copy.wait()
    projected = jnp.dot(
        att[...], w2[...].reshape(att.shape[1], width), preferred_element_type=jnp.float32
    )
    targets = half // rows
    for j in range(targets):
        pjbuf[j] = projected[j * rows : (j + 1) * rows].astype(jnp.bfloat16)

    chips = targets // cores
    low = lax.rem(mc, chips)
    away = mh
    base = (here + away - 2 * here * away) * chips
    for kc in reversed(range(chips)):
        for kh in (1, 0):
            c = base + ctx_peer[kc] - (mc - low)
            h = core_peer[kh]
            j = (c - base) * cores + h
            go = remote if kc or kh else push
            k = kc * cores + kh
            copy = go(pjbuf.at[j], pjrecv.at[mc], pj_send.at[k], pj_recv.at[mc], c, h)
            if kc or kh:
                copy.start()

    def drain_pj():
        for k in range(1, targets):
            sent(pjbuf.at[0], pj_send.at[k])

        @pl.when(base != mc - low)
        def _():
            sent(pjbuf.at[0], pj_send.at[0])

    drains.append(drain_pj)
    for h, core in enumerate((partner, mh)):
        for c in range(ctxs):
            at = (h * ctxs + c) * rows
            gx[at : at + rows, :] = jnp.broadcast_to(strecv[c, core, 2:3, :], (rows, head))
    row = lax.broadcasted_iota(jnp.int32, gx.shape, 0)
    lane = lax.broadcasted_iota(jnp.int32, gx.shape, 1)
    gate = jnp.sum(
        jnp.where(lane == me * rows + lax.rem(row, rows), gx[...], 0.0), axis=1, keepdims=True
    )

    stream = res_v[...].astype(jnp.float32)
    for kc in range(ctxs):
        c = ctx_peer[kc]
        landed(pjrecv.at[c], pj_recv.at[c])
        stream = stream + pjrecv[c].astype(jnp.float32)
    square = jnp.mean(stream * stream, axis=-1, keepdims=True)
    xbuf[...] = (stream * lax.rsqrt(square + 1e-06)).astype(jnp.bfloat16)

    for kc in reversed(range(1, ctxs)):
        remote(
            xbuf, xg.at[me], x_send.at[kc * cores], x_recv.at[me], ctx_peer[kc], mh
        ).start()
    remote(xbuf, xg.at[me], x_send.at[1], x_recv.at[me], mc, partner).start()
    pltpu.make_async_copy(xbuf, xg.at[me], x_recv.at[me]).start()
    for kc in range(1, ctxs):
        came = ctx_peer[kc] * cores + mh
        landed(xg.at[came], x_recv.at[came])
        remote(
            xg.at[came],
            xg.at[came],
            x_send.at[kc * cores + 1],
            x_recv.at[came],
            mc,
            partner,
        ).start()

    def drain_x():
        for k in range(1, devices):
            sent(xbuf, x_send.at[k])

    drains.append(drain_x)
    for one in loads[3:6]:
        one.wait()
    landed(xg.at[me], x_recv.at[me])
    for c in range(ctxs):
        at = (ctxs + c) * rows
        xs[at : at + rows, :] = xg[c * cores + mh].astype(jnp.float32)
    for c in range(ctxs):
        came = c * cores + partner
        landed(xg.at[came], x_recv.at[came])
        xs[c * rows : (c + 1) * rows, :] = xg[came].astype(jnp.float32)
    x = xs[...].astype(jnp.bfloat16)
    both = jnp.dot(x, wgu[...], preferred_element_type=jnp.float32)
    gate_values, up_values = both[:, 0:ffn], both[:, ffn : 2 * ffn]
    hidden = (gate_values / (1.0 + jnp.exp(-gate_values)) * up_values).astype(jnp.bfloat16)

    near_rows = mine.shape[0]
    result = gate * jnp.dot(hidden, wd[...], preferred_element_type=jnp.float32)
    for b in range(cores):
        block = result[b * near_rows : b * near_rows + rows]
        lead[b] = block
        lead_out[b] = block.astype(jnp.bfloat16)

    @pl.when(mh == 0)
    def _():
        remote(lead_out, lead_in, lead_send, lead_recv, mc, partner).start()

    give[...] = result[near_rows:].astype(jnp.bfloat16)
    remote(give, take, give_send, take_recv, mc, partner).start()

    @pl.when(mh == 1)
    def _():
        landed(lead_in, lead_recv)
        for b in range(cores):
            lead_sum[b] = (lead[b] + lead_in[1 - b].astype(jnp.float32)).astype(jnp.bfloat16)
        for b in range(cores):
            push(lead_sum.at[b], yrecv.at[mc], lead_left.at[b], y_recv.at[mc], 0, b)

    landed(take, take_recv)
    total = result[0:near_rows] + take[...].astype(jnp.float32)
    for c in range(1, ctxs):
        ybuf[c] = total[c * rows : (c + 1) * rows].astype(jnp.bfloat16)
    for c in range(1, ctxs):
        remote(ybuf.at[c], yrecv.at[mc], y_send.at[c], y_recv.at[mc], c, partner).start()

    def drain_y():
        sent(give, give_send)
        for c in range(1, ctxs):
            sent(ybuf.at[0], y_send.at[c])

        @pl.when(mh == 0)
        def _():
            sent(lead_out, lead_send)

        @pl.when(mh == 1)
        def _():
            for b in range(cores):
                pl.when(me != b)(lambda b=b: sent(lead_sum.at[b], lead_left.at[b]))

    drains.append(drain_y)
    for drain in drains:
        drain()
    for kc in range(ctxs):
        c = ctx_peer[kc]
        landed(yrecv.at[c], y_recv.at[c])
        stream = stream + yrecv[c].astype(jnp.float32)
    out_ref[...] = stream.astype(out_ref.dtype)


def on_device(
    queries,
    prefix_keys,
    prefix_values,
    out_weight,
    residual_in,
    expert_ids,
    gate_weights,
    w_gate,
    w_up,
    w_down,
):
    ctxs, cores = lax.axis_size("ctx"), lax.axis_size("hd")
    devices = ctxs * cores
    own, heads, head = queries.shape
    positions, groups, _ = prefix_keys.shape
    depth, width = out_weight.shape
    rows = residual_in.shape[0]
    ffn = w_gate.shape[2]
    tokens = own * ctxs
    pair_count = heads // ctxs
    fits = (
        cores == 2
        and pair_count * ctxs == heads
        and pair_count * tokens == head
        and ctxs % 8 == 0
        and ctxs & (ctxs - 1) == 0
        and groups == 2
        and cores * ctxs <= head
        and devices * rows <= head
        and own * ctxs % (cores * 16) == 0
    )
    if not fits:
        return on_device_general(
            queries,
            prefix_keys,
            prefix_values,
            out_weight,
            residual_in,
            expert_ids,
            gate_weights,
            w_gate,
            w_up,
            w_down,
        )
    half = tokens // cores
    held = [
        pltpu.with_memory_space_constraint(a, pltpu.HBM)
        for a in (
            queries.reshape(own, groups, heads // groups, head),
            prefix_keys.reshape(positions * groups, head),
            prefix_values.reshape(positions * groups, head),
            out_weight,
            residual_in,
            expert_ids,
            gate_weights,
            w_gate[0],
            w_up[0],
            w_down[0],
        )
    ]
    any_spec = pl.BlockSpec(memory_space=pl.ANY)
    vmem_spec = pl.BlockSpec(memory_space=pltpu.VMEM)
    bf, f32 = jnp.bfloat16, jnp.float32
    dma = pltpu.SemaphoreType.DMA
    return pl.pallas_call(
        functools.partial(layer_kernel, ctxs, cores),
        out_shape=jax.ShapeDtypeStruct((rows, width), bf),
        in_specs=[any_spec] * 10,
        out_specs=vmem_spec,
        scratch_shapes=[
            pltpu.VMEM((own, groups, heads // groups, head), bf),
            pltpu.VMEM(residual_in.shape, bf),
            pltpu.VMEM(expert_ids.shape, expert_ids.dtype),
            pltpu.VMEM(gate_weights.shape, f32),
            pltpu.VMEM((positions * groups, head), bf),
            pltpu.VMEM((positions * groups, head), bf),
            pltpu.VMEM((256 * groups, head), f32),
            pltpu.VMEM((groups, positions, head), bf),
            pltpu.VMEM((groups, positions, 2 * head), bf),
            pltpu.VMEM((ctxs, groups, own * heads // groups, head), bf),
            pltpu.VMEM((groups, own * heads // groups, head), f32),
            pltpu.VMEM((groups, own * heads // groups, head), bf),
            pltpu.VMEM((cores, depth, width), bf),
            pltpu.VMEM((width, 2 * ffn), bf),
            pltpu.VMEM((ffn, width), bf),
            pltpu.VMEM((cores * groups, ctxs // groups, pair_count * half, head), bf),
            pltpu.VMEM((cores * groups, ctxs // groups // 2, 3, head), f32),
            pltpu.VMEM((ctxs, cores, pair_count * half, head), bf),
            pltpu.VMEM((ctxs, cores, 3, head), f32),
            pltpu.VMEM((head, head), f32),
            pltpu.VMEM((head, head), f32),
            pltpu.VMEM((half, cores * depth), bf),
            pltpu.VMEM((half // rows, rows, width), bf),
            pltpu.VMEM((ctxs, rows, width), bf),
            pltpu.VMEM((rows, width), bf),
            pltpu.VMEM((devices, rows, width), bf),
            pltpu.VMEM((devices * rows, width), f32),
            pltpu.VMEM((devices * rows, head), f32),
            pltpu.VMEM((ctxs * rows, width), f32),
            pltpu.VMEM((ctxs * rows, width), bf),
            pltpu.VMEM((ctxs * rows, width), bf),
            pltpu.VMEM((cores, rows, width), f32),
            pltpu.VMEM((cores, rows, width), bf),
            pltpu.VMEM((cores, rows, width), bf),
            pltpu.VMEM((cores, rows, width), bf),
            pltpu.VMEM((ctxs, rows, width), bf),
            pltpu.VMEM((ctxs, rows, width), bf),
            dma((10,)),
            dma((ctxs,)),
            dma((ctxs,)),
            dma,
            dma,
            dma((cores * groups, ctxs // groups)),
            dma((ctxs, cores)),
            dma((cores * groups, ctxs // groups)),
            dma((ctxs, cores)),
            dma((half // rows,)),
            dma((ctxs,)),
            dma((devices,)),
            dma((devices,)),
            dma,
            dma,
            dma,
            dma,
            dma((cores,)),
            dma((ctxs,)),
            dma((ctxs,)),
            pltpu.SemaphoreType.REGULAR,
        ],
        compiler_params=pltpu.CompilerParams(
            collective_id=0, has_side_effects=True, vmem_limit_bytes=32 * 1024 * 1024
        ),
    )(*held)


def solution(mesh):
    placed = (
        P(("grp", "ctx"), "hd", None),
        P(("grp", "ctx"), "hd", None),
        P(("grp", "ctx"), "hd", None),
        P(("hd", "ctx"), None),
        P(("grp", "ctx", "hd"), None),
        P(("grp", "ctx", "hd"), None),
        P(("grp", "ctx", "hd"), None),
        P(("ctx", "hd"), None, None),
        P(("ctx", "hd"), None, None),
        P(("ctx", "hd"), None, None),
    )
    return jax.shard_map(
        on_device,
        mesh=mesh,
        in_specs=placed,
        out_specs=P(("grp", "ctx", "hd"), None),
        check_vma=False,
    )
```
